256 devices in a mesh: gx: 32 (over x_hi, z, core), gy: 8 (over x_lo, y).
Axes of the slice: x: 4 (x_hi: 2, x_lo: 2; x = x_hi * 2 + x_lo), y: 4, z: 8, core: 2. Of those that a mesh axis runs over, the one named last changes fastest.
Arguments:
- positions: float32 [3, 131072], P(None, ('gx', 'gy')), as said below
- species: int32 [131072], P(('gx', 'gy')), may hold values from 0 to 7
- send_lists: int32 [32, 8, 8, 32], P('gx', 'gy'), may hold values from 0 to 511, as said below
- cell_pairs: int32 [32, 8, 32, 2], P('gx', 'gy'), may hold values from 0 to 23, as said below
- block_count: int32 [32, 8], P('gx', 'gy'), may hold values from 24 to 32, as said below
- embed: float32 [8, 128], replicated, may hold values from -6 to 6
- radial_one: float32 [2, 8, 128], replicated, may hold values from -2 to 2
- mix_one: float32 [5, 128, 128], replicated, may hold values from -0.5 to 0.5
- radial_two: float32 [2, 8, 128], replicated, may hold values from -2 to 2
- mix_two: float32 [2, 128, 128], replicated, may hold values from -0.5 to 0.5
- readout: float32 [2, 128], replicated, may hold values from -0.5 to 0.5
Outputs:
- forces: float32 [3, 131072], P(None, ('gx', 'gy'))
- site_energy: float32 [131072], P(('gx', 'gy'))
The draws below stay inside these ranges and needn't reach their ends.
Inputs may be any that keep to these rules, and one draw needn't show every extreme that they name: `positions`: every coordinate lies in 0 to 5120^(1/3) in its owner's frame. `send_lists`: each entry names 32 distinct atoms of the sending device, as indices 0 to 511 among its own atoms. `cell_pairs`: column 0 is an owned cell 0 to 15, column 1 a cell 0 to 23 of the extended table; the first 24 slots of a device name every extended cell once in column 1. `block_count`: the number of used leading slots of each device; some device uses all 32 and some only 24.
All inputs are finite; a program needn't handle non-finite values.
Results may differ from the reference program's by a relative error of at most 0.0003.
Values sent between devices are 32-bit elements; how exact they have to be, the bound alone decides.
No kernel may reach another device: no remote copies, remote signals or barrier semaphores. Data moves between devices by JAX's collectives and lax.ppermute only.
A program may use at most 64 MiB of HBM per device.

```python
import jax
import jax.numpy as jnp
import numpy as np
from jax import lax

CH = 128
NB = 8
NSPEC = 8
CELL = 32
CELLS_DEV = 16
GHOST_CELLS = 1
BLOCKS_DEV = 32
ATOMS = 131072
N_GX = 32
N_GY = 8
DEVICES = 256


def draw_positions(key, part):
    atoms_dev = CELLS_DEV * CELL
    side = float((atoms_dev * 10.0) ** (1.0 / 3.0))
    values = jax.random.uniform(jax.random.fold_in(key, 31), (3, ATOMS), jnp.float32, 0.0, 1.0)
    return (values * side).astype(jnp.float32)


def draw_send_lists(key, part):
    atoms_dev = CELLS_DEV * CELL
    ghost = GHOST_CELLS * CELL
    keys = jax.random.split(key, DEVICES * 8)

    def one_list(subkey):
        return jax.random.permutation(subkey, atoms_dev)[:ghost]
    lists = jax.vmap(one_list)(keys)
    return lists.reshape(N_GX, N_GY, 8, ghost).astype(jnp.int32)


def draw_cell_pairs(key, part):
    ext_cells = CELLS_DEV + 8 * GHOST_CELLS
    key_send = jax.random.fold_in(key, 11)
    key_fill = jax.random.fold_in(key, 12)
    key_recv = jax.random.fold_in(key, 13)
    perm_keys = jax.random.split(key_send, DEVICES)

    def one_perm(subkey):
        return jax.random.permutation(subkey, ext_cells)
    covered = jax.vmap(one_perm)(perm_keys)
    extra = jax.random.randint(key_fill, (DEVICES, BLOCKS_DEV - ext_cells), 0, ext_cells)
    senders = jnp.concatenate([covered, extra], axis=1)
    receivers = jax.random.randint(key_recv, (DEVICES, BLOCKS_DEV), 0, CELLS_DEV)
    return jnp.stack([receivers, senders], axis=-1).reshape(N_GX, N_GY, BLOCKS_DEV, 2).astype(jnp.int32)


def draw_block_count(key, part):
    ext_cells = CELLS_DEV + 8 * GHOST_CELLS
    key_load = jax.random.fold_in(key, 21)
    key_high = jax.random.fold_in(key, 22)
    counts = jax.random.randint(key_load, (DEVICES,), ext_cells, BLOCKS_DEV + 1)
    places = jax.random.permutation(key_high, DEVICES)
    counts = counts.at[places[0]].set(BLOCKS_DEV)
    counts = counts.at[places[1]].set(ext_cells)
    return counts.reshape(N_GX, N_GY).astype(jnp.int32)


def with_ends(values, key, low, largest):
    spot = [jax.random.randint(jax.random.fold_in(key, axis), (), 0, length) for axis, length in enumerate(values.shape)]
    widest = values.shape.index(max(values.shape))
    next_to = spot[:widest] + [(spot[widest] + 1) % values.shape[widest]] + spot[widest + 1:]
    return values.at[tuple(spot)].set(low).at[tuple(next_to)].set(largest)


def noise(rng, shape, width, reach, kind=jnp.bfloat16):
    values = jax.random.normal(rng, shape, jnp.float32) * width
    return jnp.minimum(jnp.maximum(values, -reach), reach).astype(kind)


def setup_inputs(seed: int = 0) -> dict:
    arg_keys = jax.random.split(jax.random.key(seed), 12)
    positions = draw_positions(jax.random.fold_in(arg_keys[11], 71), 0)
    species = with_ends(jax.random.randint(arg_keys[1], (ATOMS,), 0, NSPEC), jax.random.fold_in(arg_keys[1], 1), 0, NSPEC - 1).astype(jnp.int32)
    send_lists = draw_send_lists(jax.random.fold_in(arg_keys[11], 71), 0)
    cell_pairs = draw_cell_pairs(jax.random.fold_in(arg_keys[11], 71), 0)
    block_count = draw_block_count(jax.random.fold_in(arg_keys[11], 71), 0)
    embed = noise(arg_keys[5], (NSPEC, CH), 1.0, 6.0, jnp.float32)
    radial_one = noise(arg_keys[6], (2, NB, CH), NB ** -0.5, 2.0, jnp.float32)
    mix_one = noise(arg_keys[7], (5, CH, CH), CH ** -0.5, 0.5, jnp.float32)
    radial_two = noise(arg_keys[8], (2, NB, CH), NB ** -0.5, 2.0, jnp.float32)
    mix_two = noise(arg_keys[9], (2, CH, CH), CH ** -0.5, 0.5, jnp.float32)
    readout = noise(arg_keys[10], (2, CH), CH ** -0.5, 0.5, jnp.float32)
    return {"positions": positions, "species": species, "send_lists": send_lists, "cell_pairs": cell_pairs, "block_count": block_count, "embed": embed, "radial_one": radial_one, "mix_one": mix_one, "radial_two": radial_two, "mix_two": mix_two, "readout": readout}


highest = lax.Precision.HIGHEST
cutoff_sq = 25.0
pair_scale = 0.5
steps_x = np.array([-1, -1, -1, 0, 0, 1, 1, 1])
steps_y = np.array([-1, 0, 1, -1, 1, -1, 0, 1])

def matmul(left, right):
    return jnp.dot(left, right, precision=highest, preferred_element_type=jnp.float32)

def frame_side(atoms_dev):
    return float((atoms_dev * 10.0) ** (1.0 / 3.0))

def ghost_shift(ghost, side):
    along_x = jnp.repeat(jnp.asarray(steps_x * side, jnp.float32), ghost)
    along_y = jnp.repeat(jnp.asarray(steps_y * side, jnp.float32), ghost)
    return jnp.stack([along_x, along_y, jnp.zeros_like(along_x)])

def pair_basis(pos_recv, pos_send, same):
    separation = pos_send[:, None, :] - pos_recv[:, :, None]
    squared = lax.optimization_barrier(jnp.sum(separation * separation, axis=0))
    spacing = cutoff_sq / (NB - 1)
    centers = jnp.arange(NB, dtype=jnp.float32) * spacing
    keepers = 1.0 - same * jnp.eye(pos_recv.shape[1], dtype=jnp.float32)
    envelope = jnp.square(jnp.maximum(1.0 - squared / cutoff_sq, 0.0)) * keepers
    radial = envelope[None] * jnp.exp(-jnp.square((squared[None] - centers[:, None, None]) / spacing))
    return (radial, radial[:, None] * separation[None])

def block_one(pos_recv, pos_send, feat_send, same, radial_w):
    radial, oriented = pair_basis(pos_recv, pos_send, same)
    plain_part = jnp.einsum('bij,cj->bci', radial, feat_send, precision=highest)
    vector_part = jnp.einsum('baij,cj->baci', oriented, feat_send, precision=highest)
    scalar_out = jnp.einsum('bc,bci->ci', radial_w[0], plain_part, precision=highest)
    vector_out = jnp.einsum('bc,baci->aci', radial_w[1], vector_part, precision=highest)
    return (pair_scale * scalar_out, pair_scale * vector_out)

def block_two(pos_recv, pos_send, feat_send, same, radial_w):
    radial, oriented = pair_basis(pos_recv, pos_send, same)
    channels = radial_w.shape[2]
    scal_send = feat_send[:channels]
    vect_send = feat_send[channels:].reshape(3, channels, feat_send.shape[1])
    plain_part = jnp.einsum('bij,cj->bci', radial, scal_send, precision=highest)
    cross_part = jnp.einsum('baij,acj->bci', oriented, vect_send, precision=highest)
    total = jnp.einsum('bc,bci->ci', radial_w[0], plain_part, precision=highest)
    total = total + jnp.einsum('bc,bci->ci', radial_w[1], cross_part, precision=highest)
    return (pair_scale * total,)

def update_one(acc_scal, acc_vect, start, mix_one):
    power = lax.optimization_barrier(jnp.sum(acc_vect * acc_vect, axis=0))
    scal_new = jax.nn.silu(matmul(mix_one[0], acc_scal) + matmul(mix_one[1], power)) + matmul(mix_one[2], start)
    gating = jax.nn.sigmoid(matmul(mix_one[4], acc_scal))
    vect_new = jnp.einsum('cd,adi->aci', mix_one[3], acc_vect, precision=highest) * gating[None]
    return (scal_new, vect_new)

def update_two(acc_scal, previous, mix_two):
    return jax.nn.silu(matmul(mix_two[0], acc_scal)) + matmul(mix_two[1], previous)

def run_blocks(block_fn, own_pos, ext_pos, ext_feat, pairs, count, radial_w, initial):
    slots = jnp.arange(pairs.shape[0], dtype=jnp.int32)

    def stepper(running, slot):
        receiver = pairs[slot, 0] * CELL
        sender = pairs[slot, 1] * CELL
        same = (pairs[slot, 0] == pairs[slot, 1]).astype(jnp.float32)
        weight = (slot < count).astype(jnp.float32)
        pos_recv = lax.dynamic_slice_in_dim(own_pos, receiver, CELL, 1)
        pos_send = lax.dynamic_slice_in_dim(ext_pos, sender, CELL, 1)
        feat_send = lax.dynamic_slice_in_dim(ext_feat, sender, CELL, 1)
        parts = jax.checkpoint(block_fn)(pos_recv, pos_send, feat_send, same, radial_w)
        updated = []
        for whole, piece in zip(running, parts):
            last_axis = whole.ndim - 1
            current = lax.dynamic_slice_in_dim(whole, receiver, CELL, last_axis)
            updated.append(lax.dynamic_update_slice_in_dim(whole, current + weight * piece, receiver, last_axis))
        return (tuple(updated), None)
    final, unused = lax.scan(stepper, initial, slots)
    return final

def reference(positions, species, send_lists, cell_pairs, block_count, embed, radial_one, mix_one, radial_two, mix_two, readout):
    atoms_dev = CELLS_DEV * CELL
    ghost = GHOST_CELLS * CELL
    channels = embed.shape[1]
    devices = jnp.arange(DEVICES, dtype=jnp.int32)
    dev_row = devices // N_GY
    dev_col = devices % N_GY
    src_row = (dev_row[:, None] + jnp.asarray(steps_x, jnp.int32)[None]) % N_GX
    src_col = (dev_col[:, None] + jnp.asarray(steps_y, jnp.int32)[None]) % N_GY
    backward_dir = jnp.asarray(7 - np.arange(8), jnp.int32)
    listed = send_lists[src_row, src_col, backward_dir[None, :]]
    ghost_ids = ((src_row * N_GY + src_col) * atoms_dev)[:, :, None] + listed
    own_ids = devices[:, None] * atoms_dev + jnp.arange(atoms_dev, dtype=jnp.int32)[None]
    ext_ids = jnp.concatenate([own_ids, ghost_ids.reshape(DEVICES, 8 * ghost)], axis=1)
    shift_table = jnp.concatenate([jnp.zeros((3, atoms_dev), jnp.float32), ghost_shift(ghost, frame_side(atoms_dev))], axis=1)
    kinds = jnp.arange(NSPEC, dtype=jnp.int32)
    onehot = (species[None, :] == kinds[:, None]).astype(jnp.float32)
    start = matmul(embed.T, onehot)
    pairs_all = cell_pairs.reshape(DEVICES, BLOCKS_DEV, 2)
    counts = block_count.reshape(DEVICES)

    def energies(coords):

        def layer_first(device):
            ids = ext_ids[device]
            own_pos = lax.dynamic_slice_in_dim(coords, device * atoms_dev, atoms_dev, 1)
            ext_pos = coords[:, ids] + shift_table
            ext_feat = start[:, ids]
            initial = (jnp.zeros((channels, atoms_dev), jnp.float32), jnp.zeros((3, channels, atoms_dev), jnp.float32))
            acc_scal, acc_vect = run_blocks(block_one, own_pos, ext_pos, ext_feat, pairs_all[device], counts[device], radial_one, initial)
            own_start = lax.dynamic_slice_in_dim(start, device * atoms_dev, atoms_dev, 1)
            return update_one(acc_scal, acc_vect, own_start, mix_one)
        scal_one, vect_one = lax.map(jax.checkpoint(layer_first), devices)
        stacked = jnp.concatenate([scal_one, vect_one.reshape(DEVICES, 3 * channels, atoms_dev)], axis=1)
        feat_glob = jnp.transpose(stacked, (1, 0, 2)).reshape(4 * channels, DEVICES * atoms_dev)

        def layer_second(device):
            ids = ext_ids[device]
            own_pos = lax.dynamic_slice_in_dim(coords, device * atoms_dev, atoms_dev, 1)
            ext_pos = coords[:, ids] + shift_table
            ext_feat = feat_glob[:, ids]
            initial = (jnp.zeros((channels, atoms_dev), jnp.float32),)
            acc_two, = run_blocks(block_two, own_pos, ext_pos, ext_feat, pairs_all[device], counts[device], radial_two, initial)
            scal_two = update_two(acc_two, scal_one[device], mix_two)
            return matmul(readout[0], scal_one[device]) + matmul(readout[1], scal_two)
        site = lax.map(jax.checkpoint(layer_second), devices).reshape(DEVICES * atoms_dev)
        return (jnp.sum(site), site)
    gradient, site_energy = jax.grad(energies, has_aux=True)(positions)
    return (-gradient, site_energy)
```

```python
import functools

import jax
import jax.numpy as jnp
import numpy as np
from jax import lax
from jax.experimental import pallas as pl
from jax.experimental.pallas import tpu as pltpu
from jax.sharding import PartitionSpec as P

NB = 8
CELL = 32
CH = 128
LANES = 128
OWN = 16
EXT = 24
CUT2 = 25.0
STEPS_X = np.array([-1, -1, -1, 0, 0, 1, 1, 1])
STEPS_Y = np.array([-1, 0, 1, -1, 1, -1, 0, 1])
F32 = jnp.float32
BF16 = jnp.bfloat16
VMEM = pltpu.VMEM
SMEM = pltpu.SMEM
PARAMS = pltpu.CompilerParams(vmem_limit_bytes=48 * 1024 * 1024)
CHUNK = 128

NN = (((1,), (0,)), ((), ()))
NT = (((1,), (1,)), ((), ()))
TN = (((0,), (0,)), ((), ()))


def split(x):
    hi = x.astype(BF16)
    return hi, (x - hi.astype(F32)).astype(BF16)


def mm(a, b, dims):
    return lax.dot_general(a, b, dims, preferred_element_type=F32)


def mm3(a, b, dims):
    (ah, al), (bh, bl) = a, b
    return mm(ah, bh, dims) + (mm(ah, bl, dims) + mm(al, bh, dims))


def iota(shape, dim):
    return lax.broadcasted_iota(jnp.int32, shape, dim)


def geometry(r, c, weight, prc, xt):
    own = prc[pl.ds(pl.multiple_of(r * CELL, CELL), CELL), :]
    vec = [xt[t + 1, pl.ds(c, 1), :] - own[:, t : t + 1] for t in range(3)]
    sq = vec[0] * vec[0] + vec[1] * vec[1] + vec[2] * vec[2]
    lane = iota((CELL, LANES), 1)
    row = iota((CELL, LANES), 0)
    self_pair = jnp.logical_and(lane % CELL == row, r == c)
    keep = jnp.where(self_pair, 0.0, weight)
    edge = jnp.maximum(1.0 - sq * (1.0 / CUT2), 0.0)
    slope = edge * keep
    group = lane // CELL
    vk = jnp.where(group == 0, 1.0, jnp.where(group == 1, vec[0], jnp.where(group == 2, vec[1], vec[2])))
    scaled = sq * ((NB - 1) / CUT2)
    return edge * slope, slope, scaled, vk


def basis(scaled, n):
    off = scaled - float(n)
    return jnp.exp(-(off * off))


def pair_tile(env, scaled, vk):
    m = env * vk
    return jnp.concatenate([m * basis(scaled, n) for n in range(NB)], axis=0)


def pair_force(deriv, env, slope, scaled, vk):
    total = None
    moment = None
    for n in range(NB):
        term = deriv[n * CELL : (n + 1) * CELL] * basis(scaled, n)
        total = term if n == 0 else total + term
        if n == 1:
            moment = term
        elif n > 1:
            moment = moment + float(n) * term
    spacing = CUT2 / (NB - 1)
    direct = env * total
    by_sq = (-2.0 / CUT2) * slope * total - (2.0 / spacing) * env * (scaled * total - moment)
    by_sq = by_sq * vk
    by_sq = by_sq + pltpu.roll(by_sq, 64, 1)
    by_sq = by_sq + pltpu.roll(by_sq, 32, 1)
    return direct + 2.0 * vk * by_sq


def add_force(force, r, c, recv, send):
    rows = pl.ds(pl.multiple_of(r * CELL, CELL), CELL)
    recv[rows, :] += force
    send[pl.ds(c, 1), :] += jnp.sum(force, axis=0, keepdims=True)


def species_tile(c, xt):
    row = iota((4 * NB, LANES), 0)
    lane = iota((4 * NB, LANES), 1)
    kind = xt[0, pl.ds(c, 1), :].astype(jnp.int32)
    hit = jnp.logical_and(kind == row % NB, lane // CELL == row // NB)
    return jnp.where(hit, 1.0, 0.0).astype(BF16)


def species_weights(embed, radial):
    zero = jnp.zeros((NB, CH), F32)
    rows = []
    for n in range(NB):
        for k in range(4):
            part = embed * radial[min(k, 1), n : n + 1, :]
            rows.append(jnp.concatenate([part if j == k else zero for j in range(4)], axis=1))
    return split(jnp.concatenate(rows, axis=0))


def for_blocks(pairs, count, unroll, body):
    def step(i, carry):
        for k in range(unroll):
            slot = i * unroll + k
            weight = jnp.where(slot < count[0], 1.0, 0.0).astype(F32)
            body(pairs[2 * slot], pairs[2 * slot + 1], weight)
        return carry

    lax.fori_loop(0, (count[0] + unroll - 1) // unroll, step, 0)


def pack_kernel(pos, species, lists, out):
    kinds = species[...].astype(F32)
    table = jnp.concatenate([kinds, pos[...], jnp.zeros((4, kinds.shape[1]), F32)], axis=0)
    hi = table.astype(BF16)
    rest = table - hi.astype(F32)
    mid = rest.astype(BF16)
    low = (rest - mid.astype(F32)).astype(BF16)
    atoms = kinds.shape[1]
    hot = jnp.where(iota((atoms, lists.shape[1]), 0) == lists[...], 1.0, 0.0).astype(BF16)
    out[...] = mm(hi, hot, NN) + mm(mid, hot, NN) + mm(low, hot, NN)


def first_kernel(
    pairs, count, lists, xt, prc, embed, radial, mix, feat, sent, acc, gates, lifted, hist
):
    hist[...] = jnp.zeros_like(hist)

    def block(r, c, weight):
        env, slope, scaled, vk = geometry(r, c, weight, prc, xt)
        hi, lo = split(pair_tile(env, scaled, vk))
        hot = species_tile(c, xt)
        part = mm(hi, hot, NT) + mm(lo, hot, NT)
        rows = pl.ds(pl.multiple_of(r * CELL, CELL), CELL)
        for n in range(NB):
            hist[n, rows, :] += part[n * CELL : (n + 1) * CELL]

    for_blocks(pairs, count, 2, block)

    weights = species_weights(embed[...], radial)
    mix04 = split(jnp.concatenate([mix[0], mix[4]], axis=0))
    mix1 = split(mix[1])
    mix3 = split(mix[3])
    begin = split(mm3(split(embed[...]), split(mix[2]), NT))

    def chunk(i, carry):
        rows = pl.ds(pl.multiple_of(i * CHUNK, CHUNK), CHUNK)
        joined = jnp.concatenate([hist[n, rows, :] for n in range(NB)], axis=1)
        a = mm3(split(joined), weights, NN)
        acc[rows, :] = a
        a0 = a[:, :CH]
        a1 = [a[:, (t + 1) * CH : (t + 2) * CH] for t in range(3)]
        power = a1[0] * a1[0] + a1[1] * a1[1] + a1[2] * a1[2]
        both = mm3(split(a0), mix04, NT)
        z0 = both[:, :CH] + mm3(split(power), mix1, NT)
        gate = jax.nn.sigmoid(both[:, CH:])
        kind = prc[rows, :][:, 3:4].astype(jnp.int32)
        hot = jnp.where(kind == iota((CHUNK, NB), 1), 1.0, 0.0).astype(BF16)
        own = mm(hot, begin[0], NN) + mm(hot, begin[1], NN)
        lift = mm3(split(jnp.concatenate(a1, axis=0)), mix3, NT)
        lift = jnp.concatenate([lift[t * CHUNK : (t + 1) * CHUNK] for t in range(3)], axis=1)
        gates[rows, :] = jnp.concatenate([z0, gate], axis=1)
        lifted[rows, :] = lift
        feat[rows, :] = jnp.concatenate(
            [z0 * jax.nn.sigmoid(z0) + own, lift * jnp.concatenate([gate] * 3, axis=1)], axis=1
        )
        return carry

    lax.fori_loop(0, feat.shape[0] // CHUNK, chunk, 0)

    def gather(i, carry):
        for k in range(8):
            at = i * 8 + k
            sent[pl.ds(at, 1), :] = feat[pl.ds(lists[at], 1), :]
        return carry

    lax.fori_loop(0, sent.shape[0] // 8, gather, 0)


def cell_features(table, c):
    f = table[pl.ds(pl.multiple_of(c * CELL, CELL), CELL), :]
    hi, lo = split(f)
    zero = jnp.zeros((CELL, CH), BF16)

    def lay(x):
        rows = [jnp.concatenate([x[:, :CH], zero], axis=1)]
        rows += [jnp.concatenate([zero, x[:, (t + 1) * CH : (t + 2) * CH]], axis=1) for t in range(3)]
        return jnp.concatenate(rows, axis=0)

    return lay(hi), lay(lo)


def ghost_pieces(left, right, up, down):
    return (
        [right[k * CELL : (k + 1) * CELL] for k in range(3)]
        + [up[CELL : 2 * CELL], down[CELL : 2 * CELL]]
        + [left[k * CELL : (k + 1) * CELL] for k in range(3)]
    )


def second_kernel(
    pairs, count, xt, prc, feat, left, right, up, down, radial, mix, readout,
    energy, grad_own, grad_ghost, recv, send,
    table, acc, grad_acc, grad_table,
):
    atoms = feat.shape[0]
    table[0:atoms, :] = feat[...]
    for p, piece in enumerate(ghost_pieces(left, right, up, down)):
        table[atoms + p * CELL : atoms + (p + 1) * CELL, :] = piece
    acc[...] = jnp.zeros_like(acc)
    grad_table[...] = jnp.zeros_like(grad_table)
    recv[...] = jnp.zeros_like(recv)
    send[...] = jnp.zeros_like(send)

    def forward(r, c, weight):
        env, slope, scaled, vk = geometry(r, c, weight, prc, xt)
        prod = mm3(split(pair_tile(env, scaled, vk)), cell_features(table, c), NN)
        part = None
        for n in range(NB):
            rows = prod[n * CELL : (n + 1) * CELL]
            term = rows[:, :CH] * radial[0, n : n + 1, :] + rows[:, CH:] * radial[1, n : n + 1, :]
            part = term if n == 0 else part + term
        acc[pl.ds(pl.multiple_of(r * CELL, CELL), CELL), :] += part

    for_blocks(pairs, count, 2, forward)

    mix0 = split(mix[0])
    carry_w = readout[0:1, :] + mm3(split(readout[...]), split(mix[1]), NN)[1:2, :]
    row8 = iota((8, CH), 0)
    first = split(jnp.where(row8 == 0, carry_w, 0.0))
    second = split(jnp.where(row8 == 0, readout[1:2, :], 0.0))

    for i in range(atoms // CHUNK):
        rows = pl.ds(i * CHUNK, CHUNK)
        z = mm3(split(acc[rows, :]), mix0, NT)
        sg = jax.nn.sigmoid(z)
        s1 = feat[rows, :][:, :CH]
        energy[:, i * CHUNK : (i + 1) * CHUNK] = mm3(first, split(s1), NT) + mm3(second, split(z * sg), NT)
        gz = readout[1:2, :] * (sg * (1.0 + z * (1.0 - sg)))
        grad_acc[rows, :] = mm3(split(gz), mix0, NN)

    def backward(r, c, weight):
        env, slope, scaled, vk = geometry(r, c, weight, prc, xt)
        tile = split(pair_tile(env, scaled, vk))
        g = grad_acc[pl.ds(pl.multiple_of(r * CELL, CELL), CELL), :]
        u = split(
            jnp.concatenate(
                [
                    jnp.concatenate([g * radial[0, n : n + 1, :], g * radial[1, n : n + 1, :]], axis=1)
                    for n in range(NB)
                ],
                axis=0,
            )
        )
        gf = mm3(tile, u, TN)
        rows = pl.ds(pl.multiple_of(c * CELL, CELL), CELL)
        grad_table[rows, :] += jnp.concatenate(
            [gf[0:CELL, :CH]] + [gf[(t + 1) * CELL : (t + 2) * CELL, CH:] for t in range(3)], axis=1
        )
        deriv = mm3(u, cell_features(table, c), NT)
        add_force(pair_force(deriv, env, slope, scaled, vk), r, c, recv, send)

    for_blocks(pairs, count, 1, backward)
    grad_own[...] = grad_table[0:atoms, :]
    grad_ghost[...] = grad_table[atoms:, :]


def third_kernel(
    pairs, count, lists, xt, prc, grad_own, left, right, up, down, acc, gates, lifted,
    embed, radial, mix, mix_two, readout, recv_two, send_two,
    total, send,
    recv, quad, back_hi, back_lo,
):
    atoms = grad_own.shape[0]
    for p, piece in enumerate(ghost_pieces(left, right, up, down)):
        hi, lo = split(piece)
        back_hi[p * CELL : (p + 1) * CELL, :] = hi
        back_lo[p * CELL : (p + 1) * CELL, :] = lo
    recv[...] = recv_two[...]
    send[...] = send_two[...]
    weights = species_weights(embed[...], radial)
    mix04 = split(jnp.concatenate([mix[0], mix[4]], axis=0))
    mix1 = split(mix[1])
    mix3 = split(mix[3])
    carry_w = readout[0:1, :] + mm3(split(readout[...]), split(mix_two[1]), NN)[1:2, :]

    def chunk(i, carry):
        rows = pl.ds(pl.multiple_of(i * CHUNK, CHUNK), CHUNK)
        hot = jnp.where(iota((CHUNK, lists.shape[1]), 0) + i * CHUNK == lists[...], 1.0, 0.0).astype(BF16)
        g = grad_own[rows, :] + (mm(hot, back_hi[...], NN) + mm(hot, back_lo[...], NN))
        z0 = gates[rows, :][:, :CH]
        gate = gates[rows, :][:, CH:]
        gs = g[:, :CH] + carry_w
        sg = jax.nn.sigmoid(z0)
        dz0 = gs * (sg * (1.0 + z0 * (1.0 - sg)))
        gv = [g[:, (t + 1) * CH : (t + 2) * CH] for t in range(3)]
        y = [lifted[rows, :][:, t * CH : (t + 1) * CH] for t in range(3)]
        dgate = gv[0] * y[0] + gv[1] * y[1] + gv[2] * y[2]
        dz4 = dgate * gate * (1.0 - gate)
        da0 = mm3(split(jnp.concatenate([dz0, dz4], axis=1)), mix04, NN)
        dpower = 2.0 * mm3(split(dz0), mix1, NN)
        dy = mm3(split(jnp.concatenate([v * gate for v in gv], axis=0)), mix3, NN)
        a = acc[rows, :]
        parts = [da0] + [
            dy[t * CHUNK : (t + 1) * CHUNK] + a[:, (t + 1) * CH : (t + 2) * CH] * dpower for t in range(3)
        ]
        q = mm3(split(jnp.concatenate(parts, axis=1)), weights, NT)
        for n in range(NB):
            quad[n, rows, :] = q[:, n * 4 * NB : (n + 1) * 4 * NB]
        return carry

    lax.fori_loop(0, atoms // CHUNK, chunk, 0)

    def block(r, c, weight):
        env, slope, scaled, vk = geometry(r, c, weight, prc, xt)
        rows = pl.ds(pl.multiple_of(r * CELL, CELL), CELL)
        hi, lo = split(jnp.concatenate([quad[n, rows, :] for n in range(NB)], axis=0))
        hot = species_tile(c, xt)
        deriv = mm(hi, hot, NN) + mm(lo, hot, NN)
        add_force(pair_force(deriv, env, slope, scaled, vk), r, c, recv, send)

    for_blocks(pairs, count, 2, block)

    pick = jnp.where(iota((8, LANES), 0) + 1 == iota((8, LANES), 1) // CELL, 1.0, 0.0).astype(BF16)
    hi, lo = split(recv[...])
    total[...] = mm(pick, hi, NT) + mm(pick, lo, NT)


def last_kernel(total, own_send, back, lists, out):
    hi, lo = split(back[...])
    hot = jnp.where(iota((total.shape[1], lists.shape[1]), 0) == lists[...], 1.0, 0.0).astype(BF16)
    ghost = mm(hi, hot, NT) + mm(lo, hot, NT)
    out[...] = total[0:3, :] - own_send[...] - ghost[0:3, :]


def ring(axis, step):
    count = lax.axis_size(axis)
    return [(i, (i + step) % count) for i in range(count)]


def exchange(x):
    up = lax.ppermute(jnp.concatenate([x[2:3], x[4:5], x[7:8]]), "gy", ring("gy", 1))
    down = lax.ppermute(jnp.concatenate([x[0:1], x[3:4], x[5:6]]), "gy", ring("gy", -1))
    left = lax.ppermute(jnp.concatenate([up[0:1], x[1:2], down[0:1]]), "gx", ring("gx", -1))
    right = lax.ppermute(jnp.concatenate([up[2:3], x[6:7], down[2:3]]), "gx", ring("gx", 1))
    return left, right, up, down


def in_order(left, right, up, down):
    return jnp.concatenate([right, up[1:2], down[1:2], left])


def call(kernel, outs, specs, scratch=()):
    return pl.pallas_call(
        kernel,
        out_shape=[jax.ShapeDtypeStruct(s, F32) for s in outs],
        in_specs=[pl.BlockSpec(memory_space=s) for s in specs],
        out_specs=[pl.BlockSpec(memory_space=VMEM) for _ in outs],
        scratch_shapes=list(scratch),
        compiler_params=PARAMS,
    )


def shards(
    positions, species, send_lists, cell_pairs, block_count,
    embed, radial_one, mix_one, radial_two, mix_two, readout,
):
    atoms = positions.shape[1]
    side = float((atoms * 10.0) ** (1.0 / 3.0))
    pairs = cell_pairs.reshape(-1)
    count = block_count.reshape(-1)
    lists = send_lists.reshape(-1)
    lists_row = lists[None, :]
    half_one = 0.5 * radial_one
    half_two = 0.5 * radial_two
    ghosts = lists.shape[0]

    (packed,) = call(pack_kernel, [(8, ghosts)], [VMEM] * 3)(positions, species[None, :], lists_row)
    pieces = packed[:4].reshape(4, 8, CELL).transpose(1, 0, 2)
    arrived = in_order(*exchange(pieces))
    shift = np.zeros((8, 4, 1), np.float32)
    shift[:, 1, 0] = STEPS_X * side
    shift[:, 2, 0] = STEPS_Y * side
    arrived = arrived + jnp.asarray(shift)
    kinds = species.astype(F32)
    own_cells = jnp.concatenate([kinds[None], positions]).reshape(4, OWN, CELL)
    xt = jnp.tile(jnp.concatenate([own_cells, arrived.transpose(1, 0, 2)], axis=1), (1, 1, 4))
    prc = jnp.concatenate([positions, kinds[None], jnp.zeros((4, atoms), F32)]).T

    feat, sent, acc, gates, lifted = call(
        first_kernel,
        [(atoms, 4 * CH), (ghosts, 4 * CH), (atoms, 4 * CH), (atoms, 2 * CH), (atoms, 3 * CH)],
        [SMEM] * 3 + [VMEM] * 5,
        [pltpu.VMEM((NB, atoms, 4 * NB), F32)],
    )(pairs, count, lists, xt, prc, embed, half_one, mix_one)

    flat = lambda parts: [x.reshape(3 * CELL, 4 * CH) for x in parts]
    ghost_feat = flat(exchange(sent.reshape(8, CELL, 4 * CH)))
    energy, grad_own, grad_ghost, recv_two, send_two = call(
        second_kernel,
        [(8, atoms), (atoms, 4 * CH), (ghosts, 4 * CH), (atoms, LANES), (EXT, LANES)],
        [SMEM] * 2 + [VMEM] * 10,
        [
            pltpu.VMEM((atoms + ghosts, 4 * CH), F32),
            pltpu.VMEM((atoms, CH), F32),
            pltpu.VMEM((atoms, CH), F32),
            pltpu.VMEM((atoms + ghosts, 4 * CH), F32),
        ],
    )(pairs, count, xt, prc, feat, *ghost_feat, half_two, mix_two, readout)

    returned = flat(exchange(grad_ghost.reshape(8, CELL, 4 * CH)))
    total, send = call(
        third_kernel,
        [(8, atoms), (EXT, LANES)],
        [SMEM] * 2 + [VMEM] * 18,
        [
            pltpu.VMEM((atoms, LANES), F32),
            pltpu.VMEM((NB, atoms, 4 * NB), F32),
            pltpu.VMEM((ghosts, 4 * CH), BF16),
            pltpu.VMEM((ghosts, 4 * CH), BF16),
        ],
    )(
        pairs, count, lists_row, xt, prc, grad_own, *returned, acc, gates, lifted,
        embed, half_one, mix_one, mix_two, readout, recv_two, send_two,
    )

    back = in_order(*exchange(send[OWN:].reshape(8, 1, LANES)))
    back = back.reshape(8, 4, CELL).transpose(1, 0, 2)[1:].reshape(3, ghosts)
    own_send = send[:OWN].reshape(OWN, 4, CELL).transpose(1, 0, 2)[1:].reshape(3, atoms)
    (forces,) = call(last_kernel, [(3, atoms)], [VMEM] * 4)(
        total, own_send, jnp.concatenate([back, jnp.zeros((5, ghosts), F32)]), lists_row
    )
    return forces, energy[0]


def solution(mesh):
    both = P(("gx", "gy"))
    in_specs = (
        P(None, ("gx", "gy")),
        both,
        P("gx", "gy", None, None),
        P("gx", "gy", None, None),
        P("gx", "gy"),
    ) + (P(),) * 6
    out_specs = (P(None, ("gx", "gy")), both)
    return jax.shard_map(shards, mesh=mesh, in_specs=in_specs, out_specs=out_specs, check_vma=False)
```

```python
import functools

import jax
import jax.numpy as jnp
import numpy as np
from jax import lax
from jax.experimental import pallas as pl
from jax.experimental.pallas import tpu as pltpu
from jax.sharding import PartitionSpec as P

NB = 8
CELL = 32
CH = 128
LANES = 128
OWN = 16
CUT2 = 25.0
STEPS_X = np.array([-1, -1, -1, 0, 0, 1, 1, 1])
STEPS_Y = np.array([-1, 0, 1, -1, 1, -1, 0, 1])
F32 = jnp.float32
BF16 = jnp.bfloat16
VMEM = pltpu.VMEM
SMEM = pltpu.SMEM
PARAMS = pltpu.CompilerParams(vmem_limit_bytes=32 * 1024 * 1024)
CHUNK = 128
HIST = 256
FEAT = 512
SLOTS = 32
UNROLL_OWN = 8
UNROLL_GHOST = 4
UP = (2, 4, 7)
DOWN = (0, 3, 5)
MID = (1, 6)

NN = (((1,), (0,)), ((), ()))
NT = (((1,), (1,)), ((), ()))
TN = (((0,), (0,)), ((), ()))


def split(x):
    hi = x.astype(BF16)
    return hi, (x - hi.astype(F32)).astype(BF16)


def mm(a, b, dims):
    return lax.dot_general(a, b, dims, preferred_element_type=F32)


def mm3(a, b, dims):
    (ah, al), (bh, bl) = a, b
    return mm(ah, bh, dims) + (mm(ah, bl, dims) + mm(al, bh, dims))


def mm3_deep(a, b, dims):
    (ah, al), (bh, bl) = a, b
    axis = dims[0][1][0]
    return mm(jnp.concatenate([ah, al], axis=1), jnp.concatenate([bh, bh], axis=axis), dims) + mm(ah, bl, dims)


def mm3_wide(a, b, dims):
    (ah, al), (bh, bl) = a, b
    width = 128
    out = mm(ah, jnp.concatenate([bh, bl], axis=1 - dims[0][1][0]), dims)
    return out[:, :width] + (out[:, width:] + mm(al, bh, dims))


def mm3_full(a, b, dims):
    (ah, al), (bh, bl) = a, b
    axis = dims[0][1][0]
    top = jnp.concatenate([bh, bh], axis=axis)
    low = jnp.concatenate([bl, jnp.zeros_like(bl)], axis=axis)
    out = mm(jnp.concatenate([ah, al], axis=1), jnp.concatenate([top, low], axis=1 - axis), dims)
    return out[:, :128] + out[:, 128:]


def mm3_turned(a, b):
    (ah, al), (bh, bl) = a, b
    out = mm(jnp.concatenate([ah, al], axis=1), bh, TN)
    width = ah.shape[1]
    return out[:width] + (out[width:] + mm(ah, bl, TN))


def iota(shape, dim):
    return lax.broadcasted_iota(jnp.int32, shape, dim)


def cell_rows(c):
    return pl.ds(pl.multiple_of(c * CELL, CELL), CELL)


def chunk_rows(i):
    return pl.ds(pl.multiple_of(i * CHUNK, CHUNK), CHUNK)


def geometry(r, c, keep, prc, xt):
    own = prc[cell_rows(r), :]
    far = xt[c]
    vec = [far[t + 1 : t + 2, :] - own[:, t : t + 1] for t in range(3)]
    sq = vec[0] * vec[0] + vec[1] * vec[1] + vec[2] * vec[2]
    group = iota((CELL, LANES), 1) // CELL
    edge = jnp.maximum(1.0 - sq * (1.0 / CUT2), 0.0)
    slope = edge * keep
    vk = jnp.where(group == 0, 1.0, jnp.where(group == 1, vec[0], jnp.where(group == 2, vec[1], vec[2])))
    scaled = sq * ((NB - 1) / CUT2)
    return edge * slope, slope, scaled, vk


def own_keep(r, c, weight):
    lane = iota((CELL, LANES), 1)
    row = iota((CELL, LANES), 0)
    return jnp.where(jnp.logical_and(lane % CELL == row, r == c), 0.0, weight)


def basis(scaled, n):
    off = scaled - float(n)
    return jnp.exp(-(off * off))


def pair_parts(env, scaled, vk):
    m = env * vk
    return [m * basis(scaled, n) for n in range(NB)]


def pair_force(deriv, env, slope, scaled, vk):
    total = None
    moment = None
    for n in range(NB):
        term = deriv[n] * basis(scaled, n)
        total = term if n == 0 else total + term
        if n == 1:
            moment = term
        elif n > 1:
            moment = moment + float(n) * term
    spacing = CUT2 / (NB - 1)
    by_sq = (-2.0 / CUT2) * slope * total - (2.0 / spacing) * env * (scaled * total - moment)
    by_sq = by_sq * vk
    by_sq = by_sq + pltpu.roll(by_sq, 64, 1)
    by_sq = by_sq + pltpu.roll(by_sq, 32, 1)
    return env * total + 2.0 * vk * by_sq


def add_force(force, r, c, recv, send):
    recv[cell_rows(r), :] += force
    send[pl.ds(c, 1), :] += jnp.sum(force, axis=0, keepdims=True)


def species_tile(c, xt):
    row = iota((4 * NB, LANES), 0)
    lane = iota((4 * NB, LANES), 1)
    kind = xt[c][0:1, :].astype(jnp.int32)
    hit = jnp.logical_and(kind == row % NB, lane // CELL == row // NB)
    hot = jnp.where(hit, 1.0, 0.0).astype(BF16)
    zero = jnp.zeros_like(hot)
    return jnp.concatenate(
        [jnp.concatenate([hot if j == k else zero for k in range(4)], axis=1) for j in range(4)], axis=0
    )


def add_histogram(r, c, keep, prc, xt, hist):
    env, slope, scaled, vk = geometry(r, c, keep, prc, xt)
    parts = pair_parts(env, scaled, vk)
    wide = jnp.concatenate([jnp.concatenate(parts[4 * h : 4 * h + 4], axis=1) for h in range(2)], axis=0)
    out = mm(jnp.concatenate(split(wide), axis=0), species_tile(c, xt), NT)
    out = out[: 2 * CELL] + out[2 * CELL :]
    hist[cell_rows(r), :] += jnp.concatenate([out[:CELL], out[CELL:]], axis=1)


def first_deriv(r, c, xt, quad):
    q = quad[cell_rows(r), :]
    q = jnp.concatenate([q[:, :LANES], q[:, LANES:]], axis=0)
    out = mm(jnp.concatenate(split(q), axis=0), species_tile(c, xt), NN)
    out = out[: 2 * CELL] + out[2 * CELL :]
    return [out[(n // 4) * CELL : (n // 4 + 1) * CELL, (n % 4) * LANES : (n % 4 + 1) * LANES] for n in range(NB)]


def cell_features(table, c):
    hi, lo = split(table[cell_rows(c), :])
    zero = jnp.zeros((CELL, CH), BF16)

    def lay(x):
        rows = [jnp.concatenate([x[:, :CH], zero], axis=1)]
        rows += [jnp.concatenate([zero, x[:, (t + 1) * CH : (t + 2) * CH]], axis=1) for t in range(3)]
        return jnp.concatenate(rows, axis=0)

    return lay(hi), lay(lo)


def spread(g, radial):
    both = [
        jnp.concatenate([g * radial[0, n : n + 1, :], g * radial[1, n : n + 1, :]], axis=1) for n in range(NB)
    ]
    return split(jnp.concatenate(both, axis=0))


def add_forward(r, c, keep, prc, xt, table, radial, acc):
    env, slope, scaled, vk = geometry(r, c, keep, prc, xt)
    tile = split(jnp.concatenate(pair_parts(env, scaled, vk), axis=0))
    prod = mm3_deep(tile, cell_features(table, c), NN)
    part = None
    for n in range(NB):
        rows = prod[n * CELL : (n + 1) * CELL]
        term = rows[:, :CH] * radial[0, n : n + 1, :] + rows[:, CH:] * radial[1, n : n + 1, :]
        part = term if n == 0 else part + term
    acc[cell_rows(r), :] += part


def add_feature_grad(r, c, keep, prc, xt, grad_acc, radial, grad_table):
    env, slope, scaled, vk = geometry(r, c, keep, prc, xt)
    tile = split(jnp.concatenate(pair_parts(env, scaled, vk), axis=0))
    gf = mm3_turned(tile, spread(grad_acc[cell_rows(r), :], radial))
    grad_table[cell_rows(c), :] += jnp.concatenate(
        [gf[0:CELL, :CH]] + [gf[(t + 1) * CELL : (t + 2) * CELL, CH:] for t in range(3)], axis=1
    )


def second_deriv(r, c, grad_acc, radial, table):
    out = mm3_wide(spread(grad_acc[cell_rows(r), :], radial), cell_features(table, c), NT)
    return [out[n * CELL : (n + 1) * CELL] for n in range(NB)]


def for_blocks(plan, unroll, body):
    count = plan[2 * SLOTS]

    def step(i, carry):
        for k in range(unroll):
            slot = i * unroll + k
            body(plan[2 * slot], plan[2 * slot + 1], jnp.where(slot < count, 1.0, 0.0).astype(F32))
        return carry

    lax.fori_loop(0, (count + unroll - 1) // unroll, step, 0)


def species_weights(embed, radial):
    zero = jnp.zeros((NB, CH), F32)
    rows = []
    for n in range(NB):
        for k in range(4):
            part = embed * radial[min(k, 1), n : n + 1, :]
            rows.append(jnp.concatenate([part if j == k else zero for j in range(4)], axis=1))
    return split(jnp.concatenate(rows, axis=0))


def tile_group(x, k):
    x = jnp.where(iota(x.shape, 1) // CELL == k, x, 0.0)
    x = x + pltpu.roll(x, 64, 1)
    return x + pltpu.roll(x, 32, 1)


def store_pieces(pieces, up, down, mid):
    for out, order in ((up, UP), (down, DOWN), (mid, MID)):
        size = pieces[0].shape[0]
        for k, p in enumerate(order):
            out[k * size : (k + 1) * size, :] = pieces[p]


def arrived(left, right, up, down, size):
    at = lambda x, k: x[k * size : (k + 1) * size, :]
    return [at(right, 0), at(right, 1), at(right, 2), at(up, 1), at(down, 1), at(left, 0), at(left, 1), at(left, 2)]


def pack_kernel(pos_in, species_in, lists_in, up, down, mid, table_out, row_out, pos, species, lists, sems):
    copies = [
        pltpu.make_async_copy(src, dst, sems.at[k])
        for k, (src, dst) in enumerate(((pos_in, pos), (species_in, species), (lists_in, lists)))
    ]
    for copy in copies:
        copy.start()
    for copy in copies:
        copy.wait()
    kinds = species[...].astype(F32)
    table = jnp.concatenate([kinds, pos[...], jnp.zeros((4, kinds.shape[1]), F32)], axis=0)
    table_out[...] = table
    hi = table.astype(BF16)
    rest = table - hi.astype(F32)
    mid_part = rest.astype(BF16)
    low = (rest - mid_part.astype(F32)).astype(BF16)
    row = jnp.concatenate([lists[p : p + 1, :] for p in range(8)], axis=1)
    row_out[...] = row.astype(F32)
    hot = jnp.where(iota((table.shape[1], row.shape[1]), 0) == row, 1.0, 0.0).astype(BF16)
    out = mm(hi, hot, NN) + mm(mid_part, hot, NN) + mm(low, hot, NN)
    pieces = [
        jnp.concatenate([out[k : k + 1, p * CELL : (p + 1) * CELL] for k in range(4)], axis=1) for p in range(8)
    ]
    store_pieces(pieces, up, down, mid)


def weight_kernel(
    table, embed, radial_one, mix_one, radial_two, mix_two, readout,
    w_hi, w_lo, mats, begins, radial, rows, xt, prc,
):
    w_hi[...], w_lo[...] = species_weights(embed[...], 0.5 * radial_one[...])
    for k, m in enumerate((mix_one[0], mix_one[4], mix_one[1], mix_one[3], mix_two[0])):
        mats[0, k * CH : (k + 1) * CH, :], mats[1, k * CH : (k + 1) * CH, :] = split(m)
    begins[0], begins[1] = split(mm3(split(embed[...]), split(mix_one[2]), NT))
    radial[...] = 0.5 * radial_two[...]
    both = readout[...]
    rows[0:1, :] = both[0:1, :] + mm3(split(both), split(mix_two[1]), NN)[1:2, :]
    rows[1:2, :] = both[1:2, :]
    t = table[...]
    for c in range(OWN):
        xt[c] = tile_group(t[:, (c // 4) * LANES : (c // 4 + 1) * LANES], c % 4)
    prc[...] = jnp.concatenate([t[1:4], t[0:1], t[4:8]], axis=0).T


def own_first_kernel(pairs, count, xt, prc, plan_own, plan_ghost, hist):
    def clear(i, carry):
        plan_own[i] = 0
        plan_ghost[i] = 0
        return carry

    lax.fori_loop(0, 2 * SLOTS, clear, 0)

    def sort(i, carry):
        n_own, n_ghost = carry
        r, c = pairs[0, i], pairs[1, i]
        mine = c < OWN

        @pl.when(mine)
        def _():
            plan_own[2 * n_own] = r
            plan_own[2 * n_own + 1] = c

        @pl.when(jnp.logical_not(mine))
        def _():
            plan_ghost[2 * n_ghost] = r
            plan_ghost[2 * n_ghost + 1] = c - OWN

        step = mine.astype(jnp.int32)
        return n_own + step, n_ghost + 1 - step

    n_own, n_ghost = lax.fori_loop(0, count[0, 0], sort, (jnp.int32(0), jnp.int32(0)))
    plan_own[2 * SLOTS] = n_own
    plan_ghost[2 * SLOTS] = n_ghost
    hist[...] = jnp.zeros_like(hist)

    def block(r, c, weight):
        add_histogram(r, c, own_keep(r, c, weight), prc, xt, hist)

    for_blocks(plan_own, UNROLL_OWN, block)


def ghost_first_kernel(
    side, plan, lists, left, right, up, down, prc, hist_own, hist, xt, send_up, send_down, send_mid
):
    rows = jnp.concatenate(arrived(left, right, up, down, 1), axis=0)
    for k in range(4):
        part = tile_group(rows, k)
        for p in range(8):
            shift = 0.0 if k in (0, 3) else float((STEPS_X, STEPS_Y)[k - 1][p] * side)
            xt[p, k : k + 1, :] = part[p : p + 1, :] + shift
    hist[...] = hist_own[...]

    def block(r, c, weight):
        add_histogram(r, c, weight, prc, xt, hist)

    for_blocks(plan, UNROLL_GHOST, block)

    for out, order in ((send_up, UP), (send_down, DOWN), (send_mid, MID)):
        for k, p in enumerate(order):

            def gather(i, carry):
                for j in range(8):
                    at = i * 8 + j
                    out[pl.ds(k * CELL + at, 1), :] = hist[pl.ds(lists[p, at], 1), :]
                return carry

            lax.fori_loop(0, CELL // 8, gather, 0)


def first_update(joined, kind, weights, begin, mix04, mix1, mix3):
    size = joined.shape[0]
    a = mm3(split(joined), weights, NN)
    a0 = a[:, :CH]
    a1 = [a[:, (t + 1) * CH : (t + 2) * CH] for t in range(3)]
    power = a1[0] * a1[0] + a1[1] * a1[1] + a1[2] * a1[2]
    both = mm3_deep(split(a0), mix04, NT)
    z0 = both[:, :CH] + mm3_full(split(power), mix1, NT)
    gate = jax.nn.sigmoid(both[:, CH:])
    hot = jnp.where(kind == iota((size, NB), 1), 1.0, 0.0).astype(BF16)
    own = mm(hot, begin[0], NN) + mm(hot, begin[1], NN)
    lift = mm3_full(split(jnp.concatenate(a1, axis=0)), mix3, NT)
    lift = jnp.concatenate([lift[t * size : (t + 1) * size] for t in range(3)], axis=1)
    feat = jnp.concatenate(
        [z0 * jax.nn.sigmoid(z0) + own, lift * jnp.concatenate([gate] * 3, axis=1)], axis=1
    )
    return feat, a, jnp.concatenate([z0, gate], axis=1), lift


def first_pullback(gs, gv, a, gates, lift, weights, mix04, mix1, mix3):
    size = gs.shape[0]
    z0, gate = gates[:, :CH], gates[:, CH:]
    sg = jax.nn.sigmoid(z0)
    dz0 = gs * (sg * (1.0 + z0 * (1.0 - sg)))
    y = [lift[:, t * CH : (t + 1) * CH] for t in range(3)]
    dgate = gv[0] * y[0] + gv[1] * y[1] + gv[2] * y[2]
    dz4 = dgate * gate * (1.0 - gate)
    da0 = mm3_wide(split(jnp.concatenate([dz0, dz4], axis=1)), mix04, NN)
    dpower = 2.0 * mm3_full(split(dz0), mix1, NN)
    dy = mm3_full(split(jnp.concatenate([v * gate for v in gv], axis=0)), mix3, NN)
    parts = [da0] + [
        dy[t * size : (t + 1) * size] + a[:, (t + 1) * CH : (t + 2) * CH] * dpower for t in range(3)
    ]
    return mm3(split(jnp.concatenate(parts, axis=1)), weights, NT)


def mat(mats, first, rows):
    return mats[0, first : first + rows, :], mats[1, first : first + rows, :]


def mixes(mats):
    return mat(mats, 0, 2 * CH), mat(mats, 2 * CH, CH), mat(mats, 3 * CH, CH)


def features(g):
    return g[:, :CH], [g[:, (t + 1) * CH : (t + 2) * CH] for t in range(3)]


def own_update_kernel(joined, prc, w_hi, w_lo, begins, mats, feat, acc, gates, lifted):
    begin = begins[0], begins[1]
    mix_all = mixes(mats)

    def chunk(i, carry):
        rows = chunk_rows(i)
        kind = prc[rows, :][:, 3:4].astype(jnp.int32)
        out = first_update(joined[rows, :], kind, (w_hi[...], w_lo[...]), begin, *mix_all)
        feat[rows, :], acc[rows, :], gates[rows, :], lifted[rows, :] = out
        return carry

    lax.fori_loop(0, feat.shape[0] // CHUNK, chunk, 0)


def own_second_kernel(plan, prc, xt, feat, radial, acc):
    acc[...] = jnp.zeros_like(acc)

    def block(r, c, weight):
        add_forward(r, c, own_keep(r, c, weight), prc, xt, feat, radial, acc)

    for_blocks(plan, UNROLL_OWN, block)


def ghost_second_kernel(
    plan, prc, xt, left, right, up, down, w_hi, w_lo, begins, mats, acc_own, radial, readout,
    acc, grad_acc, feat, send_up, send_down, send_mid,
    joined, lin, gates, lifted, grad_table,
):
    ghosts = feat.shape[0]
    for p, piece in enumerate(arrived(left, right, up, down, CELL)):
        joined[p * CELL : (p + 1) * CELL, :] = piece
    begin = begins[0], begins[1]
    mix_all = mixes(mats)
    acc[...] = acc_own[...]
    grad_table[...] = jnp.zeros_like(grad_table)
    kinds = jnp.concatenate([xt[p][0:8, 0:CELL] for p in range(8)], axis=1).T[:, 0:1].astype(jnp.int32)
    for i in range(ghosts // CHUNK):
        rows = pl.ds(i * CHUNK, CHUNK)
        kind = kinds[i * CHUNK : (i + 1) * CHUNK]
        out = first_update(joined[rows, :], kind, (w_hi[...], w_lo[...]), begin, *mix_all)
        feat[rows, :], lin[rows, :], gates[rows, :], lifted[rows, :] = out

    def forward(r, c, weight):
        add_forward(r, c, weight, prc, xt, feat, radial, acc)

    for_blocks(plan, UNROLL_GHOST, forward)

    mix0 = mat(mats, 4 * CH, CH)

    def chunk(i, carry):
        rows = chunk_rows(i)
        z = mm3_full(split(acc[rows, :]), mix0, NT)
        sg = jax.nn.sigmoid(z)
        gz = readout[1:2, :] * (sg * (1.0 + z * (1.0 - sg)))
        grad_acc[rows, :] = mm3_full(split(gz), mix0, NN)
        return carry

    lax.fori_loop(0, acc.shape[0] // CHUNK, chunk, 0)

    def backward(r, c, weight):
        add_feature_grad(r, c, weight, prc, xt, grad_acc, radial, grad_table)

    for_blocks(plan, UNROLL_GHOST, backward)

    pieces = []
    for i in range(ghosts // CHUNK):
        rows = pl.ds(i * CHUNK, CHUNK)
        gs, gv = features(grad_table[rows, :])
        q = first_pullback(gs, gv, lin[rows, :], gates[rows, :], lifted[rows, :], (w_hi[...], w_lo[...]), *mix_all)
        pieces += [q[k * CELL : (k + 1) * CELL] for k in range(CHUNK // CELL)]
    store_pieces(pieces, send_up, send_down, send_mid)


def own_grad_kernel(
    plan, prc, xt, grad_acc, radial, acc, feat, lin, gates, lifted, w_hi, w_lo, mats, readout,
    quad, energy,
    grad_table,
):
    atoms = feat.shape[0]
    grad_table[...] = jnp.zeros_like(grad_table)

    def block(r, c, weight):
        add_feature_grad(r, c, own_keep(r, c, weight), prc, xt, grad_acc, radial, grad_table)

    for_blocks(plan, UNROLL_OWN, block)
    mix_all = mixes(mats)
    mix0 = mat(mats, 4 * CH, CH)
    carry_w = readout[0:1, :]
    row8 = iota((8, CH), 0)
    first = split(jnp.where(row8 == 0, carry_w, 0.0))
    second = split(jnp.where(row8 == 0, readout[1:2, :], 0.0))
    for i in range(atoms // CHUNK):
        rows = pl.ds(i * CHUNK, CHUNK)
        z = mm3_full(split(acc[rows, :]), mix0, NT)
        s1 = feat[rows, :][:, :CH]
        e = mm3(first, split(s1), NT) + mm3(second, split(z * jax.nn.sigmoid(z)), NT)
        energy[:, i * CHUNK : (i + 1) * CHUNK] = e[0:1, :]

    def chunk(i, carry):
        rows = chunk_rows(i)
        gs, gv = features(grad_table[rows, :])
        quad[rows, :] = first_pullback(
            gs + carry_w, gv, lin[rows, :], gates[rows, :], lifted[rows, :], (w_hi[...], w_lo[...]), *mix_all
        )
        return carry

    lax.fori_loop(0, atoms // CHUNK, chunk, 0)


def ghost_force_kernel(plan, prc, xt, grad_acc, radial, feat, recv, send):
    recv[...] = jnp.zeros_like(recv)
    send[...] = jnp.zeros_like(send)

    def block(r, c, weight):
        env, slope, scaled, vk = geometry(r, c, weight, prc, xt)
        deriv = second_deriv(r, c, grad_acc, radial, feat)
        add_force(pair_force(deriv, env, slope, scaled, vk), r, c, recv, send)

    for_blocks(plan, UNROLL_GHOST, block)


def ghost_last_kernel(
    plan, lists, prc, xt, quad_own, left, right, up, down, recv_two, send_two,
    quad, recv, send_up, send_down, send_mid,
    back_hi, back_lo, send,
):
    for p, piece in enumerate(arrived(left, right, up, down, CELL)):
        hi, lo = split(piece)
        back_hi[p * CELL : (p + 1) * CELL, :] = hi
        back_lo[p * CELL : (p + 1) * CELL, :] = lo
    recv[...] = recv_two[...]
    send[...] = send_two[...]
    row = lists[...].astype(jnp.int32)

    def chunk(i, carry):
        rows = chunk_rows(i)
        hot = jnp.where(iota((CHUNK, row.shape[1]), 0) + i * CHUNK == row, 1.0, 0.0).astype(BF16)
        quad[rows, :] = quad_own[rows, :] + (mm(hot, back_hi[...], NN) + mm(hot, back_lo[...], NN))
        return carry

    lax.fori_loop(0, quad.shape[0] // CHUNK, chunk, 0)

    def block(r, c, weight):
        env, slope, scaled, vk = geometry(r, c, weight, prc, xt)
        add_force(pair_force(first_deriv(r, c, xt, quad), env, slope, scaled, vk), r, c, recv, send)

    for_blocks(plan, UNROLL_GHOST, block)
    store_pieces([send[p : p + 1, :] for p in range(8)], send_up, send_down, send_mid)


def by_axis(rows, count):
    lines = [
        jnp.concatenate([rows[p : p + 1, (t + 1) * CELL : (t + 2) * CELL] for p in range(count)], axis=1)
        for t in range(3)
    ]
    return lines


def own_force_kernel(plan, prc, xt, quad, grad_acc, radial, feat, recv_ghost, out, recv, send):
    recv[...] = recv_ghost[...]
    send[...] = jnp.zeros_like(send)

    def block(r, c, weight):
        env, slope, scaled, vk = geometry(r, c, own_keep(r, c, weight), prc, xt)
        one = first_deriv(r, c, xt, quad)
        two = second_deriv(r, c, grad_acc, radial, feat)
        deriv = [x + y for x, y in zip(one, two)]
        add_force(pair_force(deriv, env, slope, scaled, vk), r, c, recv, send)

    for_blocks(plan, UNROLL_OWN, block)
    pick = jnp.where(iota((8, LANES), 0) + 1 == iota((8, LANES), 1) // CELL, 1.0, 0.0).astype(BF16)
    hi, lo = split(recv[...])
    total = mm(pick, hi, NT) + mm(pick, lo, NT)
    out[...] = total[0:3, :] - jnp.concatenate(by_axis(send, OWN), axis=0)


def last_kernel(lists, left, right, up, down, partial, out):
    rows = jnp.concatenate(arrived(left, right, up, down, 1), axis=0)
    lines = by_axis(rows, 8)
    back = jnp.concatenate(lines + [jnp.zeros((5, lines[0].shape[1]), F32)], axis=0)
    hi, lo = split(back)
    row = lists[...].astype(jnp.int32)
    hot = jnp.where(iota((partial.shape[1], row.shape[1]), 0) == row, 1.0, 0.0).astype(BF16)
    ghost = mm(hi, hot, NT) + mm(lo, hot, NT)
    out[...] = partial[...] - ghost[0:3, :]


def ring(axis, step):
    count = lax.axis_size(axis)
    return [(i, (i + step) % count) for i in range(count)]


def exchange(up, down, mid, between=None):
    size = mid.shape[0] // 2
    part = lambda x, k: x[k * size : (k + 1) * size]
    up = lax.ppermute(up, "gy", ring("gy", 1))
    down = lax.ppermute(down, "gy", ring("gy", -1))
    if between is not None:
        up, down, between = lax.optimization_barrier((up, down, between))
    left = lax.ppermute(jnp.concatenate([part(up, 0), part(mid, 0), part(down, 0)]), "gx", ring("gx", -1))
    right = lax.ppermute(jnp.concatenate([part(up, 2), part(mid, 1), part(down, 2)]), "gx", ring("gx", 1))
    return (left, right, up, down), between


def call(kernel, outs, specs, scratch=()):
    spaces = [SMEM if s[1] == jnp.int32 else VMEM for s in outs]
    return pl.pallas_call(
        kernel,
        out_shape=[jax.ShapeDtypeStruct(*s) for s in outs],
        in_specs=[pl.BlockSpec(memory_space=s) for s in specs],
        out_specs=[pl.BlockSpec(memory_space=s) for s in spaces],
        scratch_shapes=list(scratch),
        compiler_params=PARAMS,
    )


def shards(
    positions, species, send_lists, cell_pairs, block_count,
    embed, radial_one, mix_one, radial_two, mix_two, readout,
):
    atoms = positions.shape[1]
    side = float((atoms * 10.0) ** (1.0 / 3.0))
    pairs = cell_pairs[0, 0].T
    lists = send_lists[0, 0]
    kinds = species[None, :]
    ghosts = lists.size
    f = lambda *shape: (shape, F32)
    b = lambda *shape: (shape, BF16)
    i = lambda *shape: (shape, jnp.int32)
    three = lambda size, width: [f(3 * size, width), f(3 * size, width), f(2 * size, width)]

    *sends, table, row = call(
        pack_kernel,
        three(1, LANES) + [f(8, atoms), f(1, ghosts)],
        [pl.ANY] * 3,
        [
            VMEM((3, atoms), F32),
            VMEM((1, atoms), jnp.int32),
            VMEM((8, CELL), jnp.int32),
            pltpu.SemaphoreType.DMA((3,)),
        ],
    )(positions, kinds, lists)
    ready = call(
        weight_kernel,
        [
            b(HIST, FEAT), b(HIST, FEAT), b(2, 5 * CH, CH), b(2, NB, CH), f(2, NB, CH), f(2, CH),
            f(OWN, 8, LANES), f(atoms, 8),
        ],
        [VMEM] * 7,
    )(table, embed, radial_one, mix_one, radial_two, mix_two, readout)
    moved, ready = exchange(*sends, ready)
    w_hi, w_lo, mats, begins, radial, rows, xt_own, prc = ready
    plan_own, plan_ghost, hist_own = call(
        own_first_kernel, [i(2 * SLOTS + 1), i(2 * SLOTS + 1), f(atoms, HIST)], [SMEM] * 2 + [VMEM] * 2
    )(pairs, block_count, xt_own, prc)
    hist, xt_ghost, *sends = call(
        functools.partial(ghost_first_kernel, side),
        [f(atoms, HIST), f(8, 8, LANES)] + three(CELL, HIST),
        [SMEM] * 2 + [VMEM] * 6,
    )(plan_ghost, lists, *moved, prc, hist_own)

    own = call(
        own_update_kernel, [f(atoms, FEAT), f(atoms, FEAT), f(atoms, 2 * CH), f(atoms, 3 * CH)], [VMEM] * 6
    )(hist, prc, w_hi, w_lo, begins, mats)
    moved, own = exchange(*sends, own)
    feat, lin, gates, lifted = own
    (acc_own,) = call(own_second_kernel, [f(atoms, CH)], [SMEM] + [VMEM] * 4)(
        plan_own, prc, xt_own, feat, radial
    )
    acc, grad_acc, feat_ghost, *sends = call(
        ghost_second_kernel,
        [f(atoms, CH), f(atoms, CH), f(ghosts, FEAT)] + three(CELL, HIST),
        [SMEM] + [VMEM] * 13,
        [
            VMEM((ghosts, HIST), F32),
            VMEM((ghosts, FEAT), F32),
            VMEM((ghosts, 2 * CH), F32),
            VMEM((ghosts, 3 * CH), F32),
            VMEM((ghosts, FEAT), F32),
        ],
    )(plan_ghost, prc, xt_ghost, *moved, w_hi, w_lo, begins, mats, acc_own, radial, rows)

    two = call(ghost_force_kernel, [f(atoms, LANES), f(8, LANES)], [SMEM] + [VMEM] * 5)(
        plan_ghost, prc, xt_ghost, grad_acc, radial, feat_ghost
    )
    moved, two = exchange(*sends, two)
    recv_two, send_two = two
    quad_own, energy = call(
        own_grad_kernel, [f(atoms, HIST), f(1, atoms)], [SMEM] + [VMEM] * 13, [VMEM((atoms, FEAT), F32)]
    )(plan_own, prc, xt_own, grad_acc, radial, acc, feat, lin, gates, lifted, w_hi, w_lo, mats, rows)
    quad, recv, *sends = call(
        ghost_last_kernel,
        [f(atoms, HIST), f(atoms, LANES)] + three(1, LANES),
        [SMEM] + [VMEM] * 10,
        [VMEM((ghosts, HIST), BF16), VMEM((ghosts, HIST), BF16), VMEM((8, LANES), F32)],
    )(plan_ghost, row, prc, xt_ghost, quad_own, *moved, recv_two, send_two)

    moved, unused = exchange(*sends)
    (partial,) = call(
        own_force_kernel,
        [f(3, atoms)],
        [SMEM] + [VMEM] * 7,
        [VMEM((atoms, LANES), F32), VMEM((OWN, LANES), F32)],
    )(plan_own, prc, xt_own, quad, grad_acc, radial, feat, recv)
    (forces,) = call(last_kernel, [f(3, atoms)], [VMEM] * 6)(row, *moved, partial)
    return forces, energy[0]


def solution(mesh):
    both = P(("gx", "gy"))
    in_specs = (
        P(None, ("gx", "gy")),
        both,
        P("gx", "gy", None, None),
        P("gx", "gy", None, None),
        P("gx", "gy"),
    ) + (P(),) * 6
    out_specs = (P(None, ("gx", "gy")), both)
    return jax.shard_map(shards, mesh=mesh, in_specs=in_specs, out_specs=out_specs, check_vma=False)
```

```python
import functools

import jax
import jax.numpy as jnp
import numpy as np
from jax import lax
from jax.experimental import pallas as pl
from jax.experimental.pallas import tpu as pltpu
from jax.sharding import PartitionSpec as P

NB = 8
CELL = 32
CH = 128
LANES = 128
OWN = 16
CUT2 = 25.0
STEPS_X = np.array([-1, -1, -1, 0, 0, 1, 1, 1])
STEPS_Y = np.array([-1, 0, 1, -1, 1, -1, 0, 1])
F32 = jnp.float32
BF16 = jnp.bfloat16
VMEM = pltpu.VMEM
SMEM = pltpu.SMEM
HBM = pltpu.HBM
PARAMS = pltpu.CompilerParams(vmem_limit_bytes=32 * 1024 * 1024)
CHUNK = 128
HIST = 256
FEAT = 512
SLOTS = 32
UNROLL_OWN = 8
UNROLL_GHOST = 4
UP = (2, 4, 7)
DOWN = (0, 3, 5)
MID = (1, 6)

NN = (((1,), (0,)), ((), ()))
NT = (((1,), (1,)), ((), ()))
TN = (((0,), (0,)), ((), ()))


def split(x):
    hi = x.astype(BF16)
    return hi, (x - hi.astype(F32)).astype(BF16)


def mm(a, b, dims):
    return lax.dot_general(a, b, dims, preferred_element_type=F32)


def mm3(a, b, dims):
    (ah, al), (bh, bl) = a, b
    return mm(ah, bh, dims) + (mm(ah, bl, dims) + mm(al, bh, dims))


def mm3_deep(a, b, dims):
    (ah, al), (bh, bl) = a, b
    axis = dims[0][1][0]
    return mm(jnp.concatenate([ah, al], axis=1), jnp.concatenate([bh, bh], axis=axis), dims) + mm(ah, bl, dims)


def mm3_wide(a, b, dims):
    (ah, al), (bh, bl) = a, b
    width = 128
    out = mm(ah, jnp.concatenate([bh, bl], axis=1 - dims[0][1][0]), dims)
    return out[:, :width] + (out[:, width:] + mm(al, bh, dims))


def mm3_full(a, b, dims):
    (ah, al), (bh, bl) = a, b
    axis = dims[0][1][0]
    top = jnp.concatenate([bh, bh], axis=axis)
    low = jnp.concatenate([bl, jnp.zeros_like(bl)], axis=axis)
    out = mm(jnp.concatenate([ah, al], axis=1), jnp.concatenate([top, low], axis=1 - axis), dims)
    return out[:, :128] + out[:, 128:]


def iota(shape, dim):
    return lax.broadcasted_iota(jnp.int32, shape, dim)


def cell_rows(c):
    return pl.ds(pl.multiple_of(c * CELL, CELL), CELL)


def chunk_rows(i):
    return pl.ds(pl.multiple_of(i * CHUNK, CHUNK), CHUNK)


def geometry(r, c, keep, prc, xt):
    own = prc[cell_rows(r), :]
    far = xt[c]
    vec = [far[t + 1 : t + 2, :] - own[:, t : t + 1] for t in range(3)]
    sq = vec[0] * vec[0] + vec[1] * vec[1] + vec[2] * vec[2]
    group = iota((CELL, LANES), 1) // CELL
    edge = jnp.maximum(1.0 - sq * (1.0 / CUT2), 0.0)
    slope = edge * keep
    vk = jnp.where(group == 0, 1.0, jnp.where(group == 1, vec[0], jnp.where(group == 2, vec[1], vec[2])))
    scaled = sq * ((NB - 1) / CUT2)
    return edge * slope, slope, scaled, vk


def own_keep(r, c, weight):
    lane = iota((CELL, LANES), 1)
    row = iota((CELL, LANES), 0)
    return jnp.where(jnp.logical_and(lane % CELL == row, r == c), 0.0, weight)


def basis(scaled, n):
    off = scaled - float(n)
    return jnp.exp(-(off * off))


def pair_parts(env, scaled, vk):
    m = env * vk
    return [m * basis(scaled, n) for n in range(NB)]


def pair_force(deriv, env, slope, scaled, vk):
    total = None
    moment = None
    for n in range(NB):
        term = deriv[n] * basis(scaled, n)
        total = term if n == 0 else total + term
        if n == 1:
            moment = term
        elif n > 1:
            moment = moment + float(n) * term
    spacing = CUT2 / (NB - 1)
    by_sq = (-2.0 / CUT2) * slope * total - (2.0 / spacing) * env * (scaled * total - moment)
    by_sq = by_sq * vk
    by_sq = by_sq + pltpu.roll(by_sq, 64, 1)
    by_sq = by_sq + pltpu.roll(by_sq, 32, 1)
    return env * total + 2.0 * vk * by_sq


def add_force(force, r, c, recv, send):
    recv[cell_rows(r), :] += force
    send[pl.ds(c, 1), :] += jnp.sum(force, axis=0, keepdims=True)


def species_tile(c, xt):
    row = iota((4 * NB, LANES), 0)
    lane = iota((4 * NB, LANES), 1)
    kind = xt[c][0:1, :].astype(jnp.int32)
    hit = jnp.logical_and(kind == row % NB, lane // CELL == row // NB)
    hot = jnp.where(hit, 1.0, 0.0).astype(BF16)
    zero = jnp.zeros_like(hot)
    return jnp.concatenate(
        [jnp.concatenate([hot if j == k else zero for k in range(4)], axis=1) for j in range(4)], axis=0
    )


def add_histogram(r, c, keep, prc, xt, hist):
    env, slope, scaled, vk = geometry(r, c, keep, prc, xt)
    parts = pair_parts(env, scaled, vk)
    wide = jnp.concatenate([jnp.concatenate(parts[4 * h : 4 * h + 4], axis=1) for h in range(2)], axis=0)
    out = mm(jnp.concatenate(split(wide), axis=0), species_tile(c, xt), NT)
    out = out[: 2 * CELL] + out[2 * CELL :]
    hist[cell_rows(r), :] += jnp.concatenate([out[:CELL], out[CELL:]], axis=1)


def first_deriv(r, c, xt, quad):
    q = quad[cell_rows(r), :]
    q = jnp.concatenate([q[:, :LANES], q[:, LANES:]], axis=0)
    out = mm(jnp.concatenate(split(q), axis=0), species_tile(c, xt), NN)
    out = out[: 2 * CELL] + out[2 * CELL :]
    return [out[(n // 4) * CELL : (n // 4 + 1) * CELL, (n % 4) * LANES : (n % 4 + 1) * LANES] for n in range(NB)]


def cell_features(table, c):
    hi, lo = split(table[cell_rows(c), :])
    zero = jnp.zeros((CELL, CH), BF16)

    def lay(x):
        rows = [jnp.concatenate([x[:, :CH], zero], axis=1)]
        rows += [jnp.concatenate([zero, x[:, (t + 1) * CH : (t + 2) * CH]], axis=1) for t in range(3)]
        return jnp.concatenate(rows, axis=0)

    return lay(hi), lay(lo)


def spread(g, radial):
    both = [
        jnp.concatenate([g * radial[0, n : n + 1, :], g * radial[1, n : n + 1, :]], axis=1) for n in range(NB)
    ]
    return split(jnp.concatenate(both, axis=0))


def pair_tile(r, c, keep, prc, xt):
    env, slope, scaled, vk = geometry(r, c, keep, prc, xt)
    return jnp.concatenate(split(jnp.concatenate(pair_parts(env, scaled, vk), axis=0)), axis=1)


def add_forward(r, c, tile, table, radial, acc):
    fh, fl = cell_features(table, c)
    prod = mm(tile, jnp.concatenate([fh, fh], axis=0), NN) + mm(tile[:, :LANES], fl, NN)
    part = None
    for n in range(NB):
        rows = prod[n * CELL : (n + 1) * CELL]
        term = rows[:, :CH] * radial[0, n : n + 1, :] + rows[:, CH:] * radial[1, n : n + 1, :]
        part = term if n == 0 else part + term
    acc[cell_rows(r), :] += part


def add_feature_grad(r, c, tile, grad_acc, radial, grad_table):
    uh, ul = spread(grad_acc[cell_rows(r), :], radial)
    gf = mm(tile, uh, TN)
    gf = gf[:LANES] + (gf[LANES:] + mm(tile[:, :LANES], ul, TN))
    grad_table[cell_rows(c), :] += jnp.concatenate(
        [gf[0:CELL, :CH]] + [gf[(t + 1) * CELL : (t + 2) * CELL, CH:] for t in range(3)], axis=1
    )


def second_deriv(r, c, grad_acc, radial, table):
    out = mm3_wide(spread(grad_acc[cell_rows(r), :], radial), cell_features(table, c), NT)
    return [out[n * CELL : (n + 1) * CELL] for n in range(NB)]


def for_blocks(plan, unroll, body):
    count = plan[2 * SLOTS]

    def step(i, carry):
        for k in range(unroll):
            slot = i * unroll + k
            body(plan[2 * slot], plan[2 * slot + 1], jnp.where(slot < count, 1.0, 0.0).astype(F32), slot)
        return carry

    lax.fori_loop(0, (count + unroll - 1) // unroll, step, 0)


def species_weights(embed, radial):
    zero = jnp.zeros((NB, CH), F32)
    rows = []
    for n in range(NB):
        for k in range(4):
            part = embed * radial[min(k, 1), n : n + 1, :]
            rows.append(jnp.concatenate([part if j == k else zero for j in range(4)], axis=1))
    return split(jnp.concatenate(rows, axis=0))


def tile_group(x, k):
    x = jnp.where(iota(x.shape, 1) // CELL == k, x, 0.0)
    x = x + pltpu.roll(x, 64, 1)
    return x + pltpu.roll(x, 32, 1)


def store_pieces(pieces, up, down, mid):
    for out, order in ((up, UP), (down, DOWN), (mid, MID)):
        size = pieces[0].shape[0]
        for k, p in enumerate(order):
            out[k * size : (k + 1) * size, :] = pieces[p]


def arrived(left, right, up, down, size):
    at = lambda x, k: x[k * size : (k + 1) * size, :]
    return [at(right, 0), at(right, 1), at(right, 2), at(up, 1), at(down, 1), at(left, 0), at(left, 1), at(left, 2)]


def fetch(sems, *pairs):
    copies = [pltpu.make_async_copy(src, dst, sems.at[k]) for k, (src, dst) in enumerate(pairs)]
    for copy in copies:
        copy.start()
    return copies


def arrive(copies):
    for copy in copies:
        copy.wait()


def pack_kernel(pos_in, species_in, lists_in, up, down, mid, table_out, row_out, pos, species, lists, sems):
    arrive(fetch(sems, (pos_in, pos), (species_in, species), (lists_in, lists)))
    kinds = species[...].astype(F32)
    table = jnp.concatenate([kinds, pos[...], jnp.zeros((4, kinds.shape[1]), F32)], axis=0)
    table_out[...] = table
    hi = table.astype(BF16)
    rest = table - hi.astype(F32)
    mid_part = rest.astype(BF16)
    low = (rest - mid_part.astype(F32)).astype(BF16)
    row = jnp.concatenate([lists[p : p + 1, :] for p in range(8)], axis=1)
    row_out[...] = row.astype(F32)
    hot = jnp.where(iota((table.shape[1], row.shape[1]), 0) == row, 1.0, 0.0).astype(BF16)
    out = mm(hi, hot, NN) + mm(mid_part, hot, NN) + mm(low, hot, NN)
    pieces = [
        jnp.concatenate([out[k : k + 1, p * CELL : (p + 1) * CELL] for k in range(4)], axis=1) for p in range(8)
    ]
    store_pieces(pieces, up, down, mid)


def weight_kernel(
    count, table, row, pairs_in, lists_in, embed_in, radial_one_in, mix_one_in, radial_two_in, mix_two_in, readout_in,
    w_hi, w_lo, mats, begins, radial, rows, xt, prc, hot, plan_own, plan_ghost, lists_out,
    pairs, embed, radial_one, mix_one, radial_two, mix_two, readout, sems,
):
    sources = (pairs_in, lists_in, embed_in, radial_one_in, mix_one_in, radial_two_in, mix_two_in, readout_in)
    targets = (pairs, lists_out, embed, radial_one, mix_one, radial_two, mix_two, readout)
    copies = fetch(sems, *zip(sources, targets))
    lists = row[...].astype(jnp.int32)
    hot[...] = jnp.where(iota(hot.shape, 0) == lists, 1.0, 0.0).astype(BF16)
    t = table[...]
    for c in range(OWN):
        xt[c] = tile_group(t[:, (c // 4) * LANES : (c // 4 + 1) * LANES], c % 4)
    prc[...] = jnp.concatenate([t[1:4], t[0:1], t[4:8]], axis=0).T
    arrive(copies[:1])
    def clear(i, carry):
        plan_own[i] = 0
        plan_ghost[i] = 0
        return carry

    lax.fori_loop(0, 2 * SLOTS, clear, 0)

    def sort(i, carry):
        n_own, n_ghost = carry
        r, c = pairs[0, i], pairs[1, i]
        mine = c < OWN

        @pl.when(mine)
        def _():
            plan_own[2 * n_own] = r
            plan_own[2 * n_own + 1] = c

        @pl.when(jnp.logical_not(mine))
        def _():
            plan_ghost[2 * n_ghost] = r
            plan_ghost[2 * n_ghost + 1] = c - OWN

        step = mine.astype(jnp.int32)
        return n_own + step, n_ghost + 1 - step

    n_own, n_ghost = lax.fori_loop(0, count[0, 0], sort, (jnp.int32(0), jnp.int32(0)))
    plan_own[2 * SLOTS] = n_own
    plan_ghost[2 * SLOTS] = n_ghost
    arrive(copies[1:])
    w_hi[...], w_lo[...] = species_weights(embed[...], 0.5 * radial_one[...])
    for k, m in enumerate((mix_one[0], mix_one[4], mix_one[1], mix_one[3], mix_two[0])):
        mats[0, k * CH : (k + 1) * CH, :], mats[1, k * CH : (k + 1) * CH, :] = split(m)
    begins[0], begins[1] = split(mm3(split(embed[...]), split(mix_one[2]), NT))
    radial[...] = 0.5 * radial_two[...]
    both = readout[...]
    rows[0:1, :] = both[0:1, :] + mm3(split(both), split(mix_two[1]), NN)[1:2, :]
    rows[1:2, :] = both[1:2, :]


def own_first_kernel(plan_own, xt, prc, hist):
    hist[...] = jnp.zeros_like(hist)

    def block(r, c, weight, slot):
        add_histogram(r, c, own_keep(r, c, weight), prc, xt, hist)

    for_blocks(plan_own, UNROLL_OWN, block)


def ghost_first_kernel(
    side, plan, lists, left, right, up, down, prc, hist_own, hist, xt, send_up, send_down, send_mid
):
    rows = jnp.concatenate(arrived(left, right, up, down, 1), axis=0)
    for k in range(4):
        part = tile_group(rows, k)
        for p in range(8):
            shift = 0.0 if k in (0, 3) else float((STEPS_X, STEPS_Y)[k - 1][p] * side)
            xt[p, k : k + 1, :] = part[p : p + 1, :] + shift
    hist[...] = hist_own[...]

    def block(r, c, weight, slot):
        add_histogram(r, c, weight, prc, xt, hist)

    for_blocks(plan, UNROLL_GHOST, block)

    for out, order in ((send_up, UP), (send_down, DOWN), (send_mid, MID)):
        for k, p in enumerate(order):

            def gather(i, carry):
                for j in range(8):
                    at = i * 8 + j
                    out[pl.ds(k * CELL + at, 1), :] = hist[pl.ds(lists[p, at], 1), :]
                return carry

            lax.fori_loop(0, CELL // 8, gather, 0)


def first_update(joined, kind, weights, begin, mix04, mix1, mix3):
    size = joined.shape[0]
    a = mm3(split(joined), weights, NN)
    a0 = a[:, :CH]
    a1 = [a[:, (t + 1) * CH : (t + 2) * CH] for t in range(3)]
    power = a1[0] * a1[0] + a1[1] * a1[1] + a1[2] * a1[2]
    both = mm3_deep(split(a0), mix04, NT)
    z0 = both[:, :CH] + mm3_full(split(power), mix1, NT)
    gate = jax.nn.sigmoid(both[:, CH:])
    hot = jnp.where(kind == iota((size, NB), 1), 1.0, 0.0).astype(BF16)
    own = mm(hot, begin[0], NN) + mm(hot, begin[1], NN)
    lift = mm3_full(split(jnp.concatenate(a1, axis=0)), mix3, NT)
    lift = jnp.concatenate([lift[t * size : (t + 1) * size] for t in range(3)], axis=1)
    feat = jnp.concatenate(
        [z0 * jax.nn.sigmoid(z0) + own, lift * jnp.concatenate([gate] * 3, axis=1)], axis=1
    )
    return feat, a, jnp.concatenate([z0, gate], axis=1), lift


def first_pullback(gs, gv, a, gates, lift, weights, mix04, mix1, mix3):
    size = gs.shape[0]
    z0, gate = gates[:, :CH], gates[:, CH:]
    sg = jax.nn.sigmoid(z0)
    dz0 = gs * (sg * (1.0 + z0 * (1.0 - sg)))
    y = [lift[:, t * CH : (t + 1) * CH] for t in range(3)]
    dgate = gv[0] * y[0] + gv[1] * y[1] + gv[2] * y[2]
    dz4 = dgate * gate * (1.0 - gate)
    da0 = mm3_wide(split(jnp.concatenate([dz0, dz4], axis=1)), mix04, NN)
    dpower = 2.0 * mm3_full(split(dz0), mix1, NN)
    dy = mm3_full(split(jnp.concatenate([v * gate for v in gv], axis=0)), mix3, NN)
    parts = [da0] + [
        dy[t * size : (t + 1) * size] + a[:, (t + 1) * CH : (t + 2) * CH] * dpower for t in range(3)
    ]
    return mm3(split(jnp.concatenate(parts, axis=1)), weights, NT)


def mat(mats, first, rows):
    return mats[0, first : first + rows, :], mats[1, first : first + rows, :]


def mixes(mats):
    return mat(mats, 0, 2 * CH), mat(mats, 2 * CH, CH), mat(mats, 3 * CH, CH)


def features(g):
    return g[:, :CH], [g[:, (t + 1) * CH : (t + 2) * CH] for t in range(3)]


def own_update_kernel(joined, prc, w_hi, w_lo, begins, mats, feat, acc, gates, lifted):
    begin = begins[0], begins[1]
    mix_all = mixes(mats)

    def chunk(i, carry):
        rows = chunk_rows(i)
        kind = prc[rows, :][:, 3:4].astype(jnp.int32)
        out = first_update(joined[rows, :], kind, (w_hi[...], w_lo[...]), begin, *mix_all)
        feat[rows, :], acc[rows, :], gates[rows, :], lifted[rows, :] = out
        return carry

    lax.fori_loop(0, feat.shape[0] // CHUNK, chunk, 0)


def own_second_kernel(plan, plan_ghost, prc, xt, xt_ghost, feat, radial, acc, tiles, tiles_ghost):
    acc[...] = jnp.zeros_like(acc)

    def block(r, c, weight, slot):
        tile = pair_tile(r, c, own_keep(r, c, weight), prc, xt)
        tiles[slot] = tile
        add_forward(r, c, tile, feat, radial, acc)

    for_blocks(plan, UNROLL_OWN, block)

    def ghost(r, c, weight, slot):
        tiles_ghost[slot] = pair_tile(r, c, weight, prc, xt_ghost)

    for_blocks(plan_ghost, UNROLL_GHOST, ghost)


def ghost_second_kernel(
    plan, tiles, xt, left, right, up, down, w_hi, w_lo, begins, mats, acc_own, radial, readout,
    acc, grad_acc, feat, send_up, send_down, send_mid,
    joined, lin, gates, lifted, grad_table,
):
    ghosts = feat.shape[0]
    for p, piece in enumerate(arrived(left, right, up, down, CELL)):
        joined[p * CELL : (p + 1) * CELL, :] = piece
    begin = begins[0], begins[1]
    mix_all = mixes(mats)
    acc[...] = acc_own[...]
    grad_table[...] = jnp.zeros_like(grad_table)
    kinds = jnp.concatenate([xt[p][0:8, 0:CELL] for p in range(8)], axis=1).T[:, 0:1].astype(jnp.int32)
    for i in range(ghosts // CHUNK):
        rows = pl.ds(i * CHUNK, CHUNK)
        kind = kinds[i * CHUNK : (i + 1) * CHUNK]
        out = first_update(joined[rows, :], kind, (w_hi[...], w_lo[...]), begin, *mix_all)
        feat[rows, :], lin[rows, :], gates[rows, :], lifted[rows, :] = out

    def forward(r, c, weight, slot):
        add_forward(r, c, tiles[slot], feat, radial, acc)

    for_blocks(plan, UNROLL_GHOST, forward)

    mix0 = mat(mats, 4 * CH, CH)

    def chunk(i, carry):
        rows = chunk_rows(i)
        z = mm3_full(split(acc[rows, :]), mix0, NT)
        sg = jax.nn.sigmoid(z)
        gz = readout[1:2, :] * (sg * (1.0 + z * (1.0 - sg)))
        grad_acc[rows, :] = mm3_full(split(gz), mix0, NN)
        return carry

    lax.fori_loop(0, acc.shape[0] // CHUNK, chunk, 0)

    def backward(r, c, weight, slot):
        add_feature_grad(r, c, tiles[slot], grad_acc, radial, grad_table)

    for_blocks(plan, UNROLL_GHOST, backward)

    pieces = []
    for i in range(ghosts // CHUNK):
        rows = pl.ds(i * CHUNK, CHUNK)
        gs, gv = features(grad_table[rows, :])
        q = first_pullback(gs, gv, lin[rows, :], gates[rows, :], lifted[rows, :], (w_hi[...], w_lo[...]), *mix_all)
        pieces += [q[k * CELL : (k + 1) * CELL] for k in range(CHUNK // CELL)]
    store_pieces(pieces, send_up, send_down, send_mid)


def own_grad_kernel(
    plan, tiles, grad_acc, radial, lin, gates, lifted, w_hi, w_lo, mats, readout,
    quad,
    grad_table,
):
    atoms = quad.shape[0]
    grad_table[...] = jnp.zeros_like(grad_table)

    def block(r, c, weight, slot):
        add_feature_grad(r, c, tiles[slot], grad_acc, radial, grad_table)

    for_blocks(plan, UNROLL_OWN, block)
    mix_all = mixes(mats)
    carry_w = readout[0:1, :]

    def chunk(i, carry):
        rows = chunk_rows(i)
        gs, gv = features(grad_table[rows, :])
        quad[rows, :] = first_pullback(
            gs + carry_w, gv, lin[rows, :], gates[rows, :], lifted[rows, :], (w_hi[...], w_lo[...]), *mix_all
        )
        return carry

    lax.fori_loop(0, atoms // CHUNK, chunk, 0)


def ghost_force_kernel(plan, prc, xt, grad_acc, radial, feat, recv, send):
    recv[...] = jnp.zeros_like(recv)
    send[...] = jnp.zeros_like(send)

    def block(r, c, weight, slot):
        env, slope, scaled, vk = geometry(r, c, weight, prc, xt)
        deriv = second_deriv(r, c, grad_acc, radial, feat)
        add_force(pair_force(deriv, env, slope, scaled, vk), r, c, recv, send)

    for_blocks(plan, UNROLL_GHOST, block)


def ghost_last_kernel(
    plan, hot, prc, xt, quad_own, left, right, up, down, recv_two, send_two,
    quad, recv, send_up, send_down, send_mid,
    back_hi, back_lo, send,
):
    for p, piece in enumerate(arrived(left, right, up, down, CELL)):
        hi, lo = split(piece)
        back_hi[p * CELL : (p + 1) * CELL, :] = hi
        back_lo[p * CELL : (p + 1) * CELL, :] = lo
    recv[...] = recv_two[...]
    send[...] = send_two[...]

    def chunk(i, carry):
        rows = chunk_rows(i)
        pick = hot[rows, :]
        quad[rows, :] = quad_own[rows, :] + (mm(pick, back_hi[...], NN) + mm(pick, back_lo[...], NN))
        return carry

    lax.fori_loop(0, quad.shape[0] // CHUNK, chunk, 0)

    def block(r, c, weight, slot):
        env, slope, scaled, vk = geometry(r, c, weight, prc, xt)
        add_force(pair_force(first_deriv(r, c, xt, quad), env, slope, scaled, vk), r, c, recv, send)

    for_blocks(plan, UNROLL_GHOST, block)
    store_pieces([send[p : p + 1, :] for p in range(8)], send_up, send_down, send_mid)


def by_axis(rows, count):
    lines = [
        jnp.concatenate([rows[p : p + 1, (t + 1) * CELL : (t + 2) * CELL] for p in range(count)], axis=1)
        for t in range(3)
    ]
    return lines


def own_force_kernel(
    plan, prc, xt, quad, grad_acc, radial, feat, recv_ghost, acc, mats, readout, out, energy, recv, send
):
    recv[...] = recv_ghost[...]
    send[...] = jnp.zeros_like(send)

    def block(r, c, weight, slot):
        env, slope, scaled, vk = geometry(r, c, own_keep(r, c, weight), prc, xt)
        one = first_deriv(r, c, xt, quad)
        two = second_deriv(r, c, grad_acc, radial, feat)
        deriv = [x + y for x, y in zip(one, two)]
        add_force(pair_force(deriv, env, slope, scaled, vk), r, c, recv, send)

    for_blocks(plan, UNROLL_OWN, block)
    pick = jnp.where(iota((8, LANES), 0) + 1 == iota((8, LANES), 1) // CELL, 1.0, 0.0).astype(BF16)
    hi, lo = split(recv[...])
    total = mm(pick, hi, NT) + mm(pick, lo, NT)
    out[...] = total[0:3, :] - jnp.concatenate(by_axis(send, OWN), axis=0)
    mix0 = mat(mats, 4 * CH, CH)
    carry_w = readout[0:1, :]
    row8 = iota((8, CH), 0)
    first = split(jnp.where(row8 == 0, carry_w, 0.0))
    second = split(jnp.where(row8 == 0, readout[1:2, :], 0.0))
    for i in range(feat.shape[0] // CHUNK):
        rows = pl.ds(i * CHUNK, CHUNK)
        z = mm3_full(split(acc[rows, :]), mix0, NT)
        s1 = feat[rows, :][:, :CH]
        e = mm3(first, split(s1), NT) + mm3(second, split(z * jax.nn.sigmoid(z)), NT)
        energy[:, i * CHUNK : (i + 1) * CHUNK] = e[0:1, :]


def last_kernel(hot, left, right, up, down, partial, out):
    rows = jnp.concatenate(arrived(left, right, up, down, 1), axis=0)
    lines = by_axis(rows, 8)
    back = jnp.concatenate(lines + [jnp.zeros((5, lines[0].shape[1]), F32)], axis=0)
    hi, lo = split(back)
    ghost = mm(hi, hot[...], NT) + mm(lo, hot[...], NT)
    out[...] = partial[...] - ghost[0:3, :]


def ring(axis, step):
    count = lax.axis_size(axis)
    return [(i, (i + step) % count) for i in range(count)]


def exchange(up, down, mid, between=None):
    size = mid.shape[0] // 2
    part = lambda x, k: x[k * size : (k + 1) * size]
    up = lax.ppermute(up, "gy", ring("gy", 1))
    down = lax.ppermute(down, "gy", ring("gy", -1))
    if between is not None:
        up, down, between = lax.optimization_barrier((up, down, between))
    left = lax.ppermute(jnp.concatenate([part(up, 0), part(mid, 0), part(down, 0)]), "gx", ring("gx", -1))
    right = lax.ppermute(jnp.concatenate([part(up, 2), part(mid, 1), part(down, 2)]), "gx", ring("gx", 1))
    return (left, right, up, down), between


def in_hbm(*arrays):
    return [pltpu.with_memory_space_constraint(x, HBM) for x in arrays]


def call(kernel, outs, specs, scratch=()):
    spaces = [SMEM if s[1] == jnp.int32 else VMEM for s in outs]
    return pl.pallas_call(
        kernel,
        out_shape=[jax.ShapeDtypeStruct(*s) for s in outs],
        in_specs=[pl.BlockSpec(memory_space=s) for s in specs],
        out_specs=[pl.BlockSpec(memory_space=s) for s in spaces],
        scratch_shapes=list(scratch),
        compiler_params=PARAMS,
    )


def shards(
    positions, species, send_lists, cell_pairs, block_count,
    embed, radial_one, mix_one, radial_two, mix_two, readout,
):
    atoms = positions.shape[1]
    side = float((atoms * 10.0) ** (1.0 / 3.0))
    pairs = cell_pairs[0, 0].T
    lists = send_lists[0, 0]
    kinds = species[None, :]
    ghosts = lists.size
    f = lambda *shape: (shape, F32)
    b = lambda *shape: (shape, BF16)
    i = lambda *shape: (shape, jnp.int32)
    three = lambda size, width: [f(3 * size, width), f(3 * size, width), f(2 * size, width)]

    *sends, table, row = call(
        pack_kernel,
        three(1, LANES) + [f(8, atoms), f(1, ghosts)],
        [HBM] * 3,
        [
            VMEM((3, atoms), F32),
            VMEM((1, atoms), jnp.int32),
            VMEM((8, CELL), jnp.int32),
            pltpu.SemaphoreType.DMA((3,)),
        ],
    )(*in_hbm(positions, kinds, lists))
    ready = call(
        weight_kernel,
        [
            b(HIST, FEAT), b(HIST, FEAT), b(2, 5 * CH, CH), b(2, NB, CH), f(2, NB, CH), f(2, CH),
            f(OWN, 8, LANES), f(atoms, 8), b(atoms, ghosts),
            i(2 * SLOTS + 1), i(2 * SLOTS + 1), i(8, CELL),
        ],
        [SMEM] + [VMEM] * 2 + [HBM] * 8,
        [SMEM(pairs.shape, jnp.int32)]
        + [VMEM(x.shape, F32) for x in (embed, radial_one, mix_one, radial_two, mix_two, readout)]
        + [pltpu.SemaphoreType.DMA((8,))],
    )(block_count, table, row, *in_hbm(pairs, lists, embed, radial_one, mix_one, radial_two, mix_two, readout))
    moved, ready = exchange(*sends, ready)
    w_hi, w_lo, mats, begins, radial, rows, xt_own, prc, hot, plan_own, plan_ghost, lists_s = ready
    (hist_own,) = call(own_first_kernel, [f(atoms, HIST)], [SMEM] + [VMEM] * 2)(plan_own, xt_own, prc)
    hist, xt_ghost, *sends = call(
        functools.partial(ghost_first_kernel, side),
        [f(atoms, HIST), f(8, 8, LANES)] + three(CELL, HIST),
        [SMEM] * 2 + [VMEM] * 6,
    )(plan_ghost, lists_s, *moved, prc, hist_own)

    own = call(
        own_update_kernel, [f(atoms, FEAT), f(atoms, FEAT), f(atoms, 2 * CH), f(atoms, 3 * CH)], [VMEM] * 6
    )(hist, prc, w_hi, w_lo, begins, mats)
    moved, own = exchange(*sends, own)
    feat, lin, gates, lifted = own
    acc_own, tiles_own, tiles_ghost = call(
        own_second_kernel,
        [f(atoms, CH), b(SLOTS, HIST, 2 * LANES), b(SLOTS // 2, HIST, 2 * LANES)],
        [SMEM] * 2 + [VMEM] * 5,
    )(plan_own, plan_ghost, prc, xt_own, xt_ghost, feat, radial)
    acc, grad_acc, feat_ghost, *sends = call(
        ghost_second_kernel,
        [f(atoms, CH), f(atoms, CH), f(ghosts, FEAT)] + three(CELL, HIST),
        [SMEM] + [VMEM] * 13,
        [
            VMEM((ghosts, HIST), F32),
            VMEM((ghosts, FEAT), F32),
            VMEM((ghosts, 2 * CH), F32),
            VMEM((ghosts, 3 * CH), F32),
            VMEM((ghosts, FEAT), F32),
        ],
    )(plan_ghost, tiles_ghost, xt_ghost, *moved, w_hi, w_lo, begins, mats, acc_own, radial, rows)

    two = call(ghost_force_kernel, [f(atoms, LANES), f(8, LANES)], [SMEM] + [VMEM] * 5)(
        plan_ghost, prc, xt_ghost, grad_acc, radial, feat_ghost
    )
    moved, two = exchange(*sends, two)
    recv_two, send_two = two
    (quad_own,) = call(
        own_grad_kernel, [f(atoms, HIST)], [SMEM] + [VMEM] * 10, [VMEM((atoms, FEAT), F32)]
    )(plan_own, tiles_own, grad_acc, radial, lin, gates, lifted, w_hi, w_lo, mats, rows)
    quad, recv, *sends = call(
        ghost_last_kernel,
        [f(atoms, HIST), f(atoms, LANES)] + three(1, LANES),
        [SMEM] + [VMEM] * 10,
        [VMEM((ghosts, HIST), BF16), VMEM((ghosts, HIST), BF16), VMEM((8, LANES), F32)],
    )(plan_ghost, hot, prc, xt_ghost, quad_own, *moved, recv_two, send_two)

    moved, unused = exchange(*sends)
    partial, energy = call(
        own_force_kernel,
        [f(3, atoms), f(1, atoms)],
        [SMEM] + [VMEM] * 10,
        [VMEM((atoms, LANES), F32), VMEM((OWN, LANES), F32)],
    )(plan_own, prc, xt_own, quad, grad_acc, radial, feat, recv, acc, mats, rows)
    (forces,) = call(last_kernel, [f(3, atoms)], [VMEM] * 6)(hot, *moved, partial)
    return forces, energy[0]


def solution(mesh):
    both = P(("gx", "gy"))
    in_specs = (
        P(None, ("gx", "gy")),
        both,
        P("gx", "gy", None, None),
        P("gx", "gy", None, None),
        P("gx", "gy"),
    ) + (P(),) * 6
    out_specs = (P(None, ("gx", "gy")), both)
    return jax.shard_map(shards, mesh=mesh, in_specs=in_specs, out_specs=out_specs, check_vma=False)
```

```python
import functools

import jax
import jax.numpy as jnp
import numpy as np
from jax import lax
from jax.experimental import pallas as pl
from jax.experimental.pallas import tpu as pltpu
from jax.sharding import PartitionSpec as P

NB = 8
CELL = 32
CH = 128
LANES = 128
OWN = 16
CUT2 = 25.0
STEPS_X = np.array([-1, -1, -1, 0, 0, 1, 1, 1])
STEPS_Y = np.array([-1, 0, 1, -1, 1, -1, 0, 1])
F32 = jnp.float32
BF16 = jnp.bfloat16
VMEM = pltpu.VMEM
SMEM = pltpu.SMEM
HBM = pltpu.HBM
PARAMS = pltpu.CompilerParams(vmem_limit_bytes=20 * 1024 * 1024)
CHUNK = 128
HIST = 256
FEAT = 512
SLOTS = 32
UNROLL_OWN = (8, 4)
UNROLL_GHOST = (8, 2)
UP = (2, 4, 7)
DOWN = (0, 3, 5)
MID = (1, 6)

NN = (((1,), (0,)), ((), ()))
NT = (((1,), (1,)), ((), ()))
TN = (((0,), (0,)), ((), ()))


def split(x):
    hi = x.astype(BF16)
    return hi, (x - hi.astype(F32)).astype(BF16)


def mm(a, b, dims):
    return lax.dot_general(a, b, dims, preferred_element_type=F32)


def mm3(a, b, dims):
    (ah, al), (bh, bl) = a, b
    return mm(ah, bh, dims) + (mm(ah, bl, dims) + mm(al, bh, dims))


def mm3_deep(a, b, dims):
    (ah, al), (bh, bl) = a, b
    axis = dims[0][1][0]
    return mm(jnp.concatenate([ah, al], axis=1), jnp.concatenate([bh, bh], axis=axis), dims) + mm(ah, bl, dims)


def mm3_wide(a, b, dims):
    (ah, al), (bh, bl) = a, b
    width = 128
    out = mm(ah, jnp.concatenate([bh, bl], axis=1 - dims[0][1][0]), dims)
    return out[:, :width] + (out[:, width:] + mm(al, bh, dims))


def mm3_full(a, b, dims):
    (ah, al), (bh, bl) = a, b
    axis = dims[0][1][0]
    top = jnp.concatenate([bh, bh], axis=axis)
    low = jnp.concatenate([bl, jnp.zeros_like(bl)], axis=axis)
    out = mm(jnp.concatenate([ah, al], axis=1), jnp.concatenate([top, low], axis=1 - axis), dims)
    return out[:, :128] + out[:, 128:]


def iota(shape, dim):
    return lax.broadcasted_iota(jnp.int32, shape, dim)


def cell_rows(c):
    return pl.ds(pl.multiple_of(c * CELL, CELL), CELL)


def chunk_rows(i):
    return pl.ds(pl.multiple_of(i * CHUNK, CHUNK), CHUNK)


def geometry(r, c, keep, prc, xt):
    own = prc[cell_rows(r), :]
    far = xt[c]
    vec = [far[t + 1 : t + 2, :] - own[:, t : t + 1] for t in range(3)]
    sq = vec[0] * vec[0] + vec[1] * vec[1] + vec[2] * vec[2]
    group = iota((CELL, LANES), 1) // CELL
    edge = jnp.maximum(1.0 - sq * (1.0 / CUT2), 0.0)
    slope = edge * keep
    vk = jnp.where(group == 0, 1.0, jnp.where(group == 1, vec[0], jnp.where(group == 2, vec[1], vec[2])))
    scaled = sq * ((NB - 1) / CUT2)
    return edge * slope, slope, scaled, vk


def own_keep(r, c, weight):
    lane = iota((CELL, LANES), 1)
    row = iota((CELL, LANES), 0)
    return jnp.where(jnp.logical_and(lane % CELL == row, r == c), 0.0, weight)


def basis(scaled, n):
    off = scaled - float(n)
    return jnp.exp(-(off * off))


def all_bases(scaled):
    return [basis(scaled, n) for n in range(NB)]


def pair_force(deriv, bases, env, slope, scaled, vk):
    total = None
    moment = None
    for n in range(NB):
        term = deriv[n] * bases[n]
        total = term if n == 0 else total + term
        if n == 1:
            moment = term
        elif n > 1:
            moment = moment + float(n) * term
    spacing = CUT2 / (NB - 1)
    by_sq = (-2.0 / CUT2) * slope * total - (2.0 / spacing) * env * (scaled * total - moment)
    by_sq = by_sq * vk
    by_sq = by_sq + pltpu.roll(by_sq, 64, 1)
    by_sq = by_sq + pltpu.roll(by_sq, 32, 1)
    return env * total + 2.0 * vk * by_sq


def add_force(force, r, c, recv, send):
    recv[cell_rows(r), :] += force
    send[pl.ds(c, 1), :] += jnp.sum(force, axis=0, keepdims=True)


def species_tile(c, xt):
    row = iota((4 * NB, LANES), 0)
    lane = iota((4 * NB, LANES), 1)
    kind = xt[c][0:1, :].astype(jnp.int32)
    hit = jnp.logical_and(kind == row % NB, lane // CELL == row // NB)
    hot = jnp.where(hit, 1.0, 0.0).astype(BF16)
    zero = jnp.zeros_like(hot)
    return jnp.concatenate(
        [jnp.concatenate([hot if j == k else zero for k in range(4)], axis=1) for j in range(4)], axis=0
    )


def add_histogram(r, c, keep, prc, xt, hist, tiles, shapes, slot):
    env, slope, scaled, vk = geometry(r, c, keep, prc, xt)
    bases = all_bases(scaled)
    m = env * vk
    parts = [split(m * e) for e in bases]
    tiles[slot] = jnp.concatenate([jnp.concatenate([p[k] for p in parts], axis=0) for k in range(2)], axis=1)
    shapes[slot] = jnp.concatenate(bases + [env, slope, scaled, vk], axis=0)
    wide = [
        jnp.concatenate([p[k] for p in parts[4 * h : 4 * h + 4]], axis=1) for k in range(2) for h in range(2)
    ]
    out = mm(jnp.concatenate(wide, axis=0), species_tile(c, xt), NT)
    out = out[: 2 * CELL] + out[2 * CELL :]
    hist[cell_rows(r), :] += jnp.concatenate([out[:CELL], out[CELL:]], axis=1)


def first_deriv(r, c, xt, quad):
    q = quad[cell_rows(r), :]
    q = jnp.concatenate([q[:, :LANES], q[:, LANES:]], axis=0)
    out = mm(jnp.concatenate(split(q), axis=0), species_tile(c, xt), NN)
    out = out[: 2 * CELL] + out[2 * CELL :]
    return [out[(n // 4) * CELL : (n // 4 + 1) * CELL, (n % 4) * LANES : (n % 4 + 1) * LANES] for n in range(NB)]


def cell_features(table, c):
    hi, lo = split(table[cell_rows(c), :])
    zero = jnp.zeros((CELL, CH), BF16)

    def lay(x):
        rows = [jnp.concatenate([x[:, :CH], zero], axis=1)]
        rows += [jnp.concatenate([zero, x[:, (t + 1) * CH : (t + 2) * CH]], axis=1) for t in range(3)]
        return jnp.concatenate(rows, axis=0)

    return lay(hi), lay(lo)


def spread(g, radial):
    both = [
        jnp.concatenate([g * radial[0, n : n + 1, :], g * radial[1, n : n + 1, :]], axis=1) for n in range(NB)
    ]
    return split(jnp.concatenate(both, axis=0))


def add_forward(r, c, tile, table, radial, acc):
    fh, fl = cell_features(table, c)
    prod = mm(tile, jnp.concatenate([fh, fh], axis=0), NN) + mm(tile[:, :LANES], fl, NN)
    part = None
    for n in range(NB):
        rows = prod[n * CELL : (n + 1) * CELL]
        term = rows[:, :CH] * radial[0, n : n + 1, :] + rows[:, CH:] * radial[1, n : n + 1, :]
        part = term if n == 0 else part + term
    acc[cell_rows(r), :] += part


def add_feature_grad(r, c, tile, grad_acc, radial, grad_table):
    uh, ul = spread(grad_acc[cell_rows(r), :], radial)
    gf = mm(tile, uh, TN)
    gf = gf[:LANES] + (gf[LANES:] + mm(tile[:, :LANES], ul, TN))
    grad_table[cell_rows(c), :] += jnp.concatenate(
        [gf[0:CELL, :CH]] + [gf[(t + 1) * CELL : (t + 2) * CELL, CH:] for t in range(3)], axis=1
    )


def second_deriv(r, c, grad_acc, radial, table):
    out = mm3_wide(spread(grad_acc[cell_rows(r), :], radial), cell_features(table, c), NT)
    return [out[n * CELL : (n + 1) * CELL] for n in range(NB)]


def for_blocks(plan, unroll, body):
    count = plan[2 * SLOTS]
    large, small = unroll
    whole = count // large
    start = whole * large

    def step(first, size):
        def run(i, carry):
            for k in range(size):
                slot = first + i * size + k
                weight = jnp.where(slot < count, 1.0, 0.0).astype(F32)
                body(plan[2 * slot], plan[2 * slot + 1], weight, slot)
            return carry

        return run

    lax.fori_loop(0, whole, step(0, large), 0)
    lax.fori_loop(0, (count - start + small - 1) // small, step(start, small), 0)


def species_weights(embed, radial):
    zero = jnp.zeros((NB, CH), F32)
    rows = []
    for n in range(NB):
        for k in range(4):
            part = embed * radial[min(k, 1), n : n + 1, :]
            rows.append(jnp.concatenate([part if j == k else zero for j in range(4)], axis=1))
    return split(jnp.concatenate(rows, axis=0))


def tile_group(x, k):
    x = jnp.where(iota(x.shape, 1) // CELL == k, x, 0.0)
    x = x + pltpu.roll(x, 64, 1)
    return x + pltpu.roll(x, 32, 1)


def store_pieces(pieces, up, down, mid):
    for out, order in ((up, UP), (down, DOWN), (mid, MID)):
        size = pieces[0].shape[0]
        for k, p in enumerate(order):
            out[k * size : (k + 1) * size, :] = pieces[p]


def arrived(left, right, up, down, size):
    at = lambda x, k: x[k * size : (k + 1) * size, :]
    return [at(right, 0), at(right, 1), at(right, 2), at(up, 1), at(down, 1), at(left, 0), at(left, 1), at(left, 2)]


def fetch(sems, *pairs):
    copies = [pltpu.make_async_copy(src, dst, sems.at[k]) for k, (src, dst) in enumerate(pairs)]
    for copy in copies:
        copy.start()
    return copies


def arrive(copies):
    for copy in copies:
        copy.wait()


def pack_kernel(pos_in, species_in, lists_in, up, down, mid, table_out, row_out, pos, species, lists, sems):
    arrive(fetch(sems, (pos_in, pos), (species_in, species), (lists_in, lists)))
    kinds = species[...].astype(F32)
    table = jnp.concatenate([kinds, pos[...], jnp.zeros((4, kinds.shape[1]), F32)], axis=0)
    table_out[...] = table
    hi = table.astype(BF16)
    rest = table - hi.astype(F32)
    mid_part = rest.astype(BF16)
    low = (rest - mid_part.astype(F32)).astype(BF16)
    row = jnp.concatenate([lists[p : p + 1, :] for p in range(8)], axis=1)
    row_out[...] = row.astype(F32)
    hot = jnp.where(iota((table.shape[1], row.shape[1]), 0) == row, 1.0, 0.0).astype(BF16)
    out = mm(hi, hot, NN) + mm(mid_part, hot, NN) + mm(low, hot, NN)
    pieces = [
        jnp.concatenate([out[k : k + 1, p * CELL : (p + 1) * CELL] for k in range(4)], axis=1) for p in range(8)
    ]
    store_pieces(pieces, up, down, mid)


def weight_kernel(
    count, table, row, pairs_in, embed_in, radial_one_in, mix_one_in, radial_two_in, mix_two_in, readout_in,
    w_hi, w_lo, mats, begins, radial, rows, xt, prc, hot, hot_t, plan_own, plan_ghost,
    pairs, embed, radial_one, mix_one, radial_two, mix_two, readout, sems,
):
    sources = (pairs_in, embed_in, radial_one_in, mix_one_in, radial_two_in, mix_two_in, readout_in)
    targets = (pairs, embed, radial_one, mix_one, radial_two, mix_two, readout)
    copies = fetch(sems, *zip(sources, targets))
    lists = row[...].astype(jnp.int32)
    hot[...] = jnp.where(iota(hot.shape, 0) == lists, 1.0, 0.0).astype(BF16)
    column = jnp.broadcast_to(row[...], (8, row.shape[1])).T[:, 0:1].astype(jnp.int32)
    hot_t[...] = jnp.where(iota(hot_t.shape, 1) == column, 1.0, 0.0).astype(BF16)
    t = table[...]
    for c in range(OWN):
        xt[c] = tile_group(t[:, (c // 4) * LANES : (c // 4 + 1) * LANES], c % 4)
    prc[...] = jnp.concatenate([t[1:4], t[0:1], t[4:8]], axis=0).T
    arrive(copies[:1])
    def clear(i, carry):
        plan_own[i] = 0
        plan_ghost[i] = 0
        return carry

    lax.fori_loop(0, 2 * SLOTS, clear, 0)

    def sort(i, carry):
        n_own, n_ghost = carry
        r, c = pairs[0, i], pairs[1, i]
        mine = c < OWN

        @pl.when(mine)
        def _():
            plan_own[2 * n_own] = r
            plan_own[2 * n_own + 1] = c

        @pl.when(jnp.logical_not(mine))
        def _():
            plan_ghost[2 * n_ghost] = r
            plan_ghost[2 * n_ghost + 1] = c - OWN

        step = mine.astype(jnp.int32)
        return n_own + step, n_ghost + 1 - step

    n_own, n_ghost = lax.fori_loop(0, count[0, 0], sort, (jnp.int32(0), jnp.int32(0)))
    plan_own[2 * SLOTS] = n_own
    plan_ghost[2 * SLOTS] = n_ghost
    arrive(copies[1:])
    w_hi[...], w_lo[...] = species_weights(embed[...], 0.5 * radial_one[...])
    for k, m in enumerate((mix_one[0], mix_one[4], mix_one[1], mix_one[3], mix_two[0])):
        mats[0, k * CH : (k + 1) * CH, :], mats[1, k * CH : (k + 1) * CH, :] = split(m)
    begins[0], begins[1] = split(mm3(split(embed[...]), split(mix_one[2]), NT))
    radial[...] = 0.5 * radial_two[...]
    both = readout[...]
    rows[0:1, :] = both[0:1, :] + mm3(split(both), split(mix_two[1]), NN)[1:2, :]
    rows[1:2, :] = both[1:2, :]


def own_first_kernel(plan_own, xt, prc, hist, tiles, shapes):
    hist[...] = jnp.zeros_like(hist)

    def block(r, c, weight, slot):
        add_histogram(r, c, own_keep(r, c, weight), prc, xt, hist, tiles, shapes, slot)

    for_blocks(plan_own, UNROLL_OWN, block)


def ghost_first_kernel(
    side, plan, hot_t, left, right, up, down, prc, hist_own,
    hist, xt, tiles, shapes, send_up, send_down, send_mid,
):
    rows = jnp.concatenate(arrived(left, right, up, down, 1), axis=0)
    for k in range(4):
        part = tile_group(rows, k)
        for p in range(8):
            shift = 0.0 if k in (0, 3) else float((STEPS_X, STEPS_Y)[k - 1][p] * side)
            xt[p, k : k + 1, :] = part[p : p + 1, :] + shift
    hist[...] = hist_own[...]

    def block(r, c, weight, slot):
        add_histogram(r, c, weight, prc, xt, hist, tiles, shapes, slot)

    for_blocks(plan, UNROLL_GHOST, block)

    hi, lo = split(hist[...])
    sent = mm(hot_t[...], hi, NN) + mm(hot_t[...], lo, NN)
    store_pieces([sent[p * CELL : (p + 1) * CELL] for p in range(8)], send_up, send_down, send_mid)


def first_update(joined, kind, weights, begin, mix04, mix1, mix3):
    size = joined.shape[0]
    a = mm3(split(joined), weights, NN)
    a0 = a[:, :CH]
    a1 = [a[:, (t + 1) * CH : (t + 2) * CH] for t in range(3)]
    power = a1[0] * a1[0] + a1[1] * a1[1] + a1[2] * a1[2]
    both = mm3_deep(split(a0), mix04, NT)
    z0 = both[:, :CH] + mm3_full(split(power), mix1, NT)
    gate = jax.nn.sigmoid(both[:, CH:])
    hot = jnp.where(kind == iota((size, NB), 1), 1.0, 0.0).astype(BF16)
    own = mm(hot, begin[0], NN) + mm(hot, begin[1], NN)
    lift = mm3_full(split(jnp.concatenate(a1, axis=0)), mix3, NT)
    lift = jnp.concatenate([lift[t * size : (t + 1) * size] for t in range(3)], axis=1)
    feat = jnp.concatenate(
        [z0 * jax.nn.sigmoid(z0) + own, lift * jnp.concatenate([gate] * 3, axis=1)], axis=1
    )
    return feat, a, jnp.concatenate([z0, gate], axis=1), lift


def first_pullback(gs, gv, a, gates, lift, weights, mix04, mix1, mix3):
    size = gs.shape[0]
    z0, gate = gates[:, :CH], gates[:, CH:]
    sg = jax.nn.sigmoid(z0)
    dz0 = gs * (sg * (1.0 + z0 * (1.0 - sg)))
    y = [lift[:, t * CH : (t + 1) * CH] for t in range(3)]
    dgate = gv[0] * y[0] + gv[1] * y[1] + gv[2] * y[2]
    dz4 = dgate * gate * (1.0 - gate)
    da0 = mm3_wide(split(jnp.concatenate([dz0, dz4], axis=1)), mix04, NN)
    dpower = 2.0 * mm3_full(split(dz0), mix1, NN)
    dy = mm3_full(split(jnp.concatenate([v * gate for v in gv], axis=0)), mix3, NN)
    parts = [da0] + [
        dy[t * size : (t + 1) * size] + a[:, (t + 1) * CH : (t + 2) * CH] * dpower for t in range(3)
    ]
    return mm3(split(jnp.concatenate(parts, axis=1)), weights, NT)


def mat(mats, first, rows):
    return mats[0, first : first + rows, :], mats[1, first : first + rows, :]


def mixes(mats):
    return mat(mats, 0, 2 * CH), mat(mats, 2 * CH, CH), mat(mats, 3 * CH, CH)


def features(g):
    return g[:, :CH], [g[:, (t + 1) * CH : (t + 2) * CH] for t in range(3)]


def own_update_kernel(joined, prc, w_hi, w_lo, begins, mats, feat, acc, gates, lifted):
    begin = begins[0], begins[1]
    mix_all = mixes(mats)

    def chunk(i, carry):
        rows = chunk_rows(i)
        kind = prc[rows, :][:, 3:4].astype(jnp.int32)
        out = first_update(joined[rows, :], kind, (w_hi[...], w_lo[...]), begin, *mix_all)
        feat[rows, :], acc[rows, :], gates[rows, :], lifted[rows, :] = out
        return carry

    lax.fori_loop(0, feat.shape[0] // CHUNK, chunk, 0)


def own_second_kernel(plan, tiles, feat, radial, acc):
    acc[...] = jnp.zeros_like(acc)

    def block(r, c, weight, slot):
        add_forward(r, c, tiles[slot], feat, radial, acc)

    for_blocks(plan, UNROLL_OWN, block)


def ghost_second_kernel(
    plan, tiles, xt, left, right, up, down, w_hi, w_lo, begins, mats, acc_own, radial, readout,
    zed, grad_acc, feat, send_up, send_down, send_mid,
    joined, lin, gates, lifted, grad_table, acc,
):
    ghosts = feat.shape[0]
    for p, piece in enumerate(arrived(left, right, up, down, CELL)):
        joined[p * CELL : (p + 1) * CELL, :] = piece
    begin = begins[0], begins[1]
    mix_all = mixes(mats)
    acc[...] = acc_own[...]
    grad_table[...] = jnp.zeros_like(grad_table)
    kinds = jnp.concatenate([xt[p][0:8, 0:CELL] for p in range(8)], axis=1).T[:, 0:1].astype(jnp.int32)
    for i in range(ghosts // CHUNK):
        rows = pl.ds(i * CHUNK, CHUNK)
        kind = kinds[i * CHUNK : (i + 1) * CHUNK]
        out = first_update(joined[rows, :], kind, (w_hi[...], w_lo[...]), begin, *mix_all)
        feat[rows, :], lin[rows, :], gates[rows, :], lifted[rows, :] = out

    def forward(r, c, weight, slot):
        add_forward(r, c, tiles[slot], feat, radial, acc)

    for_blocks(plan, UNROLL_GHOST, forward)

    mix0 = mat(mats, 4 * CH, CH)

    def chunk(i, carry):
        rows = chunk_rows(i)
        z = mm3_full(split(acc[rows, :]), mix0, NT)
        zed[rows, :] = z
        sg = jax.nn.sigmoid(z)
        gz = readout[1:2, :] * (sg * (1.0 + z * (1.0 - sg)))
        grad_acc[rows, :] = mm3_full(split(gz), mix0, NN)
        return carry

    lax.fori_loop(0, acc.shape[0] // CHUNK, chunk, 0)

    def backward(r, c, weight, slot):
        add_feature_grad(r, c, tiles[slot], grad_acc, radial, grad_table)

    for_blocks(plan, UNROLL_GHOST, backward)

    pieces = []
    for i in range(ghosts // CHUNK):
        rows = pl.ds(i * CHUNK, CHUNK)
        gs, gv = features(grad_table[rows, :])
        q = first_pullback(gs, gv, lin[rows, :], gates[rows, :], lifted[rows, :], (w_hi[...], w_lo[...]), *mix_all)
        pieces += [q[k * CELL : (k + 1) * CELL] for k in range(CHUNK // CELL)]
    store_pieces(pieces, send_up, send_down, send_mid)


def own_grad_kernel(
    plan, tiles, grad_acc, radial, lin, gates, lifted, w_hi, w_lo, mats, readout,
    quad,
    grad_table,
):
    atoms = quad.shape[0]
    grad_table[...] = jnp.zeros_like(grad_table)

    def block(r, c, weight, slot):
        add_feature_grad(r, c, tiles[slot], grad_acc, radial, grad_table)

    for_blocks(plan, UNROLL_OWN, block)
    mix_all = mixes(mats)
    carry_w = readout[0:1, :]

    def chunk(i, carry):
        rows = chunk_rows(i)
        gs, gv = features(grad_table[rows, :])
        quad[rows, :] = first_pullback(
            gs + carry_w, gv, lin[rows, :], gates[rows, :], lifted[rows, :], (w_hi[...], w_lo[...]), *mix_all
        )
        return carry

    lax.fori_loop(0, atoms // CHUNK, chunk, 0)


def shape_of(shapes, slot):
    whole = shapes[slot]
    parts = [whole[k * CELL : (k + 1) * CELL] for k in range(12)]
    return [parts[:NB]] + parts[NB:]


def ghost_force_kernel(plan, shapes, grad_acc, radial, feat, recv, send):
    recv[...] = jnp.zeros_like(recv)
    send[...] = jnp.zeros_like(send)

    def block(r, c, weight, slot):
        deriv = second_deriv(r, c, grad_acc, radial, feat)
        add_force(pair_force(deriv, *shape_of(shapes, slot)), r, c, recv, send)

    for_blocks(plan, UNROLL_GHOST, block)


def ghost_last_kernel(
    plan, hot, shapes, xt, quad_own, left, right, up, down, recv_two, send_two,
    quad, recv, send_up, send_down, send_mid,
    back_hi, back_lo, send,
):
    for p, piece in enumerate(arrived(left, right, up, down, CELL)):
        hi, lo = split(piece)
        back_hi[p * CELL : (p + 1) * CELL, :] = hi
        back_lo[p * CELL : (p + 1) * CELL, :] = lo
    recv[...] = recv_two[...]
    send[...] = send_two[...]

    def chunk(i, carry):
        rows = chunk_rows(i)
        pick = hot[rows, :]
        quad[rows, :] = quad_own[rows, :] + (mm(pick, back_hi[...], NN) + mm(pick, back_lo[...], NN))
        return carry

    lax.fori_loop(0, quad.shape[0] // CHUNK, chunk, 0)

    def block(r, c, weight, slot):
        add_force(pair_force(first_deriv(r, c, xt, quad), *shape_of(shapes, slot)), r, c, recv, send)

    for_blocks(plan, UNROLL_GHOST, block)
    store_pieces([send[p : p + 1, :] for p in range(8)], send_up, send_down, send_mid)


def by_axis(rows, count):
    lines = [
        jnp.concatenate([rows[p : p + 1, (t + 1) * CELL : (t + 2) * CELL] for p in range(count)], axis=1)
        for t in range(3)
    ]
    return lines


def own_force_kernel(
    plan, shapes, xt, quad, grad_acc, radial, feat, recv_ghost, zed, readout, out, energy, recv, send
):
    recv[...] = recv_ghost[...]
    send[...] = jnp.zeros_like(send)

    def block(r, c, weight, slot):
        one = first_deriv(r, c, xt, quad)
        two = second_deriv(r, c, grad_acc, radial, feat)
        deriv = [x + y for x, y in zip(one, two)]
        add_force(pair_force(deriv, *shape_of(shapes, slot)), r, c, recv, send)

    for_blocks(plan, UNROLL_OWN, block)
    pick = jnp.where(iota((8, LANES), 0) + 1 == iota((8, LANES), 1) // CELL, 1.0, 0.0).astype(BF16)
    hi, lo = split(recv[...])
    total = mm(pick, hi, NT) + mm(pick, lo, NT)
    out[...] = total[0:3, :] - jnp.concatenate(by_axis(send, OWN), axis=0)
    z = zed[...]
    site = readout[0:1, :] * feat[:, :CH] + readout[1:2, :] * (z * jax.nn.sigmoid(z))
    hi, lo = split(site)
    ones = jnp.ones((8, CH), BF16)
    energy[...] = (mm(ones, hi, NT) + mm(ones, lo, NT))[0:1, :]


def last_kernel(hot, left, right, up, down, partial, out):
    rows = jnp.concatenate(arrived(left, right, up, down, 1), axis=0)
    lines = by_axis(rows, 8)
    back = jnp.concatenate(lines + [jnp.zeros((5, lines[0].shape[1]), F32)], axis=0)
    hi, lo = split(back)
    ghost = mm(hi, hot[...], NT) + mm(lo, hot[...], NT)
    out[...] = partial[...] - ghost[0:3, :]


def ring(axis, step):
    count = lax.axis_size(axis)
    return [(i, (i + step) % count) for i in range(count)]


def swap_both(axis, to_lower, to_upper):
    count = lax.axis_size(axis)
    even = lax.axis_index(axis) % 2 == 0
    inner = [(i, i ^ 1) for i in range(count)]
    outer = [(i, (i - 1) % count if i % 2 == 0 else (i + 1) % count) for i in range(count)]
    one = lax.ppermute(jnp.where(even, to_upper, to_lower), axis, inner)
    two = lax.ppermute(jnp.where(even, to_lower, to_upper), axis, outer)
    return jnp.where(even, one, two), jnp.where(even, two, one)


def exchange(up, down, mid, between=None):
    size = mid.shape[0] // 2
    part = lambda x, k: x[k * size : (k + 1) * size]
    up = lax.ppermute(up, "gy", ring("gy", 1))
    down = lax.ppermute(down, "gy", ring("gy", -1))
    if between is not None:
        up, down, between = lax.optimization_barrier((up, down, between))
    to_left = jnp.concatenate([part(up, 0), part(mid, 0), part(down, 0)])
    to_right = jnp.concatenate([part(up, 2), part(mid, 1), part(down, 2)])
    left, right = swap_both("gx", to_left, to_right)
    return (left, right, up, down), between


def in_hbm(*arrays):
    return [pltpu.with_memory_space_constraint(x, HBM) for x in arrays]


def call(kernel, outs, specs, scratch=()):
    spaces = [SMEM if s[1] == jnp.int32 else VMEM for s in outs]
    return pl.pallas_call(
        kernel,
        out_shape=[jax.ShapeDtypeStruct(*s) for s in outs],
        in_specs=[pl.BlockSpec(memory_space=s) for s in specs],
        out_specs=[pl.BlockSpec(memory_space=s) for s in spaces],
        scratch_shapes=list(scratch),
        compiler_params=PARAMS,
    )


def shards(
    positions, species, send_lists, cell_pairs, block_count,
    embed, radial_one, mix_one, radial_two, mix_two, readout,
):
    atoms = positions.shape[1]
    side = float((atoms * 10.0) ** (1.0 / 3.0))
    pairs = cell_pairs[0, 0].T
    lists = send_lists[0, 0]
    kinds = species[None, :]
    ghosts = lists.size
    f = lambda *shape: (shape, F32)
    b = lambda *shape: (shape, BF16)
    i = lambda *shape: (shape, jnp.int32)
    three = lambda size, width: [f(3 * size, width), f(3 * size, width), f(2 * size, width)]

    *sends, table, row = call(
        pack_kernel,
        three(1, LANES) + [f(8, atoms), f(1, ghosts)],
        [HBM] * 3,
        [
            VMEM((3, atoms), F32),
            VMEM((1, atoms), jnp.int32),
            VMEM((8, CELL), jnp.int32),
            pltpu.SemaphoreType.DMA((3,)),
        ],
    )(*in_hbm(positions, kinds, lists))
    ready = call(
        weight_kernel,
        [
            b(HIST, FEAT), b(HIST, FEAT), b(2, 5 * CH, CH), b(2, NB, CH), f(2, NB, CH), f(2, CH),
            f(OWN, 8, LANES), f(atoms, 8), b(atoms, ghosts), b(ghosts, atoms),
            i(2 * SLOTS + 1), i(2 * SLOTS + 1),
        ],
        [SMEM] + [VMEM] * 2 + [HBM] * 7,
        [SMEM(pairs.shape, jnp.int32)]
        + [VMEM(x.shape, F32) for x in (embed, radial_one, mix_one, radial_two, mix_two, readout)]
        + [pltpu.SemaphoreType.DMA((7,))],
    )(block_count, table, row, *in_hbm(pairs, embed, radial_one, mix_one, radial_two, mix_two, readout))
    moved, unused = exchange(*sends)
    w_hi, w_lo, mats, begins, radial, rows, xt_own, prc, hot, hot_t, plan_own, plan_ghost = ready
    store = lambda slots: [b(slots, HIST, 2 * LANES), f(slots, 12 * CELL, LANES)]
    hist_own, tiles_own, shapes_own = call(
        own_first_kernel, [f(atoms, HIST)] + store(SLOTS), [SMEM] + [VMEM] * 2
    )(plan_own, xt_own, prc)
    hist, xt_ghost, tiles_ghost, shapes_ghost, *sends = call(
        functools.partial(ghost_first_kernel, side),
        [f(atoms, HIST), f(8, 8, LANES)] + store(SLOTS // 2) + three(CELL, HIST),
        [SMEM] + [VMEM] * 7,
    )(plan_ghost, hot_t, *moved, prc, hist_own)

    own = call(
        own_update_kernel, [f(atoms, FEAT), f(atoms, FEAT), f(atoms, 2 * CH), f(atoms, 3 * CH)], [VMEM] * 6
    )(hist, prc, w_hi, w_lo, begins, mats)
    moved, own = exchange(*sends, own)
    feat, lin, gates, lifted = own
    (acc_own,) = call(own_second_kernel, [f(atoms, CH)], [SMEM] + [VMEM] * 3)(plan_own, tiles_own, feat, radial)
    zed, grad_acc, feat_ghost, *sends = call(
        ghost_second_kernel,
        [f(atoms, CH), f(atoms, CH), f(ghosts, FEAT)] + three(CELL, HIST),
        [SMEM] + [VMEM] * 13,
        [
            VMEM((ghosts, HIST), F32),
            VMEM((ghosts, FEAT), F32),
            VMEM((ghosts, 2 * CH), F32),
            VMEM((ghosts, 3 * CH), F32),
            VMEM((ghosts, FEAT), F32),
            VMEM((atoms, CH), F32),
        ],
    )(plan_ghost, tiles_ghost, xt_ghost, *moved, w_hi, w_lo, begins, mats, acc_own, radial, rows)

    two = call(ghost_force_kernel, [f(atoms, LANES), f(8, LANES)], [SMEM] + [VMEM] * 4)(
        plan_ghost, shapes_ghost, grad_acc, radial, feat_ghost
    )
    moved, two = exchange(*sends, two)
    recv_two, send_two = two
    (quad_own,) = call(
        own_grad_kernel, [f(atoms, HIST)], [SMEM] + [VMEM] * 10, [VMEM((atoms, FEAT), F32)]
    )(plan_own, tiles_own, grad_acc, radial, lin, gates, lifted, w_hi, w_lo, mats, rows)
    quad, recv, *sends = call(
        ghost_last_kernel,
        [f(atoms, HIST), f(atoms, LANES)] + three(1, LANES),
        [SMEM] + [VMEM] * 10,
        [VMEM((ghosts, HIST), BF16), VMEM((ghosts, HIST), BF16), VMEM((8, LANES), F32)],
    )(plan_ghost, hot, shapes_ghost, xt_ghost, quad_own, *moved, recv_two, send_two)

    moved, unused = exchange(*sends)
    partial, energy = call(
        own_force_kernel,
        [f(3, atoms), f(1, atoms)],
        [SMEM] + [VMEM] * 9,
        [VMEM((atoms, LANES), F32), VMEM((OWN, LANES), F32)],
    )(plan_own, shapes_own, xt_own, quad, grad_acc, radial, feat, recv, zed, rows)
    (forces,) = call(last_kernel, [f(3, atoms)], [VMEM] * 6)(hot, *moved, partial)
    return forces, energy[0]


def solution(mesh):
    both = P(("gx", "gy"))
    in_specs = (
        P(None, ("gx", "gy")),
        both,
        P("gx", "gy", None, None),
        P("gx", "gy", None, None),
        P("gx", "gy"),
    ) + (P(),) * 6
    out_specs = (P(None, ("gx", "gy")), both)
    return jax.shard_map(shards, mesh=mesh, in_specs=in_specs, out_specs=out_specs, check_vma=False)
```

```python
import functools

import jax
import jax.numpy as jnp
import numpy as np
from jax import lax
from jax.experimental import pallas as pl
from jax.experimental.pallas import tpu as pltpu
from jax.sharding import PartitionSpec as P

NB = 8
CELL = 32
CH = 128
LANES = 128
OWN = 16
CUT2 = 25.0
STEPS_X = np.array([-1, -1, -1, 0, 0, 1, 1, 1])
STEPS_Y = np.array([-1, 0, 1, -1, 1, -1, 0, 1])
F32 = jnp.float32
BF16 = jnp.bfloat16
VMEM = pltpu.VMEM
SMEM = pltpu.SMEM
HBM = pltpu.HBM
PARAMS = pltpu.CompilerParams(vmem_limit_bytes=20 * 1024 * 1024)
CHUNK = 128
HIST = 256
FEAT = 512
SLOTS = 32
UNROLL_OWN = (8, 4)
EARLY = 8
UNROLL_GHOST = (8, 2)
UP = (2, 4, 7)
DOWN = (0, 3, 5)
MID = (1, 6)

NN = (((1,), (0,)), ((), ()))
NT = (((1,), (1,)), ((), ()))
TN = (((0,), (0,)), ((), ()))


def split(x):
    hi = x.astype(BF16)
    return hi, (x - hi.astype(F32)).astype(BF16)


def mm(a, b, dims):
    return lax.dot_general(a, b, dims, preferred_element_type=F32)


def mm3(a, b, dims):
    (ah, al), (bh, bl) = a, b
    return mm(ah, bh, dims) + (mm(ah, bl, dims) + mm(al, bh, dims))


def mm3_deep(a, b, dims):
    (ah, al), (bh, bl) = a, b
    axis = dims[0][1][0]
    return mm(jnp.concatenate([ah, al], axis=1), jnp.concatenate([bh, bh], axis=axis), dims) + mm(ah, bl, dims)


def mm3_wide(a, b, dims):
    (ah, al), (bh, bl) = a, b
    width = 128
    out = mm(ah, jnp.concatenate([bh, bl], axis=1 - dims[0][1][0]), dims)
    return out[:, :width] + (out[:, width:] + mm(al, bh, dims))


def mm3_full(a, b, dims):
    (ah, al), (bh, bl) = a, b
    axis = dims[0][1][0]
    top = jnp.concatenate([bh, bh], axis=axis)
    low = jnp.concatenate([bl, jnp.zeros_like(bl)], axis=axis)
    out = mm(jnp.concatenate([ah, al], axis=1), jnp.concatenate([top, low], axis=1 - axis), dims)
    return out[:, :128] + out[:, 128:]


def iota(shape, dim):
    return lax.broadcasted_iota(jnp.int32, shape, dim)


def cell_rows(c):
    return pl.ds(pl.multiple_of(c * CELL, CELL), CELL)


def chunk_rows(i):
    return pl.ds(pl.multiple_of(i * CHUNK, CHUNK), CHUNK)


def geometry(r, c, keep, prc, xt):
    own = prc[cell_rows(r), :]
    far = xt[c]
    vec = [far[t + 1 : t + 2, :] - own[:, t : t + 1] for t in range(3)]
    sq = vec[0] * vec[0] + vec[1] * vec[1] + vec[2] * vec[2]
    group = iota((CELL, LANES), 1) // CELL
    edge = jnp.maximum(1.0 - sq * (1.0 / CUT2), 0.0)
    slope = edge * keep
    vk = jnp.where(group == 0, 1.0, jnp.where(group == 1, vec[0], jnp.where(group == 2, vec[1], vec[2])))
    scaled = sq * ((NB - 1) / CUT2)
    return edge * slope, slope, scaled, vk


def own_keep(r, c, weight):
    lane = iota((CELL, LANES), 1)
    row = iota((CELL, LANES), 0)
    return jnp.where(jnp.logical_and(lane % CELL == row, r == c), 0.0, weight)


def basis(scaled, n):
    off = scaled - float(n)
    return jnp.exp(-(off * off))


def all_bases(scaled):
    return [basis(scaled, n) for n in range(NB)]


def pair_force(deriv, bases, env, slope, scaled, vk):
    total = None
    moment = None
    for n in range(NB):
        term = deriv[n] * bases[n]
        total = term if n == 0 else total + term
        if n == 1:
            moment = term
        elif n > 1:
            moment = moment + float(n) * term
    spacing = CUT2 / (NB - 1)
    by_sq = (-2.0 / CUT2) * slope * total - (2.0 / spacing) * env * (scaled * total - moment)
    by_sq = by_sq * vk
    by_sq = by_sq + pltpu.roll(by_sq, 64, 1)
    by_sq = by_sq + pltpu.roll(by_sq, 32, 1)
    return env * total + 2.0 * vk * by_sq


def add_force(force, r, c, recv, send):
    recv[cell_rows(r), :] += force
    send[pl.ds(c, 1), :] += jnp.sum(force, axis=0, keepdims=True)


def species_tile(c, xt):
    row = iota((4 * NB, LANES), 0)
    lane = iota((4 * NB, LANES), 1)
    kind = xt[c][0:1, :].astype(jnp.int32)
    hit = jnp.logical_and(kind == row % NB, lane // CELL == row // NB)
    hot = jnp.where(hit, 1.0, 0.0).astype(BF16)
    zero = jnp.zeros_like(hot)
    return jnp.concatenate(
        [jnp.concatenate([hot if j == k else zero for k in range(4)], axis=1) for j in range(4)], axis=0
    )


def add_histogram(r, c, keep, prc, xt, hist, tiles, shapes, slot):
    env, slope, scaled, vk = geometry(r, c, keep, prc, xt)
    bases = all_bases(scaled)
    m = env * vk
    parts = [split(m * e) for e in bases]
    tiles[slot] = jnp.concatenate([jnp.concatenate([p[k] for p in parts], axis=0) for k in range(2)], axis=1)
    shapes[slot] = jnp.concatenate(bases + [env, slope, scaled, vk], axis=0)
    wide = [
        jnp.concatenate([p[k] for p in parts[4 * h : 4 * h + 4]], axis=1) for k in range(2) for h in range(2)
    ]
    out = mm(jnp.concatenate(wide, axis=0), species_tile(c, xt), NT)
    out = out[: 2 * CELL] + out[2 * CELL :]
    hist[cell_rows(r), :] += jnp.concatenate([out[:CELL], out[CELL:]], axis=1)


def first_deriv(r, c, xt, quad):
    q = quad[cell_rows(r), :]
    q = jnp.concatenate([q[:, :LANES], q[:, LANES:]], axis=0)
    out = mm(jnp.concatenate(split(q), axis=0), species_tile(c, xt), NN)
    out = out[: 2 * CELL] + out[2 * CELL :]
    return [out[(n // 4) * CELL : (n // 4 + 1) * CELL, (n % 4) * LANES : (n % 4 + 1) * LANES] for n in range(NB)]


def cell_features(table, c):
    hi, lo = split(table[cell_rows(c), :])
    zero = jnp.zeros((CELL, CH), BF16)

    def lay(x):
        rows = [jnp.concatenate([x[:, :CH], zero], axis=1)]
        rows += [jnp.concatenate([zero, x[:, (t + 1) * CH : (t + 2) * CH]], axis=1) for t in range(3)]
        return jnp.concatenate(rows, axis=0)

    return lay(hi), lay(lo)


def spread(g, radial):
    both = [
        jnp.concatenate([g * radial[0, n : n + 1, :], g * radial[1, n : n + 1, :]], axis=1) for n in range(NB)
    ]
    return split(jnp.concatenate(both, axis=0))


def add_forward(r, c, tile, table, radial, acc):
    fh, fl = cell_features(table, c)
    prod = mm(tile, jnp.concatenate([fh, fh], axis=0), NN) + mm(tile[:, :LANES], fl, NN)
    part = None
    for n in range(NB):
        rows = prod[n * CELL : (n + 1) * CELL]
        term = rows[:, :CH] * radial[0, n : n + 1, :] + rows[:, CH:] * radial[1, n : n + 1, :]
        part = term if n == 0 else part + term
    acc[cell_rows(r), :] += part


def add_feature_grad(r, c, tile, grad_acc, radial, grad_table):
    uh, ul = spread(grad_acc[cell_rows(r), :], radial)
    gf = mm(tile, uh, TN)
    gf = gf[:LANES] + (gf[LANES:] + mm(tile[:, :LANES], ul, TN))
    grad_table[cell_rows(c), :] += jnp.concatenate(
        [gf[0:CELL, :CH]] + [gf[(t + 1) * CELL : (t + 2) * CELL, CH:] for t in range(3)], axis=1
    )


def second_deriv(r, c, grad_acc, radial, table):
    out = mm3_wide(spread(grad_acc[cell_rows(r), :], radial), cell_features(table, c), NT)
    return [out[n * CELL : (n + 1) * CELL] for n in range(NB)]


def for_blocks(plan, unroll, body, skip=0):
    count = plan[2 * SLOTS]
    large, small = unroll
    whole = (count - skip) // large
    start = skip + whole * large

    def step(first, size):
        def run(i, carry):
            for k in range(size):
                slot = first + i * size + k
                weight = jnp.where(slot < count, 1.0, 0.0).astype(F32)
                body(plan[2 * slot], plan[2 * slot + 1], weight, slot)
            return carry

        return run

    lax.fori_loop(0, whole, step(skip, large), 0)
    lax.fori_loop(0, (count - start + small - 1) // small, step(start, small), 0)


def species_weights(embed, radial):
    zero = jnp.zeros((NB, CH), F32)
    rows = []
    for n in range(NB):
        for k in range(4):
            part = embed * radial[min(k, 1), n : n + 1, :]
            rows.append(jnp.concatenate([part if j == k else zero for j in range(4)], axis=1))
    return split(jnp.concatenate(rows, axis=0))


def tile_group(x, k):
    x = jnp.where(iota(x.shape, 1) // CELL == k, x, 0.0)
    x = x + pltpu.roll(x, 64, 1)
    return x + pltpu.roll(x, 32, 1)


def store_pieces(pieces, up, down, mid):
    for out, order in ((up, UP), (down, DOWN), (mid, MID)):
        size = pieces[0].shape[0]
        for k, p in enumerate(order):
            out[k * size : (k + 1) * size, :] = pieces[p]


def arrived(left, right, up, down, size):
    at = lambda x, k: x[k * size : (k + 1) * size, :]
    return [at(right, 0), at(right, 1), at(right, 2), at(up, 1), at(down, 1), at(left, 0), at(left, 1), at(left, 2)]


def fetch(sems, *pairs):
    copies = [pltpu.make_async_copy(src, dst, sems.at[k]) for k, (src, dst) in enumerate(pairs)]
    for copy in copies:
        copy.start()
    return copies


def arrive(copies):
    for copy in copies:
        copy.wait()


def pack_kernel(pos_in, species_in, lists_in, up, down, mid, table_out, row_out, pos, species, lists, sems):
    arrive(fetch(sems, (pos_in, pos), (species_in, species), (lists_in, lists)))
    kinds = species[...].astype(F32)
    table = jnp.concatenate([kinds, pos[...], jnp.zeros((4, kinds.shape[1]), F32)], axis=0)
    table_out[...] = table
    hi = table.astype(BF16)
    rest = table - hi.astype(F32)
    mid_part = rest.astype(BF16)
    low = (rest - mid_part.astype(F32)).astype(BF16)
    row = jnp.concatenate([lists[p : p + 1, :] for p in range(8)], axis=1)
    row_out[...] = row.astype(F32)
    hot = jnp.where(iota((table.shape[1], row.shape[1]), 0) == row, 1.0, 0.0).astype(BF16)
    out = mm(hi, hot, NN) + mm(mid_part, hot, NN) + mm(low, hot, NN)
    pieces = [
        jnp.concatenate([out[k : k + 1, p * CELL : (p + 1) * CELL] for k in range(4)], axis=1) for p in range(8)
    ]
    store_pieces(pieces, up, down, mid)


def weight_kernel(
    count, table, row, pairs_in, embed_in, radial_one_in, mix_one_in, radial_two_in, mix_two_in, readout_in,
    w_hi, w_lo, mats, begins, radial, rows, xt, prc, hot, hot_t, plan_own, plan_ghost,
    pairs, embed, radial_one, mix_one, radial_two, mix_two, readout, sems,
):
    sources = (pairs_in, embed_in, radial_one_in, mix_one_in, radial_two_in, mix_two_in, readout_in)
    targets = (pairs, embed, radial_one, mix_one, radial_two, mix_two, readout)
    copies = fetch(sems, *zip(sources, targets))
    lists = row[...].astype(jnp.int32)
    hot[...] = jnp.where(iota(hot.shape, 0) == lists, 1.0, 0.0).astype(BF16)
    column = jnp.broadcast_to(row[...], (8, row.shape[1])).T[:, 0:1].astype(jnp.int32)
    hot_t[...] = jnp.where(iota(hot_t.shape, 1) == column, 1.0, 0.0).astype(BF16)
    t = table[...]
    for c in range(OWN):
        xt[c] = tile_group(t[:, (c // 4) * LANES : (c // 4 + 1) * LANES], c % 4)
    prc[...] = jnp.concatenate([t[1:4], t[0:1], t[4:8]], axis=0).T
    arrive(copies[:1])
    def clear(i, carry):
        plan_own[i] = 0
        plan_ghost[i] = 0
        return carry

    lax.fori_loop(0, 2 * SLOTS, clear, 0)

    def sort(i, carry):
        n_own, n_ghost = carry
        r, c = pairs[0, i], pairs[1, i]
        mine = c < OWN

        @pl.when(mine)
        def _():
            plan_own[2 * n_own] = r
            plan_own[2 * n_own + 1] = c

        @pl.when(jnp.logical_not(mine))
        def _():
            plan_ghost[2 * n_ghost] = r
            plan_ghost[2 * n_ghost + 1] = c - OWN

        step = mine.astype(jnp.int32)
        return n_own + step, n_ghost + 1 - step

    n_own, n_ghost = lax.fori_loop(0, count[0, 0], sort, (jnp.int32(0), jnp.int32(0)))
    plan_own[2 * SLOTS] = n_own
    plan_ghost[2 * SLOTS] = n_ghost
    arrive(copies[1:])
    w_hi[...], w_lo[...] = species_weights(embed[...], 0.5 * radial_one[...])
    for k, m in enumerate((mix_one[0], mix_one[4], mix_one[1], mix_one[3], mix_two[0])):
        mats[0, k * CH : (k + 1) * CH, :], mats[1, k * CH : (k + 1) * CH, :] = split(m)
    begins[0], begins[1] = split(mm3(split(embed[...]), split(mix_one[2]), NT))
    radial[...] = 0.5 * radial_two[...]
    both = readout[...]
    rows[0:1, :] = both[0:1, :] + mm3(split(both), split(mix_two[1]), NN)[1:2, :]
    rows[1:2, :] = both[1:2, :]


def own_first_kernel(plan_own, xt, prc, hist, tiles, shapes):
    hist[...] = jnp.zeros_like(hist)

    def block(r, c, weight, slot):
        add_histogram(r, c, own_keep(r, c, weight), prc, xt, hist, tiles, shapes, slot)

    for_blocks(plan_own, UNROLL_OWN, block)


def ghost_first_kernel(
    side, plan, hot_t, left, right, up, down, prc, hist_own,
    hist, xt, tiles, shapes, send_up, send_down, send_mid,
):
    rows = jnp.concatenate(arrived(left, right, up, down, 1), axis=0)
    for k in range(4):
        part = tile_group(rows, k)
        for p in range(8):
            shift = 0.0 if k in (0, 3) else float((STEPS_X, STEPS_Y)[k - 1][p] * side)
            xt[p, k : k + 1, :] = part[p : p + 1, :] + shift
    hist[...] = hist_own[...]

    def block(r, c, weight, slot):
        add_histogram(r, c, weight, prc, xt, hist, tiles, shapes, slot)

    for_blocks(plan, UNROLL_GHOST, block)

    hi, lo = split(hist[...])
    sent = mm(hot_t[...], hi, NN) + mm(hot_t[...], lo, NN)
    store_pieces([sent[p * CELL : (p + 1) * CELL] for p in range(8)], send_up, send_down, send_mid)


def first_update(joined, kind, weights, begin, mix04, mix1, mix3):
    size = joined.shape[0]
    a = mm3(split(joined), weights, NN)
    a0 = a[:, :CH]
    a1 = [a[:, (t + 1) * CH : (t + 2) * CH] for t in range(3)]
    power = a1[0] * a1[0] + a1[1] * a1[1] + a1[2] * a1[2]
    both = mm3_deep(split(a0), mix04, NT)
    z0 = both[:, :CH] + mm3_full(split(power), mix1, NT)
    gate = jax.nn.sigmoid(both[:, CH:])
    hot = jnp.where(kind == iota((size, NB), 1), 1.0, 0.0).astype(BF16)
    own = mm(hot, begin[0], NN) + mm(hot, begin[1], NN)
    lift = mm3_full(split(jnp.concatenate(a1, axis=0)), mix3, NT)
    lift = jnp.concatenate([lift[t * size : (t + 1) * size] for t in range(3)], axis=1)
    feat = jnp.concatenate(
        [z0 * jax.nn.sigmoid(z0) + own, lift * jnp.concatenate([gate] * 3, axis=1)], axis=1
    )
    return feat, a, jnp.concatenate([z0, gate], axis=1), lift


def first_pullback(gs, gv, a, gates, lift, weights, mix04, mix1, mix3):
    size = gs.shape[0]
    z0, gate = gates[:, :CH], gates[:, CH:]
    sg = jax.nn.sigmoid(z0)
    dz0 = gs * (sg * (1.0 + z0 * (1.0 - sg)))
    y = [lift[:, t * CH : (t + 1) * CH] for t in range(3)]
    dgate = gv[0] * y[0] + gv[1] * y[1] + gv[2] * y[2]
    dz4 = dgate * gate * (1.0 - gate)
    da0 = mm3_wide(split(jnp.concatenate([dz0, dz4], axis=1)), mix04, NN)
    dpower = 2.0 * mm3_full(split(dz0), mix1, NN)
    dy = mm3_full(split(jnp.concatenate([v * gate for v in gv], axis=0)), mix3, NN)
    parts = [da0] + [
        dy[t * size : (t + 1) * size] + a[:, (t + 1) * CH : (t + 2) * CH] * dpower for t in range(3)
    ]
    return mm3(split(jnp.concatenate(parts, axis=1)), weights, NT)


def mat(mats, first, rows):
    return mats[0, first : first + rows, :], mats[1, first : first + rows, :]


def mixes(mats):
    return mat(mats, 0, 2 * CH), mat(mats, 2 * CH, CH), mat(mats, 3 * CH, CH)


def features(g):
    return g[:, :CH], [g[:, (t + 1) * CH : (t + 2) * CH] for t in range(3)]


def own_update_kernel(joined, prc, w_hi, w_lo, begins, mats, feat, acc, gates, lifted):
    begin = begins[0], begins[1]
    mix_all = mixes(mats)

    def chunk(i, carry):
        rows = chunk_rows(i)
        kind = prc[rows, :][:, 3:4].astype(jnp.int32)
        out = first_update(joined[rows, :], kind, (w_hi[...], w_lo[...]), begin, *mix_all)
        feat[rows, :], acc[rows, :], gates[rows, :], lifted[rows, :] = out
        return carry

    lax.fori_loop(0, feat.shape[0] // CHUNK, chunk, 0)


def own_second_kernel(plan, tiles, feat, radial, acc):
    acc[...] = jnp.zeros_like(acc)

    def block(r, c, weight, slot):
        add_forward(r, c, tiles[slot], feat, radial, acc)

    for_blocks(plan, UNROLL_OWN, block)


def ghost_second_kernel(
    plan, tiles, xt, left, right, up, down, w_hi, w_lo, begins, mats, acc_own, radial, readout,
    zed, grad_acc, feat, send_up, send_down, send_mid,
    joined, lin, gates, lifted, grad_table, acc,
):
    ghosts = feat.shape[0]
    for p, piece in enumerate(arrived(left, right, up, down, CELL)):
        joined[p * CELL : (p + 1) * CELL, :] = piece
    begin = begins[0], begins[1]
    mix_all = mixes(mats)
    acc[...] = acc_own[...]
    grad_table[...] = jnp.zeros_like(grad_table)
    kinds = jnp.concatenate([xt[p][0:8, 0:CELL] for p in range(8)], axis=1).T[:, 0:1].astype(jnp.int32)
    for i in range(ghosts // CHUNK):
        rows = pl.ds(i * CHUNK, CHUNK)
        kind = kinds[i * CHUNK : (i + 1) * CHUNK]
        out = first_update(joined[rows, :], kind, (w_hi[...], w_lo[...]), begin, *mix_all)
        feat[rows, :], lin[rows, :], gates[rows, :], lifted[rows, :] = out

    def forward(r, c, weight, slot):
        add_forward(r, c, tiles[slot], feat, radial, acc)

    for_blocks(plan, UNROLL_GHOST, forward)

    mix0 = mat(mats, 4 * CH, CH)

    def chunk(i, carry):
        rows = chunk_rows(i)
        z = mm3_full(split(acc[rows, :]), mix0, NT)
        zed[rows, :] = z
        sg = jax.nn.sigmoid(z)
        gz = readout[1:2, :] * (sg * (1.0 + z * (1.0 - sg)))
        grad_acc[rows, :] = mm3_full(split(gz), mix0, NN)
        return carry

    lax.fori_loop(0, acc.shape[0] // CHUNK, chunk, 0)

    def backward(r, c, weight, slot):
        add_feature_grad(r, c, tiles[slot], grad_acc, radial, grad_table)

    for_blocks(plan, UNROLL_GHOST, backward)

    pieces = []
    for i in range(ghosts // CHUNK):
        rows = pl.ds(i * CHUNK, CHUNK)
        gs, gv = features(grad_table[rows, :])
        q = first_pullback(gs, gv, lin[rows, :], gates[rows, :], lifted[rows, :], (w_hi[...], w_lo[...]), *mix_all)
        pieces += [q[k * CELL : (k + 1) * CELL] for k in range(CHUNK // CELL)]
    store_pieces(pieces, send_up, send_down, send_mid)


def own_grad_kernel(
    plan, tiles, grad_acc, radial, lin, gates, lifted, w_hi, w_lo, mats, readout,
    quad,
    grad_table,
):
    atoms = quad.shape[0]
    grad_table[...] = jnp.zeros_like(grad_table)

    def block(r, c, weight, slot):
        add_feature_grad(r, c, tiles[slot], grad_acc, radial, grad_table)

    for_blocks(plan, UNROLL_OWN, block)
    mix_all = mixes(mats)
    carry_w = readout[0:1, :]

    def chunk(i, carry):
        rows = chunk_rows(i)
        gs, gv = features(grad_table[rows, :])
        quad[rows, :] = first_pullback(
            gs + carry_w, gv, lin[rows, :], gates[rows, :], lifted[rows, :], (w_hi[...], w_lo[...]), *mix_all
        )
        return carry

    lax.fori_loop(0, atoms // CHUNK, chunk, 0)


def shape_of(shapes, slot):
    whole = shapes[slot]
    parts = [whole[k * CELL : (k + 1) * CELL] for k in range(12)]
    return [parts[:NB]] + parts[NB:]


def ghost_force_kernel(plan, shapes, grad_acc, radial, feat, recv, send):
    recv[...] = jnp.zeros_like(recv)
    send[...] = jnp.zeros_like(send)

    def block(r, c, weight, slot):
        deriv = second_deriv(r, c, grad_acc, radial, feat)
        add_force(pair_force(deriv, *shape_of(shapes, slot)), r, c, recv, send)

    for_blocks(plan, UNROLL_GHOST, block)


def ghost_last_kernel(
    plan, hot, shapes, xt, quad_own, left, right, up, down, recv_two, send_two,
    quad, recv, send_up, send_down, send_mid,
    back_hi, back_lo, send,
):
    for p, piece in enumerate(arrived(left, right, up, down, CELL)):
        hi, lo = split(piece)
        back_hi[p * CELL : (p + 1) * CELL, :] = hi
        back_lo[p * CELL : (p + 1) * CELL, :] = lo
    recv[...] = recv_two[...]
    send[...] = send_two[...]

    def chunk(i, carry):
        rows = chunk_rows(i)
        pick = hot[rows, :]
        quad[rows, :] = quad_own[rows, :] + (mm(pick, back_hi[...], NN) + mm(pick, back_lo[...], NN))
        return carry

    lax.fori_loop(0, quad.shape[0] // CHUNK, chunk, 0)

    def block(r, c, weight, slot):
        add_force(pair_force(first_deriv(r, c, xt, quad), *shape_of(shapes, slot)), r, c, recv, send)

    for_blocks(plan, UNROLL_GHOST, block)
    store_pieces([send[p : p + 1, :] for p in range(8)], send_up, send_down, send_mid)


def by_axis(rows, count):
    lines = [
        jnp.concatenate([rows[p : p + 1, (t + 1) * CELL : (t + 2) * CELL] for p in range(count)], axis=1)
        for t in range(3)
    ]
    return lines


def add_own_force(plan, slot, shapes, xt, quad, grad_acc, radial, feat, recv, send):
    r, c = plan[2 * slot], plan[2 * slot + 1]
    one = first_deriv(r, c, xt, quad)
    two = second_deriv(r, c, grad_acc, radial, feat)
    add_force(pair_force([x + y for x, y in zip(one, two)], *shape_of(shapes, slot)), r, c, recv, send)


def own_start_kernel(
    plan, shapes, xt, quad, grad_acc, radial, feat, recv_ghost, zed, readout, recv, send, energy
):
    recv[...] = recv_ghost[...]
    send[...] = jnp.zeros_like(send)
    z = zed[...]
    site = readout[0:1, :] * feat[:, :CH] + readout[1:2, :] * (z * jax.nn.sigmoid(z))
    hi, lo = split(site)
    ones = jnp.ones((8, CH), BF16)
    energy[...] = (mm(ones, hi, NT) + mm(ones, lo, NT))[0:1, :]
    for slot in range(EARLY):
        add_own_force(plan, slot, shapes, xt, quad, grad_acc, radial, feat, recv, send)


def own_force_kernel(
    plan, shapes, xt, quad, grad_acc, radial, feat, recv_start, send_start, out, recv, send
):
    recv[...] = recv_start[...]
    send[...] = send_start[...]

    def block(r, c, weight, slot):
        add_own_force(plan, slot, shapes, xt, quad, grad_acc, radial, feat, recv, send)

    for_blocks(plan, UNROLL_OWN, block, EARLY)
    pick = jnp.where(iota((8, LANES), 0) + 1 == iota((8, LANES), 1) // CELL, 1.0, 0.0).astype(BF16)
    hi, lo = split(recv[...])
    total = mm(pick, hi, NT) + mm(pick, lo, NT)
    out[...] = total[0:3, :] - jnp.concatenate(by_axis(send, OWN), axis=0)


def last_kernel(hot, left, right, up, down, partial, out):
    rows = jnp.concatenate(arrived(left, right, up, down, 1), axis=0)
    lines = by_axis(rows, 8)
    back = jnp.concatenate(lines + [jnp.zeros((5, lines[0].shape[1]), F32)], axis=0)
    hi, lo = split(back)
    ghost = mm(hi, hot[...], NT) + mm(lo, hot[...], NT)
    out[...] = partial[...] - ghost[0:3, :]


def ring(axis, step):
    count = lax.axis_size(axis)
    return [(i, (i + step) % count) for i in range(count)]


def swap_both(axis, to_lower, to_upper):
    count = lax.axis_size(axis)
    even = lax.axis_index(axis) % 2 == 0
    inner = [(i, i ^ 1) for i in range(count)]
    outer = [(i, (i - 1) % count if i % 2 == 0 else (i + 1) % count) for i in range(count)]
    one = lax.ppermute(jnp.where(even, to_upper, to_lower), axis, inner)
    two = lax.ppermute(jnp.where(even, to_lower, to_upper), axis, outer)
    return jnp.where(even, one, two), jnp.where(even, two, one)


def exchange(up, down, mid, between=None):
    size = mid.shape[0] // 2
    part = lambda x, k: x[k * size : (k + 1) * size]
    down, up = swap_both("gy", down, up)
    if between is not None:
        up, down, between = lax.optimization_barrier((up, down, between))
    to_left = jnp.concatenate([part(up, 0), part(mid, 0), part(down, 0)])
    to_right = jnp.concatenate([part(up, 2), part(mid, 1), part(down, 2)])
    left, right = swap_both("gx", to_left, to_right)
    return (left, right, up, down), between


def in_hbm(*arrays):
    return [pltpu.with_memory_space_constraint(x, HBM) for x in arrays]


def call(kernel, outs, specs, scratch=()):
    spaces = [SMEM if s[1] == jnp.int32 else VMEM for s in outs]
    return pl.pallas_call(
        kernel,
        out_shape=[jax.ShapeDtypeStruct(*s) for s in outs],
        in_specs=[pl.BlockSpec(memory_space=s) for s in specs],
        out_specs=[pl.BlockSpec(memory_space=s) for s in spaces],
        scratch_shapes=list(scratch),
        compiler_params=PARAMS,
    )


def shards(
    positions, species, send_lists, cell_pairs, block_count,
    embed, radial_one, mix_one, radial_two, mix_two, readout,
):
    atoms = positions.shape[1]
    side = float((atoms * 10.0) ** (1.0 / 3.0))
    pairs = cell_pairs[0, 0].T
    lists = send_lists[0, 0]
    kinds = species[None, :]
    ghosts = lists.size
    f = lambda *shape: (shape, F32)
    b = lambda *shape: (shape, BF16)
    i = lambda *shape: (shape, jnp.int32)
    three = lambda size, width: [f(3 * size, width), f(3 * size, width), f(2 * size, width)]

    *sends, table, row = call(
        pack_kernel,
        three(1, LANES) + [f(8, atoms), f(1, ghosts)],
        [HBM] * 3,
        [
            VMEM((3, atoms), F32),
            VMEM((1, atoms), jnp.int32),
            VMEM((8, CELL), jnp.int32),
            pltpu.SemaphoreType.DMA((3,)),
        ],
    )(*in_hbm(positions, kinds, lists))
    ready = call(
        weight_kernel,
        [
            b(HIST, FEAT), b(HIST, FEAT), b(2, 5 * CH, CH), b(2, NB, CH), f(2, NB, CH), f(2, CH),
            f(OWN, 8, LANES), f(atoms, 8), b(atoms, ghosts), b(ghosts, atoms),
            i(2 * SLOTS + 1), i(2 * SLOTS + 1),
        ],
        [SMEM] + [VMEM] * 2 + [HBM] * 7,
        [SMEM(pairs.shape, jnp.int32)]
        + [VMEM(x.shape, F32) for x in (embed, radial_one, mix_one, radial_two, mix_two, readout)]
        + [pltpu.SemaphoreType.DMA((7,))],
    )(block_count, table, row, *in_hbm(pairs, embed, radial_one, mix_one, radial_two, mix_two, readout))
    moved, ready = exchange(*sends, ready)
    w_hi, w_lo, mats, begins, radial, rows, xt_own, prc, hot, hot_t, plan_own, plan_ghost = ready
    store = lambda slots: [b(slots, HIST, 2 * LANES), f(slots, 12 * CELL, LANES)]
    hist_own, tiles_own, shapes_own = call(
        own_first_kernel, [f(atoms, HIST)] + store(SLOTS), [SMEM] + [VMEM] * 2
    )(plan_own, xt_own, prc)
    hist, xt_ghost, tiles_ghost, shapes_ghost, *sends = call(
        functools.partial(ghost_first_kernel, side),
        [f(atoms, HIST), f(8, 8, LANES)] + store(SLOTS // 2) + three(CELL, HIST),
        [SMEM] + [VMEM] * 7,
    )(plan_ghost, hot_t, *moved, prc, hist_own)

    own = call(
        own_update_kernel, [f(atoms, FEAT), f(atoms, FEAT), f(atoms, 2 * CH), f(atoms, 3 * CH)], [VMEM] * 6
    )(hist, prc, w_hi, w_lo, begins, mats)
    moved, own = exchange(*sends, own)
    feat, lin, gates, lifted = own
    (acc_own,) = call(own_second_kernel, [f(atoms, CH)], [SMEM] + [VMEM] * 3)(plan_own, tiles_own, feat, radial)
    zed, grad_acc, feat_ghost, *sends = call(
        ghost_second_kernel,
        [f(atoms, CH), f(atoms, CH), f(ghosts, FEAT)] + three(CELL, HIST),
        [SMEM] + [VMEM] * 13,
        [
            VMEM((ghosts, HIST), F32),
            VMEM((ghosts, FEAT), F32),
            VMEM((ghosts, 2 * CH), F32),
            VMEM((ghosts, 3 * CH), F32),
            VMEM((ghosts, FEAT), F32),
            VMEM((atoms, CH), F32),
        ],
    )(plan_ghost, tiles_ghost, xt_ghost, *moved, w_hi, w_lo, begins, mats, acc_own, radial, rows)

    two = call(ghost_force_kernel, [f(atoms, LANES), f(8, LANES)], [SMEM] + [VMEM] * 4)(
        plan_ghost, shapes_ghost, grad_acc, radial, feat_ghost
    )
    moved, two = exchange(*sends, two)
    recv_two, send_two = two
    (quad_own,) = call(
        own_grad_kernel, [f(atoms, HIST)], [SMEM] + [VMEM] * 10, [VMEM((atoms, FEAT), F32)]
    )(plan_own, tiles_own, grad_acc, radial, lin, gates, lifted, w_hi, w_lo, mats, rows)
    quad, recv, *sends = call(
        ghost_last_kernel,
        [f(atoms, HIST), f(atoms, LANES)] + three(1, LANES),
        [SMEM] + [VMEM] * 10,
        [VMEM((ghosts, HIST), BF16), VMEM((ghosts, HIST), BF16), VMEM((8, LANES), F32)],
    )(plan_ghost, hot, shapes_ghost, xt_ghost, quad_own, *moved, recv_two, send_two)

    shared = (plan_own, shapes_own, xt_own, quad, grad_acc, radial, feat)
    early = call(
        own_start_kernel, [f(atoms, LANES), f(OWN, LANES), f(1, atoms)], [SMEM] + [VMEM] * 9
    )(*shared, recv, zed, rows)
    moved, early = exchange(*sends, early)
    recv, send, energy = early
    (partial,) = call(
        own_force_kernel,
        [f(3, atoms)],
        [SMEM] + [VMEM] * 8,
        [VMEM((atoms, LANES), F32), VMEM((OWN, LANES), F32)],
    )(*shared, recv, send)
    (forces,) = call(last_kernel, [f(3, atoms)], [VMEM] * 6)(hot, *moved, partial)
    return forces, energy[0]


def solution(mesh):
    both = P(("gx", "gy"))
    in_specs = (
        P(None, ("gx", "gy")),
        both,
        P("gx", "gy", None, None),
        P("gx", "gy", None, None),
        P("gx", "gy"),
    ) + (P(),) * 6
    out_specs = (P(None, ("gx", "gy")), both)
    return jax.shard_map(shards, mesh=mesh, in_specs=in_specs, out_specs=out_specs, check_vma=False)
```

```python
import functools

import jax
import jax.numpy as jnp
import numpy as np
from jax import lax
from jax.experimental import pallas as pl
from jax.experimental.pallas import tpu as pltpu
from jax.sharding import PartitionSpec as P

NB = 8
CELL = 32
CH = 128
LANES = 128
OWN = 16
CUT2 = 25.0
STEPS_X = np.array([-1, -1, -1, 0, 0, 1, 1, 1])
STEPS_Y = np.array([-1, 0, 1, -1, 1, -1, 0, 1])
F32 = jnp.float32
BF16 = jnp.bfloat16
VMEM = pltpu.VMEM
SMEM = pltpu.SMEM
HBM = pltpu.HBM
PARAMS = pltpu.CompilerParams(vmem_limit_bytes=20 * 1024 * 1024)
CHUNK = 128
HIST = 256
FEAT = 512
SLOTS = 32
UNROLL_OWN = (8, 4)
EARLY = 8
UNROLL_GHOST = (8, 2)
UP = (2, 4, 7)
DOWN = (0, 3, 5)
MID = (1, 6)

NN = (((1,), (0,)), ((), ()))
NT = (((1,), (1,)), ((), ()))
TN = (((0,), (0,)), ((), ()))


def split(x):
    hi = x.astype(BF16)
    return hi, (x - hi.astype(F32)).astype(BF16)


def mm(a, b, dims):
    return lax.dot_general(a, b, dims, preferred_element_type=F32)


def mm3(a, b, dims):
    (ah, al), (bh, bl) = a, b
    return mm(ah, bh, dims) + (mm(ah, bl, dims) + mm(al, bh, dims))


def mm3_deep(a, b, dims):
    (ah, al), (bh, bl) = a, b
    axis = dims[0][1][0]
    return mm(jnp.concatenate([ah, al], axis=1), jnp.concatenate([bh, bh], axis=axis), dims) + mm(ah, bl, dims)


def mm3_wide(a, b, dims):
    (ah, al), (bh, bl) = a, b
    width = 128
    out = mm(ah, jnp.concatenate([bh, bl], axis=1 - dims[0][1][0]), dims)
    return out[:, :width] + (out[:, width:] + mm(al, bh, dims))


def mm3_full(a, b, dims):
    (ah, al), (bh, bl) = a, b
    axis = dims[0][1][0]
    top = jnp.concatenate([bh, bh], axis=axis)
    low = jnp.concatenate([bl, jnp.zeros_like(bl)], axis=axis)
    out = mm(jnp.concatenate([ah, al], axis=1), jnp.concatenate([top, low], axis=1 - axis), dims)
    return out[:, :128] + out[:, 128:]


def iota(shape, dim):
    return lax.broadcasted_iota(jnp.int32, shape, dim)


def cell_rows(c):
    return pl.ds(pl.multiple_of(c * CELL, CELL), CELL)


def chunk_rows(i):
    return pl.ds(pl.multiple_of(i * CHUNK, CHUNK), CHUNK)


def geometry(r, c, keep, prc, xt):
    own = prc[cell_rows(r), :]
    far = xt[c]
    vec = [far[t + 1 : t + 2, :] - own[:, t : t + 1] for t in range(3)]
    sq = vec[0] * vec[0] + vec[1] * vec[1] + vec[2] * vec[2]
    group = iota((CELL, LANES), 1) // CELL
    edge = jnp.maximum(1.0 - sq * (1.0 / CUT2), 0.0)
    slope = edge * keep
    vk = jnp.where(group == 0, 1.0, jnp.where(group == 1, vec[0], jnp.where(group == 2, vec[1], vec[2])))
    scaled = sq * ((NB - 1) / CUT2)
    return edge * slope, slope, scaled, vk


def own_keep(r, c, weight):
    lane = iota((CELL, LANES), 1)
    row = iota((CELL, LANES), 0)
    return jnp.where(jnp.logical_and(lane % CELL == row, r == c), 0.0, weight)


def basis(scaled, n):
    off = scaled - float(n)
    return jnp.exp(-(off * off))


def all_bases(scaled):
    return [basis(scaled, n) for n in range(NB)]


def pair_force(deriv, bases, env, slope, scaled, vk):
    total = None
    moment = None
    for n in range(NB):
        term = deriv[n] * bases[n]
        total = term if n == 0 else total + term
        if n == 1:
            moment = term
        elif n > 1:
            moment = moment + float(n) * term
    spacing = CUT2 / (NB - 1)
    by_sq = (-2.0 / CUT2) * slope * total - (2.0 / spacing) * env * (scaled * total - moment)
    by_sq = by_sq * vk
    by_sq = by_sq + pltpu.roll(by_sq, 64, 1)
    by_sq = by_sq + pltpu.roll(by_sq, 32, 1)
    return env * total + 2.0 * vk * by_sq


def add_force(force, r, c, recv, send):
    recv[cell_rows(r), :] += force
    send[pl.ds(c, 1), :] += jnp.sum(force, axis=0, keepdims=True)


def species_tile(c, xt):
    row = iota((4 * NB, LANES), 0)
    lane = iota((4 * NB, LANES), 1)
    kind = xt[c][0:1, :].astype(jnp.int32)
    hit = jnp.logical_and(kind == row % NB, lane // CELL == row // NB)
    hot = jnp.where(hit, 1.0, 0.0).astype(BF16)
    zero = jnp.zeros_like(hot)
    return jnp.concatenate(
        [jnp.concatenate([hot if j == k else zero for k in range(4)], axis=1) for j in range(4)], axis=0
    )


def add_histogram(r, c, keep, prc, xt, hist, tiles, shapes, slot):
    env, slope, scaled, vk = geometry(r, c, keep, prc, xt)
    bases = all_bases(scaled)
    m = env * vk
    parts = [split(m * e) for e in bases]
    tiles[slot] = jnp.concatenate([jnp.concatenate([p[k] for p in parts], axis=0) for k in range(2)], axis=1)
    shapes[slot] = jnp.concatenate(bases + [env, slope, scaled, vk], axis=0)
    wide = [
        jnp.concatenate([p[k] for p in parts[4 * h : 4 * h + 4]], axis=1) for k in range(2) for h in range(2)
    ]
    out = mm(jnp.concatenate(wide, axis=0), species_tile(c, xt), NT)
    out = out[: 2 * CELL] + out[2 * CELL :]
    hist[cell_rows(r), :] += jnp.concatenate([out[:CELL], out[CELL:]], axis=1)


def first_deriv(r, c, xt, quad):
    q = quad[cell_rows(r), :]
    q = jnp.concatenate([q[:, :LANES], q[:, LANES:]], axis=0)
    out = mm(jnp.concatenate(split(q), axis=0), species_tile(c, xt), NN)
    out = out[: 2 * CELL] + out[2 * CELL :]
    return [out[(n // 4) * CELL : (n // 4 + 1) * CELL, (n % 4) * LANES : (n % 4 + 1) * LANES] for n in range(NB)]


def cell_features(table, c):
    hi, lo = split(table[cell_rows(c), :])
    zero = jnp.zeros((CELL, CH), BF16)

    def lay(x):
        rows = [jnp.concatenate([x[:, :CH], zero], axis=1)]
        rows += [jnp.concatenate([zero, x[:, (t + 1) * CH : (t + 2) * CH]], axis=1) for t in range(3)]
        return jnp.concatenate(rows, axis=0)

    return lay(hi), lay(lo)


def spread(g, radial):
    both = [
        jnp.concatenate([g * radial[0, n : n + 1, :], g * radial[1, n : n + 1, :]], axis=1) for n in range(NB)
    ]
    return split(jnp.concatenate(both, axis=0))


def add_forward(r, c, tile, table, radial, acc):
    fh, fl = cell_features(table, c)
    prod = mm(tile, jnp.concatenate([fh, fh], axis=0), NN) + mm(tile[:, :LANES], fl, NN)
    part = None
    for n in range(NB):
        rows = prod[n * CELL : (n + 1) * CELL]
        term = rows[:, :CH] * radial[0, n : n + 1, :] + rows[:, CH:] * radial[1, n : n + 1, :]
        part = term if n == 0 else part + term
    acc[cell_rows(r), :] += part


def add_feature_grad(r, c, tile, grad_acc, radial, grad_table):
    uh, ul = spread(grad_acc[cell_rows(r), :], radial)
    gf = mm(tile, uh, TN)
    gf = gf[:LANES] + (gf[LANES:] + mm(tile[:, :LANES], ul, TN))
    grad_table[cell_rows(c), :] += jnp.concatenate(
        [gf[0:CELL, :CH]] + [gf[(t + 1) * CELL : (t + 2) * CELL, CH:] for t in range(3)], axis=1
    )


def second_deriv(r, c, grad_acc, radial, table):
    out = mm3_wide(spread(grad_acc[cell_rows(r), :], radial), cell_features(table, c), NT)
    return [out[n * CELL : (n + 1) * CELL] for n in range(NB)]


def for_blocks(plan, unroll, body, skip=0):
    count = plan[2 * SLOTS]
    large, small = unroll
    whole = (count - skip) // large
    start = skip + whole * large

    def step(first, size):
        def run(i, carry):
            for k in range(size):
                slot = first + i * size + k
                weight = jnp.where(slot < count, 1.0, 0.0).astype(F32)
                body(plan[2 * slot], plan[2 * slot + 1], weight, slot)
            return carry

        return run

    lax.fori_loop(0, whole, step(skip, large), 0)
    lax.fori_loop(0, (count - start + small - 1) // small, step(start, small), 0)


def species_weights(embed, radial):
    zero = jnp.zeros((NB, CH), F32)
    rows = []
    for n in range(NB):
        for k in range(4):
            part = embed * radial[min(k, 1), n : n + 1, :]
            rows.append(jnp.concatenate([part if j == k else zero for j in range(4)], axis=1))
    return split(jnp.concatenate(rows, axis=0))


def tile_group(x, k):
    x = jnp.where(iota(x.shape, 1) // CELL == k, x, 0.0)
    x = x + pltpu.roll(x, 64, 1)
    return x + pltpu.roll(x, 32, 1)


def store_pieces(pieces, up, down, mid):
    for out, order in ((up, UP), (down, DOWN), (mid, MID)):
        size = pieces[0].shape[0]
        for k, p in enumerate(order):
            out[k * size : (k + 1) * size, :] = pieces[p]


def arrived(left, right, up, down, size):
    at = lambda x, k: x[k * size : (k + 1) * size, :]
    return [at(right, 0), at(right, 1), at(right, 2), at(up, 1), at(down, 1), at(left, 0), at(left, 1), at(left, 2)]


def fetch(sems, *pairs):
    copies = [pltpu.make_async_copy(src, dst, sems.at[k]) for k, (src, dst) in enumerate(pairs)]
    for copy in copies:
        copy.start()
    return copies


def arrive(copies):
    for copy in copies:
        copy.wait()


def pack_kernel(pos_in, species_in, lists_in, up, down, mid, table_out, row_out, pos, species, lists, sems):
    arrive(fetch(sems, (pos_in, pos), (species_in, species), (lists_in, lists)))
    kinds = species[...].astype(F32)
    table = jnp.concatenate([kinds, pos[...], jnp.zeros((4, kinds.shape[1]), F32)], axis=0)
    table_out[...] = table
    hi = table.astype(BF16)
    rest = table - hi.astype(F32)
    mid_part = rest.astype(BF16)
    low = (rest - mid_part.astype(F32)).astype(BF16)
    row = jnp.concatenate([lists[p : p + 1, :] for p in range(8)], axis=1)
    row_out[...] = row.astype(F32)
    hot = jnp.where(iota((table.shape[1], row.shape[1]), 0) == row, 1.0, 0.0).astype(BF16)
    out = mm(hi, hot, NN) + mm(mid_part, hot, NN) + mm(low, hot, NN)
    pieces = [
        jnp.concatenate([out[k : k + 1, p * CELL : (p + 1) * CELL] for k in range(4)], axis=1) for p in range(8)
    ]
    store_pieces(pieces, up, down, mid)


def weight_kernel(
    count, table, row, pairs_in, embed_in, radial_one_in, mix_one_in, radial_two_in, mix_two_in, readout_in,
    w_hi, w_lo, mats, begins, radial, rows, xt, prc, hot, hot_t, plan_own, plan_ghost,
    pairs, embed, radial_one, mix_one, radial_two, mix_two, readout, sems,
):
    sources = (pairs_in, embed_in, radial_one_in, mix_one_in, radial_two_in, mix_two_in, readout_in)
    targets = (pairs, embed, radial_one, mix_one, radial_two, mix_two, readout)
    copies = fetch(sems, *zip(sources, targets))
    lists = row[...].astype(jnp.int32)
    hot[...] = jnp.where(iota(hot.shape, 0) == lists, 1.0, 0.0).astype(BF16)
    column = jnp.broadcast_to(row[...], (8, row.shape[1])).T[:, 0:1].astype(jnp.int32)
    hot_t[...] = jnp.where(iota(hot_t.shape, 1) == column, 1.0, 0.0).astype(BF16)
    t = table[...]
    for c in range(OWN):
        xt[c] = tile_group(t[:, (c // 4) * LANES : (c // 4 + 1) * LANES], c % 4)
    prc[...] = jnp.concatenate([t[1:4], t[0:1], t[4:8]], axis=0).T
    arrive(copies[:1])
    def clear(i, carry):
        plan_own[i] = 0
        plan_ghost[i] = 0
        return carry

    lax.fori_loop(0, 2 * SLOTS, clear, 0)

    def sort(i, carry):
        n_own, n_ghost = carry
        r, c = pairs[0, i], pairs[1, i]
        mine = c < OWN

        @pl.when(mine)
        def _():
            plan_own[2 * n_own] = r
            plan_own[2 * n_own + 1] = c

        @pl.when(jnp.logical_not(mine))
        def _():
            plan_ghost[2 * n_ghost] = r
            plan_ghost[2 * n_ghost + 1] = c - OWN

        step = mine.astype(jnp.int32)
        return n_own + step, n_ghost + 1 - step

    n_own, n_ghost = lax.fori_loop(0, count[0, 0], sort, (jnp.int32(0), jnp.int32(0)))
    plan_own[2 * SLOTS] = n_own
    plan_ghost[2 * SLOTS] = n_ghost
    arrive(copies[1:])
    w_hi[...], w_lo[...] = species_weights(embed[...], 0.5 * radial_one[...])
    for k, m in enumerate((mix_one[0], mix_one[4], mix_one[1], mix_one[3], mix_two[0])):
        mats[0, k * CH : (k + 1) * CH, :], mats[1, k * CH : (k + 1) * CH, :] = split(m)
    begins[0], begins[1] = split(mm3(split(embed[...]), split(mix_one[2]), NT))
    radial[...] = 0.5 * radial_two[...]
    both = readout[...]
    rows[0:1, :] = both[0:1, :] + mm3(split(both), split(mix_two[1]), NN)[1:2, :]
    rows[1:2, :] = both[1:2, :]


def own_first_kernel(plan_own, xt, prc, hist, tiles, shapes):
    hist[...] = jnp.zeros_like(hist)

    def block(r, c, weight, slot):
        add_histogram(r, c, own_keep(r, c, weight), prc, xt, hist, tiles, shapes, slot)

    for_blocks(plan_own, UNROLL_OWN, block)


def ghost_first_kernel(
    side, plan, hot_t, left, right, up, down, prc, hist_own,
    hist, xt, tiles, shapes, send_up, send_down, send_mid,
):
    rows = jnp.concatenate(arrived(left, right, up, down, 1), axis=0)
    for k in range(4):
        part = tile_group(rows, k)
        for p in range(8):
            shift = 0.0 if k in (0, 3) else float((STEPS_X, STEPS_Y)[k - 1][p] * side)
            xt[p, k : k + 1, :] = part[p : p + 1, :] + shift
    hist[...] = hist_own[...]

    def block(r, c, weight, slot):
        add_histogram(r, c, weight, prc, xt, hist, tiles, shapes, slot)

    for_blocks(plan, UNROLL_GHOST, block)

    hi, lo = split(hist[...])
    sent = mm(hot_t[...], hi, NN) + mm(hot_t[...], lo, NN)
    store_pieces([sent[p * CELL : (p + 1) * CELL] for p in range(8)], send_up, send_down, send_mid)


def first_update(joined, kind, weights, begin, mix04, mix1, mix3):
    size = joined.shape[0]
    a = mm3(split(joined), weights, NN)
    a0 = a[:, :CH]
    a1 = [a[:, (t + 1) * CH : (t + 2) * CH] for t in range(3)]
    power = a1[0] * a1[0] + a1[1] * a1[1] + a1[2] * a1[2]
    both = mm3_deep(split(a0), mix04, NT)
    z0 = both[:, :CH] + mm3_full(split(power), mix1, NT)
    gate = jax.nn.sigmoid(both[:, CH:])
    hot = jnp.where(kind == iota((size, NB), 1), 1.0, 0.0).astype(BF16)
    own = mm(hot, begin[0], NN) + mm(hot, begin[1], NN)
    lift = mm3_full(split(jnp.concatenate(a1, axis=0)), mix3, NT)
    lift = jnp.concatenate([lift[t * size : (t + 1) * size] for t in range(3)], axis=1)
    feat = jnp.concatenate(
        [z0 * jax.nn.sigmoid(z0) + own, lift * jnp.concatenate([gate] * 3, axis=1)], axis=1
    )
    return feat, a, jnp.concatenate([z0, gate], axis=1), lift


def first_pullback(gs, gv, a, gates, lift, weights, mix04, mix1, mix3):
    size = gs.shape[0]
    z0, gate = gates[:, :CH], gates[:, CH:]
    sg = jax.nn.sigmoid(z0)
    dz0 = gs * (sg * (1.0 + z0 * (1.0 - sg)))
    y = [lift[:, t * CH : (t + 1) * CH] for t in range(3)]
    dgate = gv[0] * y[0] + gv[1] * y[1] + gv[2] * y[2]
    dz4 = dgate * gate * (1.0 - gate)
    da0 = mm3_wide(split(jnp.concatenate([dz0, dz4], axis=1)), mix04, NN)
    dpower = 2.0 * mm3_full(split(dz0), mix1, NN)
    dy = mm3_full(split(jnp.concatenate([v * gate for v in gv], axis=0)), mix3, NN)
    parts = [da0] + [
        dy[t * size : (t + 1) * size] + a[:, (t + 1) * CH : (t + 2) * CH] * dpower for t in range(3)
    ]
    return mm3(split(jnp.concatenate(parts, axis=1)), weights, NT)


def mat(mats, first, rows):
    return mats[0, first : first + rows, :], mats[1, first : first + rows, :]


def mixes(mats):
    return mat(mats, 0, 2 * CH), mat(mats, 2 * CH, CH), mat(mats, 3 * CH, CH)


def features(g):
    return g[:, :CH], [g[:, (t + 1) * CH : (t + 2) * CH] for t in range(3)]


def own_update_kernel(joined, prc, w_hi, w_lo, begins, mats, feat, acc, gates, lifted):
    begin = begins[0], begins[1]
    mix_all = mixes(mats)

    def chunk(i, carry):
        rows = chunk_rows(i)
        kind = prc[rows, :][:, 3:4].astype(jnp.int32)
        out = first_update(joined[rows, :], kind, (w_hi[...], w_lo[...]), begin, *mix_all)
        feat[rows, :], acc[rows, :], gates[rows, :], lifted[rows, :] = out
        return carry

    lax.fori_loop(0, feat.shape[0] // CHUNK, chunk, 0)


def own_second_kernel(plan, tiles, feat, radial, acc):
    acc[...] = jnp.zeros_like(acc)

    def block(r, c, weight, slot):
        add_forward(r, c, tiles[slot], feat, radial, acc)

    for_blocks(plan, UNROLL_OWN, block)


def ghost_second_kernel(
    plan, tiles, xt, left, right, up, down, w_hi, w_lo, begins, mats, acc_own, radial, readout,
    zed, grad_acc, feat, send_up, send_down, send_mid,
    joined, lin, gates, lifted, grad_table, acc,
):
    ghosts = feat.shape[0]
    for p, piece in enumerate(arrived(left, right, up, down, CELL)):
        joined[p * CELL : (p + 1) * CELL, :] = piece
    begin = begins[0], begins[1]
    mix_all = mixes(mats)
    acc[...] = acc_own[...]
    grad_table[...] = jnp.zeros_like(grad_table)
    kinds = jnp.concatenate([xt[p][0:8, 0:CELL] for p in range(8)], axis=1).T[:, 0:1].astype(jnp.int32)
    for i in range(ghosts // CHUNK):
        rows = pl.ds(i * CHUNK, CHUNK)
        kind = kinds[i * CHUNK : (i + 1) * CHUNK]
        out = first_update(joined[rows, :], kind, (w_hi[...], w_lo[...]), begin, *mix_all)
        feat[rows, :], lin[rows, :], gates[rows, :], lifted[rows, :] = out

    def forward(r, c, weight, slot):
        add_forward(r, c, tiles[slot], feat, radial, acc)

    for_blocks(plan, UNROLL_GHOST, forward)

    mix0 = mat(mats, 4 * CH, CH)

    def chunk(i, carry):
        rows = chunk_rows(i)
        z = mm3_full(split(acc[rows, :]), mix0, NT)
        zed[rows, :] = z
        sg = jax.nn.sigmoid(z)
        gz = readout[1:2, :] * (sg * (1.0 + z * (1.0 - sg)))
        grad_acc[rows, :] = mm3_full(split(gz), mix0, NN)
        return carry

    lax.fori_loop(0, acc.shape[0] // CHUNK, chunk, 0, unroll=True)

    def backward(r, c, weight, slot):
        add_feature_grad(r, c, tiles[slot], grad_acc, radial, grad_table)

    for_blocks(plan, UNROLL_GHOST, backward)

    pieces = []
    for i in range(ghosts // CHUNK):
        rows = pl.ds(i * CHUNK, CHUNK)
        gs, gv = features(grad_table[rows, :])
        q = first_pullback(gs, gv, lin[rows, :], gates[rows, :], lifted[rows, :], (w_hi[...], w_lo[...]), *mix_all)
        pieces += [q[k * CELL : (k + 1) * CELL] for k in range(CHUNK // CELL)]
    store_pieces(pieces, send_up, send_down, send_mid)


def own_grad_kernel(
    plan, tiles, grad_acc, radial, lin, gates, lifted, w_hi, w_lo, mats, readout,
    quad,
    grad_table,
):
    atoms = quad.shape[0]
    grad_table[...] = jnp.zeros_like(grad_table)

    def block(r, c, weight, slot):
        add_feature_grad(r, c, tiles[slot], grad_acc, radial, grad_table)

    for_blocks(plan, UNROLL_OWN, block)
    mix_all = mixes(mats)
    carry_w = readout[0:1, :]

    def chunk(i, carry):
        rows = chunk_rows(i)
        gs, gv = features(grad_table[rows, :])
        quad[rows, :] = first_pullback(
            gs + carry_w, gv, lin[rows, :], gates[rows, :], lifted[rows, :], (w_hi[...], w_lo[...]), *mix_all
        )
        return carry

    lax.fori_loop(0, atoms // CHUNK, chunk, 0)


def shape_of(shapes, slot):
    whole = shapes[slot]
    parts = [whole[k * CELL : (k + 1) * CELL] for k in range(12)]
    return [parts[:NB]] + parts[NB:]


def ghost_force_kernel(plan, shapes, grad_acc, radial, feat, recv, send):
    recv[...] = jnp.zeros_like(recv)
    send[...] = jnp.zeros_like(send)

    def block(r, c, weight, slot):
        deriv = second_deriv(r, c, grad_acc, radial, feat)
        add_force(pair_force(deriv, *shape_of(shapes, slot)), r, c, recv, send)

    for_blocks(plan, UNROLL_GHOST, block)


def ghost_last_kernel(
    plan, hot, shapes, xt, quad_own, left, right, up, down, recv_two, send_two,
    quad, recv, send_up, send_down, send_mid,
    back_hi, back_lo, send,
):
    for p, piece in enumerate(arrived(left, right, up, down, CELL)):
        hi, lo = split(piece)
        back_hi[p * CELL : (p + 1) * CELL, :] = hi
        back_lo[p * CELL : (p + 1) * CELL, :] = lo
    recv[...] = recv_two[...]
    send[...] = send_two[...]

    def chunk(i, carry):
        rows = chunk_rows(i)
        pick = hot[rows, :]
        quad[rows, :] = quad_own[rows, :] + (mm(pick, back_hi[...], NN) + mm(pick, back_lo[...], NN))
        return carry

    lax.fori_loop(0, quad.shape[0] // CHUNK, chunk, 0, unroll=True)

    def block(r, c, weight, slot):
        add_force(pair_force(first_deriv(r, c, xt, quad), *shape_of(shapes, slot)), r, c, recv, send)

    for_blocks(plan, UNROLL_GHOST, block)
    store_pieces([send[p : p + 1, :] for p in range(8)], send_up, send_down, send_mid)


def by_axis(rows, count):
    lines = [
        jnp.concatenate([rows[p : p + 1, (t + 1) * CELL : (t + 2) * CELL] for p in range(count)], axis=1)
        for t in range(3)
    ]
    return lines


def add_own_force(plan, slot, shapes, xt, quad, grad_acc, radial, feat, recv, send):
    r, c = plan[2 * slot], plan[2 * slot + 1]
    one = first_deriv(r, c, xt, quad)
    two = second_deriv(r, c, grad_acc, radial, feat)
    add_force(pair_force([x + y for x, y in zip(one, two)], *shape_of(shapes, slot)), r, c, recv, send)


def own_start_kernel(
    plan, shapes, xt, quad, grad_acc, radial, feat, recv_ghost, zed, readout, recv, send, energy
):
    recv[...] = recv_ghost[...]
    send[...] = jnp.zeros_like(send)
    z = zed[...]
    site = readout[0:1, :] * feat[:, :CH] + readout[1:2, :] * (z * jax.nn.sigmoid(z))
    hi, lo = split(site)
    ones = jnp.ones((8, CH), BF16)
    energy[...] = (mm(ones, hi, NT) + mm(ones, lo, NT))[0:1, :]
    for slot in range(EARLY):
        add_own_force(plan, slot, shapes, xt, quad, grad_acc, radial, feat, recv, send)


def own_force_kernel(
    plan, shapes, xt, quad, grad_acc, radial, feat, recv_start, send_start, out, recv, send
):
    recv[...] = recv_start[...]
    send[...] = send_start[...]

    def block(r, c, weight, slot):
        add_own_force(plan, slot, shapes, xt, quad, grad_acc, radial, feat, recv, send)

    for_blocks(plan, UNROLL_OWN, block, EARLY)
    pick = jnp.where(iota((8, LANES), 0) + 1 == iota((8, LANES), 1) // CELL, 1.0, 0.0).astype(BF16)
    hi, lo = split(recv[...])
    total = mm(pick, hi, NT) + mm(pick, lo, NT)
    out[...] = total[0:3, :] - jnp.concatenate(by_axis(send, OWN), axis=0)


def last_kernel(hot, left, right, up, down, partial, out):
    rows = jnp.concatenate(arrived(left, right, up, down, 1), axis=0)
    lines = by_axis(rows, 8)
    back = jnp.concatenate(lines + [jnp.zeros((5, lines[0].shape[1]), F32)], axis=0)
    hi, lo = split(back)
    ghost = mm(hi, hot[...], NT) + mm(lo, hot[...], NT)
    out[...] = partial[...] - ghost[0:3, :]


def ring(axis, step):
    count = lax.axis_size(axis)
    return [(i, (i + step) % count) for i in range(count)]


def swap_both(axis, to_lower, to_upper):
    count = lax.axis_size(axis)
    even = lax.axis_index(axis) % 2 == 0
    inner = [(i, i ^ 1) for i in range(count)]
    outer = [(i, (i - 1) % count if i % 2 == 0 else (i + 1) % count) for i in range(count)]
    one = lax.ppermute(jnp.where(even, to_upper, to_lower), axis, inner)
    two = lax.ppermute(jnp.where(even, to_lower, to_upper), axis, outer)
    return jnp.where(even, one, two), jnp.where(even, two, one)


def exchange(up, down, mid, between=None):
    size = mid.shape[0] // 2
    part = lambda x, k: x[k * size : (k + 1) * size]
    down, up = swap_both("gy", down, up)
    if between is not None:
        up, down, between = lax.optimization_barrier((up, down, between))
    to_left = jnp.concatenate([part(up, 0), part(mid, 0), part(down, 0)])
    to_right = jnp.concatenate([part(up, 2), part(mid, 1), part(down, 2)])
    left, right = swap_both("gx", to_left, to_right)
    return (left, right, up, down), between


def in_hbm(*arrays):
    return [pltpu.with_memory_space_constraint(x, HBM) for x in arrays]


def call(kernel, outs, specs, scratch=()):
    spaces = [SMEM if s[1] == jnp.int32 else VMEM for s in outs]
    return pl.pallas_call(
        kernel,
        out_shape=[jax.ShapeDtypeStruct(*s) for s in outs],
        in_specs=[pl.BlockSpec(memory_space=s) for s in specs],
        out_specs=[pl.BlockSpec(memory_space=s) for s in spaces],
        scratch_shapes=list(scratch),
        compiler_params=PARAMS,
    )


def shards(
    positions, species, send_lists, cell_pairs, block_count,
    embed, radial_one, mix_one, radial_two, mix_two, readout,
):
    atoms = positions.shape[1]
    side = float((atoms * 10.0) ** (1.0 / 3.0))
    pairs = cell_pairs[0, 0].T
    lists = send_lists[0, 0]
    kinds = species[None, :]
    ghosts = lists.size
    f = lambda *shape: (shape, F32)
    b = lambda *shape: (shape, BF16)
    i = lambda *shape: (shape, jnp.int32)
    three = lambda size, width: [f(3 * size, width), f(3 * size, width), f(2 * size, width)]

    *sends, table, row = call(
        pack_kernel,
        three(1, LANES) + [f(8, atoms), f(1, ghosts)],
        [HBM] * 3,
        [
            VMEM((3, atoms), F32),
            VMEM((1, atoms), jnp.int32),
            VMEM((8, CELL), jnp.int32),
            pltpu.SemaphoreType.DMA((3,)),
        ],
    )(*in_hbm(positions, kinds, lists))
    ready = call(
        weight_kernel,
        [
            b(HIST, FEAT), b(HIST, FEAT), b(2, 5 * CH, CH), b(2, NB, CH), f(2, NB, CH), f(2, CH),
            f(OWN, 8, LANES), f(atoms, 8), b(atoms, ghosts), b(ghosts, atoms),
            i(2 * SLOTS + 1), i(2 * SLOTS + 1),
        ],
        [SMEM] + [VMEM] * 2 + [HBM] * 7,
        [SMEM(pairs.shape, jnp.int32)]
        + [VMEM(x.shape, F32) for x in (embed, radial_one, mix_one, radial_two, mix_two, readout)]
        + [pltpu.SemaphoreType.DMA((7,))],
    )(block_count, table, row, *in_hbm(pairs, embed, radial_one, mix_one, radial_two, mix_two, readout))
    moved, ready = exchange(*sends, ready)
    w_hi, w_lo, mats, begins, radial, rows, xt_own, prc, hot, hot_t, plan_own, plan_ghost = ready
    store = lambda slots: [b(slots, HIST, 2 * LANES), f(slots, 12 * CELL, LANES)]
    hist_own, tiles_own, shapes_own = call(
        own_first_kernel, [f(atoms, HIST)] + store(SLOTS), [SMEM] + [VMEM] * 2
    )(plan_own, xt_own, prc)
    hist, xt_ghost, tiles_ghost, shapes_ghost, *sends = call(
        functools.partial(ghost_first_kernel, side),
        [f(atoms, HIST), f(8, 8, LANES)] + store(SLOTS // 2) + three(CELL, HIST),
        [SMEM] + [VMEM] * 7,
    )(plan_ghost, hot_t, *moved, prc, hist_own)

    own = call(
        own_update_kernel, [f(atoms, FEAT), f(atoms, FEAT), f(atoms, 2 * CH), f(atoms, 3 * CH)], [VMEM] * 6
    )(hist, prc, w_hi, w_lo, begins, mats)
    moved, own = exchange(*sends, own)
    feat, lin, gates, lifted = own
    (acc_own,) = call(own_second_kernel, [f(atoms, CH)], [SMEM] + [VMEM] * 3)(plan_own, tiles_own, feat, radial)
    zed, grad_acc, feat_ghost, *sends = call(
        ghost_second_kernel,
        [f(atoms, CH), f(atoms, CH), f(ghosts, FEAT)] + three(CELL, HIST),
        [SMEM] + [VMEM] * 13,
        [
            VMEM((ghosts, HIST), F32),
            VMEM((ghosts, FEAT), F32),
            VMEM((ghosts, 2 * CH), F32),
            VMEM((ghosts, 3 * CH), F32),
            VMEM((ghosts, FEAT), F32),
            VMEM((atoms, CH), F32),
        ],
    )(plan_ghost, tiles_ghost, xt_ghost, *moved, w_hi, w_lo, begins, mats, acc_own, radial, rows)

    two = call(ghost_force_kernel, [f(atoms, LANES), f(8, LANES)], [SMEM] + [VMEM] * 4)(
        plan_ghost, shapes_ghost, grad_acc, radial, feat_ghost
    )
    moved, two = exchange(*sends, two)
    recv_two, send_two = two
    (quad_own,) = call(
        own_grad_kernel, [f(atoms, HIST)], [SMEM] + [VMEM] * 10, [VMEM((atoms, FEAT), F32)]
    )(plan_own, tiles_own, grad_acc, radial, lin, gates, lifted, w_hi, w_lo, mats, rows)
    quad, recv, *sends = call(
        ghost_last_kernel,
        [f(atoms, HIST), f(atoms, LANES)] + three(1, LANES),
        [SMEM] + [VMEM] * 10,
        [VMEM((ghosts, HIST), BF16), VMEM((ghosts, HIST), BF16), VMEM((8, LANES), F32)],
    )(plan_ghost, hot, shapes_ghost, xt_ghost, quad_own, *moved, recv_two, send_two)

    shared = (plan_own, shapes_own, xt_own, quad, grad_acc, radial, feat)
    early = call(
        own_start_kernel, [f(atoms, LANES), f(OWN, LANES), f(1, atoms)], [SMEM] + [VMEM] * 9
    )(*shared, recv, zed, rows)
    moved, early = exchange(*sends, early)
    recv, send, energy = early
    (partial,) = call(
        own_force_kernel,
        [f(3, atoms)],
        [SMEM] + [VMEM] * 8,
        [VMEM((atoms, LANES), F32), VMEM((OWN, LANES), F32)],
    )(*shared, recv, send)
    (forces,) = call(last_kernel, [f(3, atoms)], [VMEM] * 6)(hot, *moved, partial)
    return forces, energy[0]


def solution(mesh):
    both = P(("gx", "gy"))
    in_specs = (
        P(None, ("gx", "gy")),
        both,
        P("gx", "gy", None, None),
        P("gx", "gy", None, None),
        P("gx", "gy"),
    ) + (P(),) * 6
    out_specs = (P(None, ("gx", "gy")), both)
    return jax.shard_map(shards, mesh=mesh, in_specs=in_specs, out_specs=out_specs, check_vma=False)
```
